128 devices in a mesh: ctx: 16 (over x, y), tensor: 8 (over z, core).
Axes of the slice: x: 4, y: 4, z: 4, core: 2. Of those that a mesh axis runs over, the one named last changes fastest.
Arguments:
- queries: bfloat16 [16384, 4096], P('ctx', 'tensor'), may hold values from -6 to 6
- keys: bfloat16 [16384, 4096], P('ctx', 'tensor'), may hold values from -6 to 6
- values: bfloat16 [16384, 4096], P('ctx', 'tensor'), may hold values from -6 to 6
- doc_ids: int32 [16384], P('ctx'), may hold values from 0 to 7, never falling along the last dimension, each value on 1 to 8192 neighbouring positions
- out_weight: bfloat16 [4096, 6144], P('tensor'), may hold values from -0.125 to 0.125
- grad_out: bfloat16 [16384, 6144], P('ctx', 'tensor'), may hold values from -6 to 6
Outputs:
- attended: bfloat16 [16384, 6144], P('ctx', 'tensor')
- grad_queries: bfloat16 [16384, 4096], P('ctx', 'tensor')
- grad_keys: bfloat16 [16384, 4096], P('ctx', 'tensor')
- grad_values: bfloat16 [16384, 4096], P('ctx', 'tensor')
- grad_weight: float32 [4096, 6144], P('tensor', 'ctx')
The draws below stay inside these ranges and needn't reach their ends.
Inputs may be any that keep to these rules, and one draw needn't show every extreme that they name: `doc_ids`: never falling along the sequence; each document has 1 to 8192 positions, and one has exactly 8192.
All inputs are finite; a program needn't handle non-finite values.
Results may differ from the reference program's by a relative error of at most 0.015.
Values may be sent and summed in bfloat16 or wider, within the bound.
No kernel may reach another device: no remote copies, remote signals or barrier semaphores. Data moves between devices by JAX's collectives and lax.ppermute only.
A program may use at most 192 MiB of HBM per device.

```python
import math
import jax
import jax.numpy as jnp
import numpy as np
from jax import lax

D = 6144
HEADS = 32
HEAD = 128
DOCS = 8
TOK_DEV = 1024
LENGTH = 16384
N_TENSOR = 8


def with_spikes(values, rng, source, target, shards_of, factor):
    def block_of(dim):
        return (jnp.arange(values.shape[dim]) // (values.shape[dim] // shards_of)).reshape((-1,) + (1,) * (values.ndim - 1 - dim))

    one_side = jax.random.permutation(rng, shards_of)[block_of(target)]
    second = (block_of(target) + shards_of // 2) % shards_of
    return jnp.where((block_of(source) == one_side) | (block_of(source) == second), factor * values, values)


def block_scale(key, extent, shards, smallest, high):
    loudness = 1.0
    for axis_at, blocks in shards:
        heights = jax.random.uniform(jax.random.fold_in(jax.random.fold_in(key, 6), axis_at), (blocks,), jnp.float32, smallest / len(shards), high / len(shards))
        loudness = loudness * jnp.repeat(jnp.exp(heights), extent[axis_at] // blocks).reshape((-1,) + (1,) * (len(extent) - 1 - axis_at))
    return loudness


def length_profile(amount, total, bound, skew):
    loads = [(1 << 20) // math.isqrt(grade ** skew) + 1 for grade in range(2, amount + 1)]
    rest, given = total - bound - (amount - 1), [1] * (amount - 1)
    while rest > 0:
        free = [i for i in range(amount - 1) if given[i] < bound]
        mass, remaining = sum([loads[i] for i in free]), rest
        for i in free:
            more = min(bound - given[i], max(1, remaining * loads[i] // mass), rest)
            given[i] = given[i] + more
            rest = rest - more
    return np.array([bound] + given)


def uneven(stream_key, number_of, total, limit, skew):
    if number_of == 2:
        one = jax.random.randint(stream_key, (), max(1, total - limit), min(limit, total - 1) + 1)
        return jnp.stack([one, total - one])
    tallies = jnp.asarray(length_profile(number_of, total, limit, skew), jnp.int32)
    pairs = (number_of - 1) // 2
    source_of, sink = tallies[1:1 + 2 * pairs:2], tallies[2:2 + 2 * pairs:2]
    room = jnp.minimum(source_of - 1, limit - sink)
    moved = jax.random.randint(jax.random.fold_in(stream_key, 1), (pairs,), 0, 1 << 20) % (room + 1)
    tallies = tallies.at[1:1 + 2 * pairs:2].set(source_of - moved).at[2:2 + 2 * pairs:2].set(sink + moved)
    return tallies[jax.random.permutation(jax.random.fold_in(stream_key, 2), number_of)]


def scatter_about(rng, shape, spread, limit, pieces=(), dtype=jnp.bfloat16):
    entries = spread * jax.random.normal(rng, shape, jnp.float32)
    if pieces:
        entries = entries * block_scale(rng, shape, pieces, -0.22, 0.18)
    return jnp.clip(entries, -limit, limit).astype(dtype)


def gaussian_with(rng, shape, spread, reach, cuts, heavy, dtype=jnp.bfloat16):
    values = spread * jax.random.normal(rng, shape, jnp.float32)
    if cuts:
        values = values * block_scale(rng, shape, cuts, -0.22, 0.18)
    return jnp.clip(with_spikes(values, jax.random.fold_in(rng, 3), *heavy), -reach, reach).astype(dtype)


def setup_inputs(seed: int = 0) -> dict:
    streams_of = jax.random.split(jax.random.key(seed), 7)
    queries = scatter_about(streams_of[0], (LENGTH, HEADS * HEAD), 1.0, 6.0, ((0, 16), (1, 8)))
    keys = scatter_about(streams_of[1], (LENGTH, HEADS * HEAD), 1.0, 6.0, ((0, 16), (1, 8)))
    values = scatter_about(streams_of[2], (LENGTH, HEADS * HEAD), 1.0, 6.0, ((0, 16), (1, 8)))
    doc_ids = jnp.searchsorted(jnp.cumsum(uneven(streams_of[3], DOCS, LENGTH, LENGTH // 2, 1)), jnp.arange(LENGTH), side="right").astype(jnp.int32)
    out_weight = gaussian_with(streams_of[4], (HEADS * HEAD, D), (HEADS * HEAD) ** -0.5, 0.125, ((0, 8),), (0, 1, 8, 2.0))
    grad_out = gaussian_with(streams_of[5], (LENGTH, D), 1.0, 6.0, ((0, 16), (1, 8)), (0, 1, 16, 2.0))
    return {"queries": queries, "keys": keys, "values": values, "doc_ids": doc_ids, "out_weight": out_weight, "grad_out": grad_out}


highest = lax.Precision.HIGHEST
epsilon = 1e-06

def attend(query_float, key_float, value_float, doc_ids):
    blocks = LENGTH // TOK_DEV
    order = jnp.arange(TOK_DEV)
    causal = order[:, None] >= order[None, :]

    def shaped(array):
        return array.reshape(blocks, TOK_DEV, HEADS, HEAD)

    def advance(carry, block):
        state, last_doc = carry
        query, key, value, documents = block
        mask = (causal & (documents[:, None] == documents[None, :])).astype(jnp.float32)
        scores = jnp.einsum('the,uhe->htu', query, key, precision=highest) * mask[None]
        local = jnp.einsum('htu,uhf->thf', scores, value, precision=highest)
        carried = jnp.einsum('the,hef->thf', query, state, precision=highest)
        joined = (documents == last_doc).astype(jnp.float32)[:, None, None]
        output = local + joined * carried
        tail = (documents == documents[-1]).astype(jnp.float32)[:, None, None]
        added = jnp.einsum('uhe,uhf->hef', key * tail, value, precision=highest)
        keeping = (documents[-1] == last_doc).astype(jnp.float32)
        return ((added + keeping * state, documents[-1]), output)
    start = (jnp.zeros((HEADS, HEAD, HEAD), jnp.float32), jnp.array(-1, jnp.int32))
    final_carry, outputs = lax.scan(advance, start, (shaped(query_float), shaped(key_float), shaped(value_float), doc_ids.reshape(blocks, TOK_DEV).astype(jnp.int32)))
    return outputs.reshape(LENGTH, HEADS, HEAD)

def reference(queries, keys, values, doc_ids, out_weight, grad_out):
    query_float = queries.astype(jnp.float32).reshape(LENGTH, HEADS, HEAD)
    key_float = keys.astype(jnp.float32).reshape(LENGTH, HEADS, HEAD)
    value_float = values.astype(jnp.float32).reshape(LENGTH, HEADS, HEAD)

    def forward(query_in, key_in, value_in):
        return attend(query_in, key_in, value_in, doc_ids)
    opened, pullback = jax.vjp(forward, query_float, key_float, value_float)
    inverse = lax.rsqrt(lax.optimization_barrier(jnp.mean(opened * opened, axis=-1, keepdims=True)) + epsilon)
    normed = opened * inverse
    normed_low = normed.reshape(LENGTH, HEADS * HEAD).astype(jnp.bfloat16)
    group = HEADS * HEAD // N_TENSOR
    total = jnp.zeros((LENGTH, D), jnp.float32)
    for index in range(N_TENSOR):
        part = jnp.dot(normed_low[:, index * group:(index + 1) * group], out_weight[index * group:(index + 1) * group], preferred_element_type=jnp.float32)
        total = total + part.astype(jnp.bfloat16).astype(jnp.float32)
    attended = total.astype(jnp.bfloat16)
    grad_normed = lax.dot_general(grad_out, out_weight, (((1,), (1,)), ((), ())), preferred_element_type=jnp.float32)
    grad_weight = lax.dot_general(normed_low, grad_out, (((0,), (0,)), ((), ())), preferred_element_type=jnp.float32)
    grad_normed = grad_normed.reshape(LENGTH, HEADS, HEAD)
    grad_opened = inverse * (grad_normed - normed * lax.optimization_barrier(jnp.mean(grad_normed * normed, axis=-1, keepdims=True)))
    grad_query, grad_key, grad_value = pullback(grad_opened)
    width = HEADS * HEAD
    return (attended, grad_query.reshape(LENGTH, width).astype(jnp.bfloat16), grad_key.reshape(LENGTH, width).astype(jnp.bfloat16), grad_value.reshape(LENGTH, width).astype(jnp.bfloat16), grad_weight)
```

```python
import jax
import jax.numpy as jnp
from jax import lax
from jax.experimental import pallas as pl
from jax.experimental.pallas import tpu as pltpu
from jax.sharding import Mesh
from jax.sharding import PartitionSpec as P

HEAD = 128
CHUNK = 256
CTX = ("cx", "cy")
TENSOR = ("z", "core")
EPSILON = 1e-06
F32 = jnp.float32
BF16 = jnp.bfloat16
NT = (((1,), (1,)), ((), ()))
TN = (((0,), (0,)), ((), ()))
NN = (((1,), (0,)), ((), ()))


def dot(a, b, dims):
    return lax.dot_general(a, b, dims, preferred_element_type=F32)


def whole(shape):
    return pl.BlockSpec(shape, lambda *_: (0,) * len(shape))


def rows_of(width, count=None):
    if count is None:
        return pl.BlockSpec((CHUNK, width), lambda i: (i, 0))
    return pl.BlockSpec((CHUNK, width), lambda i: (count - 1 - i, 0))


def head_cols(h):
    return slice(h * HEAD, (h + 1) * HEAD)


def params():
    return pltpu.CompilerParams(vmem_limit_bytes=56 << 20, dimension_semantics=("arbitrary",))


def state_of(ref):
    return ref[:-16, :].astype(F32), ref[-16:-15, :].astype(F32)


def entering_state(beside, rows, doc, place):
    total = None
    for s, ref in enumerate(beside):
        state, found = state_of(ref)
        part = jnp.where((found == doc) & (place > s + 0.5), state, 0.0)
        total = part if total is None else total + part
    for ref in rows:
        state, found = state_of(ref)
        total = total + jnp.where(found == doc, state, 0.0)
    return total


def row_kernel(latest, *refs):
    states = [state_of(ref) for ref in refs[:-1]]
    out = refs[-1]
    doc = states[0][1]
    for _, found in states[1:]:
        doc = jnp.maximum(doc, found) if latest else jnp.minimum(doc, found)
    total = None
    for state, found in states:
        part = jnp.where(found == doc, state, 0.0)
        total = part if total is None else total + part
    out[:-16, :] = total.astype(BF16)
    out[-16:, :] = jnp.broadcast_to(doc, (16, HEAD)).astype(BF16)


def tail_kernel(k, v, dcol, table, out):
    heads = k.shape[1] // HEAD
    last = table[7:8, :]
    tail = dcol[...] == last
    for h in range(heads):
        c = head_cols(h)
        kept = jnp.where(tail, k[:, c].astype(F32), 0.0).astype(BF16)
        out[c, :] = dot(kept, v[:, c], TN).astype(BF16)
    out[heads * HEAD :, :] = jnp.broadcast_to(last, (16, HEAD)).astype(BF16)


def forward_kernel(q, k, v, dcol, drow, table, *refs):
    arrived, (opened, low, turned, states, carry) = refs[:-5], refs[-5:]
    i = pl.program_id(0)
    heads = q.shape[1] // HEAD
    first = table[pl.ds(i, 1), :]
    following = table[pl.ds(i + 1, 1), :]

    @pl.when(i == 0)
    def _():
        carry[...] = entering_state(arrived[:3], arrived[3:], first, table[8:9, :])

    docs = dcol[...]
    joined = docs == first
    tail = docs == following
    keep = following == first
    t = lax.broadcasted_iota(jnp.int32, (CHUNK, CHUNK), 0)
    u = lax.broadcasted_iota(jnp.int32, (CHUNK, CHUNK), 1)
    mask = (t >= u) & (docs[:, :1] == drow[...])
    for h in range(heads):
        c = head_cols(h)
        qh, kh, vh = q[:, c], k[:, c], v[:, c]
        state = carry[c, :]
        state_low = state.astype(BF16)
        states[0, c, :] = state_low
        scores = jnp.where(mask, dot(qh, kh, NT), 0.0).astype(BF16)
        out = dot(scores, vh, NN) + jnp.where(joined, dot(qh, state_low, NN), 0.0)
        opened[:, c] = out
        inverse = lax.rsqrt(jnp.mean(out * out, axis=-1, keepdims=True) + EPSILON)
        normed = (out * inverse).astype(BF16)
        low[:, c] = normed
        turned[c, :] = normed.T
        kept = jnp.where(tail, kh.astype(F32), 0.0).astype(BF16)
        carry[c, :] = jnp.where(keep, state, 0.0) + dot(kept, vh, TN)


def cotangent_kernel(grad, weight, opened, q, dcol, table, grad_opened, out, carry):
    i = pl.program_id(0)
    heads = q.shape[1] // HEAD
    width = grad.shape[2]
    gn = dot(grad[0], weight[:, :width], NT)
    for j in range(1, grad.shape[0]):
        gn = gn + dot(grad[j], weight[:, j * width : (j + 1) * width], NT)

    @pl.when(i == 0)
    def _():
        carry[...] = jnp.zeros_like(carry)

    first = table[0:1, :]
    starts = dcol[...] == first
    for h in range(heads):
        c = head_cols(h)
        opened_h = opened[:, c]
        gh = gn[:, c]
        inverse = lax.rsqrt(jnp.mean(opened_h * opened_h, axis=-1, keepdims=True) + EPSILON)
        normed = opened_h * inverse
        go = inverse * (gh - normed * jnp.mean(gh * normed, axis=-1, keepdims=True))
        grad_opened[:, c] = go
        kept = jnp.where(starts, q[:, c].astype(F32), 0.0).astype(BF16)
        carry[c, :] += dot(kept, go.astype(BF16), TN)

    @pl.when(i == pl.num_programs(0) - 1)
    def _():
        size = heads * HEAD
        out[:size, :] = carry[...].astype(BF16)
        out[size:, :] = jnp.broadcast_to(first, (16, HEAD)).astype(BF16)


def split(value):
    high = value.astype(BF16)
    return high, (value - high.astype(F32)).astype(BF16)


def query_kernel(go, k, v, dcol, drow, table, states, out):
    i = pl.program_id(0)
    heads = k.shape[1] // HEAD
    first = table[pl.ds(i, 1), :]
    docs = dcol[...]
    joined = docs == first
    t = lax.broadcasted_iota(jnp.int32, (CHUNK, CHUNK), 0)
    u = lax.broadcasted_iota(jnp.int32, (CHUNK, CHUNK), 1)
    mask = (t >= u) & (docs[:, :1] == drow[...])
    for h in range(heads):
        c = head_cols(h)
        high, rest = split(go[:, c])
        vh = v[:, c]
        both = jnp.concatenate([high, rest], axis=1)
        twice = jnp.concatenate([vh, vh], axis=1)
        scores = jnp.where(mask, dot(both, twice, NT), 0.0).astype(BF16)
        carried = jnp.where(joined, dot(high, states[0, c, :], NT), 0.0)
        out[:, c] = (dot(scores, k[:, c], NN) + carried).astype(BF16)


def key_value_kernel(go, q, k, v, dcol, drow, table, *refs):
    arrived, (grad_k, grad_v, carry) = refs[:-3], refs[-3:]
    step = pl.program_id(0)
    i = pl.num_programs(0) - 1 - step
    heads = k.shape[1] // HEAD
    last = table[pl.ds(4 + i, 1), :]
    previous = table[pl.ds(3 + i, 1), :]

    @pl.when(step == 0)
    def _():
        carry[...] = entering_state(arrived[:3], arrived[3:], last, table[9:10, :])

    docs = dcol[...]
    joined = docs == last
    ahead = docs == previous
    keep = previous == last
    u = lax.broadcasted_iota(jnp.int32, (CHUNK, CHUNK), 0)
    t = lax.broadcasted_iota(jnp.int32, (CHUNK, CHUNK), 1)
    mask = (t >= u) & (docs[:, :1] == drow[...])
    for h in range(heads):
        c = head_cols(h)
        high, rest = split(go[:, c])
        qh, kh, vh = q[:, c], k[:, c], v[:, c]
        state = carry[c, :]
        state_low = state.astype(BF16)
        both = jnp.concatenate([high, rest], axis=1)
        twice = jnp.concatenate([vh, vh], axis=1)
        scores = jnp.where(mask, dot(kh, qh, NT), 0.0).astype(BF16)
        grad_scores = jnp.where(mask, dot(twice, both, NT), 0.0).astype(BF16)
        grad_v[:, c] = (
            dot(scores, high, NN) + jnp.where(joined, dot(kh, state_low, NN), 0.0)
        ).astype(BF16)
        grad_k[:, c] = (
            dot(grad_scores, qh, NN) + jnp.where(joined, dot(vh, state_low, NT), 0.0)
        ).astype(BF16)
        kept = jnp.where(ahead, qh.astype(F32), 0.0).astype(BF16)
        carry[c, :] = jnp.where(keep, state, 0.0) + dot(kept, high, TN)


def weight_kernel(turned, grad, first, second):
    part = dot(turned[...], grad[0], NN).astype(BF16)
    rows, cols = part.shape[0] // 2, part.shape[1] // 2
    for h in range(2):
        c = slice(h * cols, (h + 1) * cols)
        first[h, 0] = part[:rows, c]
        second[0, h] = part[rows:, c]


def middle_sum_kernel(places, a, a1, a2, a3, b, b1, b2, b3, *outs):
    for own, others, base in ((a, (a1, a2, a3), 0), (b, (b1, b2, b3), 4)):
        total = own[0, 0].astype(F32)
        for other in others:
            total = total + other[0].astype(F32)
        for s in range(4):

            @pl.when(pl.program_id(0) == s)
            def _():
                outs[base + s][...] = total.astype(outs[base + s].dtype)


def last_sum_kernel(a, a1, a2, a3, b, b1, b2, b3, out):
    half = a.shape[0]
    for parts, rows in (((a, a1, a2, a3), slice(0, half)), ((b, b1, b2, b3), slice(half, 2 * half))):
        total = parts[0][...].astype(F32)
        for part in parts[1:]:
            total = total + part[...].astype(F32)
        out[rows, :] = total


def attended_kernel(places, low, own, right, left, far_a, far_b, out, columns, sems):
    i = pl.program_id(0)
    lines = 4
    half = lines // 2

    def copies():
        for y, pieces in enumerate(((own,), (right,), (far_a, far_b), (left,))):
            for x in range(lines):
                piece = pieces[0] if len(pieces) == 1 else pieces[x // half]
                at = x if len(pieces) == 1 else x % half
                for o in range(2):
                    group = places[2 * y + o]
                    row = pl.multiple_of(places[8 + x] * HEAD, HEAD)
                    to = columns.at[group, pl.ds(row, HEAD)]
                    yield pltpu.make_async_copy(piece.at[at, o], to, sems.at[8 * y + 2 * x + o])

    @pl.when(i == 0)
    def _():
        for copy in copies():
            copy.start()
        for copy in copies():
            copy.wait()

    total = None
    for j in range(low.shape[0]):
        part = dot(low[j], columns[j], NN)
        total = part if total is None else total + part
    out[...] = total.astype(BF16)


def turned_by(value, axis, step):
    size = lax.axis_size(axis)
    return lax.ppermute(value, axis, [(i, (i + step) % size) for i in range(size)])


def moved_by(value, axis, step):
    size = lax.axis_size(axis)
    pairs = [(i, i + step) for i in range(size) if 0 <= i + step < size]
    return lax.ppermute(value, axis, pairs)


def swapped(value):
    return lax.ppermute(value, "core", [(0, 1), (1, 0)])


def pick(value, index, axis=0):
    return lax.dynamic_index_in_dim(value, index, axis, keepdims=False)


def exchanged(state, step):
    beside = [turned_by(state, "cy", step * s) for s in range(1, 4)]
    row = pl.pallas_call(
        lambda *refs: row_kernel(step > 0, *refs),
        out_shape=jax.ShapeDtypeStruct(state.shape, state.dtype),
        name="row_state",
    )(state, *beside)
    return beside + [moved_by(row, "cx", step * s) for s in range(1, 3)]


def column_pieces(out_weight, share, cx, core):
    cy, z = lax.axis_index("cy"), lax.axis_index("z")
    at = (cx * HEAD, (z - cy) % 4 * 2 * share)
    sent = lax.dynamic_slice(out_weight, at, (HEAD, 2 * share))
    pairs = [(4 * y + (i + y) % 4, 4 * y + i) for y in range(4) for i in range(4)]
    held = lax.ppermute(sent, ("cy", "z"), pairs)
    mine = lax.dynamic_slice(held, (0, core * share), (HEAD, share))
    other = lax.dynamic_slice(held, (0, (1 - core) * share), (HEAD, share))
    both = jnp.stack([mine, swapped(other)])
    return jnp.stack([both] + [turned_by(both, "cx", s) for s in range(1, 4)])


def scattered_sum(first, second, cx, cy):
    half, part = first.shape[2:]
    to_y = [turned_by(pick(first, (cy + s) % 4), "cy", s) for s in range(1, 4)]
    to_x = [turned_by(pick(second, (cx + s) % 4), "cx", s) for s in range(1, 4)]

    def own(line, start):
        shape = (1, 1, half, part)
        return pl.BlockSpec(shape, lambda i, p: (p[line], (p[start] + i) % 4, 0, 0))

    def piece(start):
        return pl.BlockSpec((1, half, part), lambda i, p: ((p[start] + i) % 4, 0, 0))

    kinds = [F32, BF16, BF16, BF16] * 2
    sums = pl.pallas_call(
        middle_sum_kernel,
        grid_spec=pltpu.PrefetchScalarGridSpec(
            num_scalar_prefetch=1,
            grid=(4,),
            in_specs=[own(1, 0)] + [piece(0)] * 3 + [own(0, 1)] + [piece(1)] * 3,
            out_specs=[pl.BlockSpec((half, part), lambda i, p: (0, 0))] * 8,
        ),
        out_shape=[jax.ShapeDtypeStruct((half, part), kind) for kind in kinds],
        compiler_params=params(),
        name="middle_sum",
    )(jnp.stack([cx, cy]), first, *to_y, second, *to_x)
    to_x = [turned_by(sums[s], "cx", s) for s in range(1, 4)]
    to_y = [turned_by(sums[4 + s], "cy", s) for s in range(1, 4)]
    return pl.pallas_call(
        last_sum_kernel,
        out_shape=jax.ShapeDtypeStruct((2 * half, part), F32),
        name="last_sum",
    )(sums[0], *to_x, sums[4], *to_y)


def body(queries, keys, values, doc_ids, out_weight, grad_out):
    rows, width = queries.shape
    blocks = rows // CHUNK
    groups = lax.axis_size(TENSOR)
    share = grad_out.shape[1]
    size = width
    payload = jax.ShapeDtypeStruct((size + 16, HEAD), BF16)
    cx, cy = lax.axis_index("cx"), lax.axis_index("cy")
    z, core = lax.axis_index("z"), lax.axis_index("core")

    grad_whole = lax.all_gather(grad_out, TENSOR, axis=0)

    docs = doc_ids.astype(F32)
    dcol = jnp.broadcast_to(docs[:, None], (rows, HEAD))
    drow = docs[None, :]
    chunked = docs.reshape(blocks, CHUNK)
    place = cy.astype(F32)[None]
    table = jnp.concatenate([chunked[:, 0], chunked[:, -1], place, 3 - place, jnp.zeros((6,), F32)])
    table = jnp.broadcast_to(table[:, None], (16, HEAD))

    tail = pl.pallas_call(tail_kernel, out_shape=payload, name="tail")(keys, values, dcol, table)
    arrived = exchanged(tail, 1)

    own = column_pieces(out_weight, share, cx, core)
    arrived, own = lax.optimization_barrier((arrived, own))

    row_block = pl.BlockSpec((1, CHUNK), lambda i: (0, i))
    state_block = pl.BlockSpec((1, size, HEAD), lambda i: (i, 0, 0))
    opened, low, turned, states = pl.pallas_call(
        forward_kernel,
        grid=(blocks,),
        in_specs=[rows_of(width)] * 3
        + [rows_of(HEAD), row_block, whole(table.shape)]
        + [whole(payload.shape)] * len(arrived),
        out_specs=[
            rows_of(width),
            rows_of(width),
            pl.BlockSpec((width, CHUNK), lambda i: (0, i)),
            state_block,
        ],
        out_shape=[
            jax.ShapeDtypeStruct((rows, width), F32),
            jax.ShapeDtypeStruct((rows, width), BF16),
            jax.ShapeDtypeStruct((width, rows), BF16),
            jax.ShapeDtypeStruct((blocks, size, HEAD), BF16),
        ],
        scratch_shapes=[pltpu.VMEM((size, HEAD), F32)],
        compiler_params=params(),
        name="forward",
    )(queries, keys, values, dcol, drow, table, *arrived)

    low_whole = lax.all_gather(low, TENSOR, axis=0)

    right = turned_by(own, "cy", -1)
    left = turned_by(own, "cy", 1)
    turned, right, left = lax.optimization_barrier((turned, right, left))

    pair = (width // 2, share // 2)
    first, second = pl.pallas_call(
        weight_kernel,
        grid=(groups,),
        in_specs=[whole((width, rows)), pl.BlockSpec((1, rows, share), lambda j: (j, 0, 0))],
        out_specs=[
            pl.BlockSpec((2, 1, *pair), lambda j: (j % 2, j // 2, 0, 0)),
            pl.BlockSpec((1, 2, *pair), lambda j: (j // 2, j % 2, 0, 0)),
        ],
        out_shape=[jax.ShapeDtypeStruct((4, 4, *pair), BF16)] * 2,
        compiler_params=params(),
        name="weight_grad",
    )(turned, grad_whole)
    grad_weight = scattered_sum(first, second, cx, cy)

    grad_opened, head = pl.pallas_call(
        cotangent_kernel,
        grid=(blocks,),
        in_specs=[
            pl.BlockSpec((groups, CHUNK, share), lambda i: (0, i, 0)),
            whole(out_weight.shape),
            rows_of(width),
            rows_of(width),
            rows_of(HEAD),
            whole(table.shape),
        ],
        out_specs=[rows_of(width), whole(payload.shape)],
        out_shape=[jax.ShapeDtypeStruct((rows, width), F32), payload],
        scratch_shapes=[pltpu.VMEM((size, HEAD), F32)],
        compiler_params=params(),
        name="cotangent",
    )(grad_whole, out_weight, opened, queries, dcol, table)
    returned = exchanged(head, -1)

    far_a = turned_by(right[:2], "cy", -1)
    far_b = turned_by(left[2:], "cy", 1)

    grad_query = pl.pallas_call(
        query_kernel,
        grid=(blocks,),
        in_specs=[rows_of(width)] * 3
        + [rows_of(HEAD), row_block, whole(table.shape), state_block],
        out_specs=rows_of(width),
        out_shape=jax.ShapeDtypeStruct((rows, width), BF16),
        compiler_params=params(),
        name="grad_query",
    )(grad_opened, keys, values, dcol, drow, table, states)

    back_row = pl.BlockSpec((1, CHUNK), lambda i: (0, blocks - 1 - i))
    grad_key, grad_value = pl.pallas_call(
        key_value_kernel,
        grid=(blocks,),
        in_specs=[rows_of(width, blocks)] * 4
        + [rows_of(HEAD, blocks), back_row, whole(table.shape)]
        + [whole(payload.shape)] * len(returned),
        out_specs=[rows_of(width, blocks)] * 2,
        out_shape=[jax.ShapeDtypeStruct((rows, width), BF16)] * 2,
        scratch_shapes=[pltpu.VMEM((size, HEAD), F32)],
        compiler_params=params(),
        name="grad_key_value",
    )(grad_opened, queries, keys, values, dcol, drow, table, *returned)

    around = [2 * ((z + cy + s) % 4) + (core if o == 0 else 1 - core) for s in range(4) for o in range(2)]
    heads_at = [(cx - s) % 4 for s in range(4)]
    held = pl.BlockSpec(memory_space=pl.ANY)
    attended = pl.pallas_call(
        attended_kernel,
        grid_spec=pltpu.PrefetchScalarGridSpec(
            num_scalar_prefetch=1,
            grid=(blocks,),
            in_specs=[pl.BlockSpec((groups, CHUNK, width), lambda i, at: (0, i, 0))] + [held] * 5,
            out_specs=pl.BlockSpec((CHUNK, share), lambda i, at: (i, 0)),
            scratch_shapes=[
                pltpu.VMEM((groups, width, share), BF16),
                pltpu.SemaphoreType.DMA((32,)),
            ],
        ),
        out_shape=jax.ShapeDtypeStruct((rows, share), BF16),
        compiler_params=params(),
        name="attended",
    )(jnp.stack(around + heads_at), low_whole, own, right, left, far_a, far_b)
    return attended, grad_query, grad_key, grad_value, grad_weight


def solution(mesh):
    finer = Mesh(mesh.devices.reshape(4, 4, 4, 2), ("cx", "cy", "z", "core"))
    by_both = P(CTX, TENSOR)
    return jax.shard_map(
        body,
        mesh=finer,
        in_specs=(by_both, by_both, by_both, P(CTX), P(TENSOR, None), by_both),
        out_specs=(by_both, by_both, by_both, by_both, P(TENSOR, CTX)),
        check_vma=False,
    )
```

```python
import jax
import jax.numpy as jnp
from jax import lax
from jax.experimental import pallas as pl
from jax.experimental.pallas import tpu as pltpu
from jax.sharding import Mesh
from jax.sharding import PartitionSpec as P

HEAD = 128
CHUNK = 256
CTX = ("cx", "cy")
TENSOR = ("z", "core")
EPSILON = 1e-06
F32 = jnp.float32
BF16 = jnp.bfloat16
NT = (((1,), (1,)), ((), ()))
TN = (((0,), (0,)), ((), ()))
NN = (((1,), (0,)), ((), ()))


def dot(a, b, dims):
    return lax.dot_general(a, b, dims, preferred_element_type=F32)


def whole(shape):
    return pl.BlockSpec(shape, lambda *_: (0,) * len(shape))


def rows_of(width, count=None):
    if count is None:
        return pl.BlockSpec((CHUNK, width), lambda i: (i, 0))
    return pl.BlockSpec((CHUNK, width), lambda i: (count - 1 - i, 0))


def head_cols(h):
    return slice(h * HEAD, (h + 1) * HEAD)


def params():
    return pltpu.CompilerParams(vmem_limit_bytes=56 << 20, dimension_semantics=("arbitrary",))


def state_of(ref):
    return ref[:-16, :].astype(F32), ref[-16:-15, :].astype(F32)


def entering_state(beside, rows, doc, place):
    total = None
    for s, ref in enumerate(beside):
        state, found = state_of(ref)
        part = jnp.where((found == doc) & (place > s + 0.5), state, 0.0)
        total = part if total is None else total + part
    for ref in rows:
        state, found = state_of(ref)
        total = total + jnp.where(found == doc, state, 0.0)
    return total


def row_kernel(latest, *refs):
    states = [state_of(ref) for ref in refs[:-1]]
    out = refs[-1]
    doc = states[0][1]
    for _, found in states[1:]:
        doc = jnp.maximum(doc, found) if latest else jnp.minimum(doc, found)
    total = None
    for state, found in states:
        part = jnp.where(found == doc, state, 0.0)
        total = part if total is None else total + part
    out[:-16, :] = total.astype(BF16)
    out[-16:, :] = jnp.broadcast_to(doc, (16, HEAD)).astype(BF16)


def tail_kernel(k, v, dcol, table, out):
    heads = k.shape[1] // HEAD
    last = table[7:8, :]
    tail = dcol[...] == last
    for h in range(heads):
        c = head_cols(h)
        kept = jnp.where(tail, k[:, c].astype(F32), 0.0).astype(BF16)
        out[c, :] = dot(kept, v[:, c], TN).astype(BF16)
    out[heads * HEAD :, :] = jnp.broadcast_to(last, (16, HEAD)).astype(BF16)


def forward_kernel(q, k, v, dcol, drow, table, *refs):
    arrived, (opened, low, turned, states, carry) = refs[:-5], refs[-5:]
    i = pl.program_id(0)
    heads = q.shape[1] // HEAD
    first = table[pl.ds(i, 1), :]
    following = table[pl.ds(i + 1, 1), :]

    @pl.when(i == 0)
    def _():
        carry[...] = entering_state(arrived[:3], arrived[3:], first, table[8:9, :])

    docs = dcol[...]
    joined = docs == first
    tail = docs == following
    keep = following == first
    t = lax.broadcasted_iota(jnp.int32, (CHUNK, CHUNK), 0)
    u = lax.broadcasted_iota(jnp.int32, (CHUNK, CHUNK), 1)
    mask = (t >= u) & (docs[:, :1] == drow[...])
    for h in range(heads):
        c = head_cols(h)
        qh, kh, vh = q[:, c], k[:, c], v[:, c]
        state = carry[c, :]
        state_low = state.astype(BF16)
        states[0, c, :] = state_low
        scores = jnp.where(mask, dot(qh, kh, NT), 0.0).astype(BF16)
        out = dot(scores, vh, NN) + jnp.where(joined, dot(qh, state_low, NN), 0.0)
        opened[:, c] = out
        inverse = lax.rsqrt(jnp.mean(out * out, axis=-1, keepdims=True) + EPSILON)
        normed = (out * inverse).astype(BF16)
        low[:, c] = normed
        turned[c, :] = normed.T
        kept = jnp.where(tail, kh.astype(F32), 0.0).astype(BF16)
        carry[c, :] = jnp.where(keep, state, 0.0) + dot(kept, vh, TN)


def near_cotangent_kernel(places, *refs):
    out = refs[-1]
    count = (len(refs) - 1) // 2
    total = dot(refs[0][...], refs[count][...], NT)
    for p in range(1, count):
        total = total + dot(refs[p][...], refs[count + p][...], NT)
    out[...] = total


def cotangent_kernel(
    places, near, a0, b0, a1, b1, w0, w1, opened, q, dcol, table, grad_opened, out, carry
):
    i = pl.program_id(0)
    heads = q.shape[1] // HEAD
    early = i < pl.num_programs(0) // 2
    gn = near[...] + dot(jnp.where(early, a0[...], b0[...]), w0[...], NT)
    gn = gn + dot(jnp.where(early, a1[...], b1[...]), w1[...], NT)

    @pl.when(i == 0)
    def _():
        carry[...] = jnp.zeros_like(carry)

    first = table[0:1, :]
    starts = dcol[...] == first
    for h in range(heads):
        c = head_cols(h)
        opened_h = opened[:, c]
        gh = gn[:, c]
        inverse = lax.rsqrt(jnp.mean(opened_h * opened_h, axis=-1, keepdims=True) + EPSILON)
        normed = opened_h * inverse
        go = inverse * (gh - normed * jnp.mean(gh * normed, axis=-1, keepdims=True))
        grad_opened[:, c] = go
        kept = jnp.where(starts, q[:, c].astype(F32), 0.0).astype(BF16)
        carry[c, :] += dot(kept, go.astype(BF16), TN)

    @pl.when(i == pl.num_programs(0) - 1)
    def _():
        size = heads * HEAD
        out[:size, :] = carry[...].astype(BF16)
        out[size:, :] = jnp.broadcast_to(first, (16, HEAD)).astype(BF16)


def split(value):
    high = value.astype(BF16)
    return high, (value - high.astype(F32)).astype(BF16)


def query_kernel(go, k, v, dcol, drow, table, states, out):
    i = pl.program_id(0)
    heads = k.shape[1] // HEAD
    first = table[pl.ds(i, 1), :]
    docs = dcol[...]
    joined = docs == first
    t = lax.broadcasted_iota(jnp.int32, (CHUNK, CHUNK), 0)
    u = lax.broadcasted_iota(jnp.int32, (CHUNK, CHUNK), 1)
    mask = (t >= u) & (docs[:, :1] == drow[...])
    for h in range(heads):
        c = head_cols(h)
        high, rest = split(go[:, c])
        vh = v[:, c]
        both = jnp.concatenate([high, rest], axis=1)
        twice = jnp.concatenate([vh, vh], axis=1)
        scores = jnp.where(mask, dot(both, twice, NT), 0.0).astype(BF16)
        carried = jnp.where(joined, dot(high, states[0, c, :], NT), 0.0)
        out[:, c] = (dot(scores, k[:, c], NN) + carried).astype(BF16)


def key_value_kernel(go, q, k, v, dcol, drow, table, *refs):
    arrived, (grad_k, grad_v, carry) = refs[:-3], refs[-3:]
    step = pl.program_id(0)
    i = pl.num_programs(0) - 1 - step
    heads = k.shape[1] // HEAD
    last = table[pl.ds(4 + i, 1), :]
    previous = table[pl.ds(3 + i, 1), :]

    @pl.when(step == 0)
    def _():
        carry[...] = entering_state(arrived[:3], arrived[3:], last, table[9:10, :])

    docs = dcol[...]
    joined = docs == last
    ahead = docs == previous
    keep = previous == last
    u = lax.broadcasted_iota(jnp.int32, (CHUNK, CHUNK), 0)
    t = lax.broadcasted_iota(jnp.int32, (CHUNK, CHUNK), 1)
    mask = (t >= u) & (docs[:, :1] == drow[...])
    for h in range(heads):
        c = head_cols(h)
        high, rest = split(go[:, c])
        qh, kh, vh = q[:, c], k[:, c], v[:, c]
        state = carry[c, :]
        state_low = state.astype(BF16)
        both = jnp.concatenate([high, rest], axis=1)
        twice = jnp.concatenate([vh, vh], axis=1)
        scores = jnp.where(mask, dot(kh, qh, NT), 0.0).astype(BF16)
        grad_scores = jnp.where(mask, dot(twice, both, NT), 0.0).astype(BF16)
        grad_v[:, c] = (
            dot(scores, high, NN) + jnp.where(joined, dot(kh, state_low, NN), 0.0)
        ).astype(BF16)
        grad_k[:, c] = (
            dot(grad_scores, qh, NN) + jnp.where(joined, dot(vh, state_low, NT), 0.0)
        ).astype(BF16)
        kept = jnp.where(ahead, qh.astype(F32), 0.0).astype(BF16)
        carry[c, :] = jnp.where(keep, state, 0.0) + dot(kept, high, TN)


def put_columns(part, out):
    low = part.astype(BF16)
    half = low.shape[1] // 2
    out[0, 0] = low[:, :half]
    out[0, 1] = low[:, half:]


def near_weight_kernel(places, turned, *refs):
    pieces, (out, held, sems) = refs[:-3], refs[-3:]
    step = pl.program_id(0)

    def fetch(p):
        return pltpu.make_async_copy(pieces[p], held.at[p % 2], sems.at[p % 2])

    for p in range(len(pieces)):

        @pl.when(step == p)
        def _():
            if p == 0:
                fetch(0).start()
            if p + 1 < len(pieces):
                fetch(p + 1).start()
            fetch(p).wait()
            put_columns(dot(turned[...], held[p % 2], NN), out)


def far_weight_kernel(places, turned, a0, b0, a1, b1, started, out):
    half = turned.shape[1] // 2
    for p, (a, b) in enumerate(((a0, b0), (a1, b1))):

        @pl.when(pl.program_id(0) == p)
        def _():
            part = dot(turned[:, :half], a[...], NN) + dot(turned[:, half:], b[...], NN)
            put_columns(part, out)


def sum_kernel(place, own, *refs):
    total = own[0].astype(F32)
    for ref in refs[:-1]:
        total = total + ref[...].astype(F32)
    refs[-1][...] = total


def attended_kernel(places, low, own, right, left, far_a, far_b, out, columns, sems):
    i = pl.program_id(0)
    lines = 4
    half = lines // 2

    def copies():
        for y, pieces in enumerate(((own,), (right,), (far_a, far_b), (left,))):
            for x in range(lines):
                piece = pieces[0] if len(pieces) == 1 else pieces[x // half]
                at = x if len(pieces) == 1 else x % half
                for o in range(2):
                    group = places[2 * y + o]
                    row = pl.multiple_of(places[8 + x] * HEAD, HEAD)
                    to = columns.at[group, pl.ds(row, HEAD)]
                    yield pltpu.make_async_copy(piece.at[at, o], to, sems.at[8 * y + 2 * x + o])

    @pl.when(i == 0)
    def _():
        for copy in copies():
            copy.start()
        for copy in copies():
            copy.wait()

    total = None
    for j in range(low.shape[0]):
        part = dot(low[j], columns[j], NN)
        total = part if total is None else total + part
    out[...] = total.astype(BF16)


def turned_by(value, axis, step):
    size = lax.axis_size(axis)
    return lax.ppermute(value, axis, [(i, (i + step) % size) for i in range(size)])


def moved_by(value, axis, step):
    size = lax.axis_size(axis)
    pairs = [(i, i + step) for i in range(size) if 0 <= i + step < size]
    return lax.ppermute(value, axis, pairs)


def swapped(value):
    return lax.ppermute(value, "core", [(0, 1), (1, 0)])


def pick(value, index, axis=0):
    return lax.dynamic_index_in_dim(value, index, axis, keepdims=False)


def exchanged(state, step, extra=()):
    beside = [turned_by(state, "cy", step * s) for s in range(1, 4)]
    beside, extra = lax.optimization_barrier((beside, extra))
    row = pl.pallas_call(
        lambda *refs: row_kernel(step > 0, *refs),
        out_shape=jax.ShapeDtypeStruct(state.shape, state.dtype),
        name="row_state",
    )(state, *beside)
    return beside + [moved_by(row, "cx", step * s) for s in range(1, 3)], extra


def column_strip(out_weight, share, cx):
    cy, z = lax.axis_index("cy"), lax.axis_index("z")
    at = (cx * HEAD, (z - cy) % 4 * 2 * share)
    sent = lax.dynamic_slice(out_weight, at, (HEAD, 2 * share))
    pairs = [(4 * y + (i + y) % 4, 4 * y + i) for y in range(4) for i in range(4)]
    return lax.ppermute(sent, ("cy", "z"), pairs)


def column_pieces(strip, share, core):
    mine = lax.dynamic_slice(strip, (0, core * share), (HEAD, share))
    other = lax.dynamic_slice(strip, (0, (1 - core) * share), (HEAD, share))
    both = jnp.stack([mine, swapped(other)])
    return jnp.stack([both] + [turned_by(both, "cx", s) for s in range(1, 4)])


def row_sum(mine, cy):
    got = [turned_by(pick(mine, (cy + s) % 4), "cy", s) for s in range(1, 4)]
    height, part = mine.shape[1:]
    block = (CHUNK, part)
    return pl.pallas_call(
        sum_kernel,
        grid_spec=pltpu.PrefetchScalarGridSpec(
            num_scalar_prefetch=1,
            grid=(height // CHUNK,),
            in_specs=[pl.BlockSpec((1, *block), lambda i, p: (p[0], i, 0))]
            + [pl.BlockSpec(block, lambda i, p: (i, 0))] * 3,
            out_specs=pl.BlockSpec(block, lambda i, p: (i, 0)),
        ),
        out_shape=jax.ShapeDtypeStruct((height, part), F32),
        compiler_params=params(),
        name="last_sum",
    )(cy[None], mine, *got)


def body(queries, keys, values, doc_ids, out_weight, grad_out):
    rows, width = queries.shape
    blocks = rows // CHUNK
    groups = lax.axis_size(TENSOR)
    share = grad_out.shape[1]
    size = width
    payload = jax.ShapeDtypeStruct((size + 16, HEAD), BF16)
    cx, cy = lax.axis_index("cx"), lax.axis_index("cy")
    z, core = lax.axis_index("z"), lax.axis_index("core")

    above = turned_by(grad_out, "z", -1)
    below = turned_by(grad_out, "z", 1)
    beside = swapped(grad_out)

    docs = doc_ids.astype(F32)
    dcol = jnp.broadcast_to(docs[:, None], (rows, HEAD))
    drow = docs[None, :]
    chunked = docs.reshape(blocks, CHUNK)
    place = cy.astype(F32)[None]
    table = jnp.concatenate([chunked[:, 0], chunked[:, -1], place, 3 - place, jnp.zeros((6,), F32)])
    table = jnp.broadcast_to(table[:, None], (16, HEAD))

    tail = pl.pallas_call(tail_kernel, out_shape=payload, name="tail")(keys, values, dcol, table)
    strip = column_strip(out_weight, share, cx)
    arrived, strip = exchanged(tail, 1, strip)
    own = column_pieces(strip, share, core)
    ready = (arrived, above, below, beside, own)
    arrived, above, below, beside, own = lax.optimization_barrier(ready)

    row_block = pl.BlockSpec((1, CHUNK), lambda i: (0, i))
    state_block = pl.BlockSpec((1, size, HEAD), lambda i: (i, 0, 0))
    opened, low, turned, states = pl.pallas_call(
        forward_kernel,
        grid=(blocks,),
        in_specs=[rows_of(width)] * 3
        + [rows_of(HEAD), row_block, whole(table.shape)]
        + [whole(payload.shape)] * len(arrived),
        out_specs=[
            rows_of(width),
            rows_of(width),
            pl.BlockSpec((width, CHUNK), lambda i: (0, i)),
            state_block,
        ],
        out_shape=[
            jax.ShapeDtypeStruct((rows, width), F32),
            jax.ShapeDtypeStruct((rows, width), BF16),
            jax.ShapeDtypeStruct((width, rows), BF16),
            jax.ShapeDtypeStruct((blocks, size, HEAD), BF16),
        ],
        scratch_shapes=[pltpu.VMEM((size, HEAD), F32)],
        compiler_params=params(),
        name="forward",
    )(queries, keys, values, dcol, drow, table, *arrived)

    low_whole = lax.all_gather(low, TENSOR, axis=0)

    half_rows = rows // 2
    far_a = turned_by(above[:half_rows], "z", -1)
    far_b = turned_by(below[half_rows:], "z", 1)
    near = [grad_out, beside, above, swapped(above), below, swapped(below)]
    lines = [(z + s) % 4 for s in (0, 0, 1, 1, 3, 3, 2, 2)]
    sides = [core if p % 2 == 0 else 1 - core for p in range(8)]
    places = jnp.stack([2 * a + b for a, b in zip(lines, sides)])

    def weight_block(p):
        return pl.BlockSpec((width, share), lambda i, at: (0, at[p]))

    def some_rows(columns):
        return pl.BlockSpec((CHUNK, columns), lambda i, at: (i, 0))

    def column_block(first):
        def index(g, at):
            return (at[first + g] // 2, at[first + g] % 2, 0, 0)

        return pl.BlockSpec((1, 2, width, share // 2), index)

    held = pl.BlockSpec(memory_space=pl.ANY)
    term = jax.ShapeDtypeStruct((4, 4, width, share // 2), BF16)
    started = pl.pallas_call(
        near_weight_kernel,
        grid_spec=pltpu.PrefetchScalarGridSpec(
            num_scalar_prefetch=1,
            grid=(6,),
            in_specs=[whole((width, rows))] + [held] * 6,
            out_specs=column_block(0),
            scratch_shapes=[pltpu.VMEM((2, rows, share), BF16), pltpu.SemaphoreType.DMA((2,))],
        ),
        out_shape=term,
        compiler_params=params(),
        name="near_weight",
    )(places, turned, *near)
    started, far_a, far_b, own = lax.optimization_barrier((started, far_a, far_b, own))
    right = turned_by(own, "cy", -1)
    left = turned_by(own, "cy", 1)
    far = [far_a, far_b, swapped(far_a), swapped(far_b)]
    term = pl.pallas_call(
        far_weight_kernel,
        grid_spec=pltpu.PrefetchScalarGridSpec(
            num_scalar_prefetch=1,
            grid=(2,),
            in_specs=[whole((width, rows))] + [whole((half_rows, share))] * 4 + [held],
            out_specs=column_block(6),
        ),
        out_shape=term,
        input_output_aliases={6: 0},
        compiler_params=params(),
        name="far_weight",
    )(places, turned, *far, started)
    grad_part = lax.psum_scatter(term, "cx", scatter_dimension=0, tiled=True)[0]

    near_sum = pl.pallas_call(
        near_cotangent_kernel,
        grid_spec=pltpu.PrefetchScalarGridSpec(
            num_scalar_prefetch=1,
            grid=(blocks,),
            in_specs=[some_rows(share)] * 6 + [weight_block(p) for p in range(6)],
            out_specs=some_rows(width),
        ),
        out_shape=jax.ShapeDtypeStruct((rows, width), F32),
        compiler_params=params(),
        name="near_cotangent",
    )(places, *near, *[out_weight] * 6)

    upper = pl.BlockSpec((CHUNK, share), lambda i, at: (jnp.minimum(i, blocks // 2 - 1), 0))
    lower = pl.BlockSpec((CHUNK, share), lambda i, at: (jnp.maximum(i - blocks // 2, 0), 0))
    grad_opened, head = pl.pallas_call(
        cotangent_kernel,
        grid_spec=pltpu.PrefetchScalarGridSpec(
            num_scalar_prefetch=1,
            grid=(blocks,),
            in_specs=[some_rows(width), upper, lower, upper, lower]
            + [weight_block(6), weight_block(7)]
            + [some_rows(width), some_rows(width), some_rows(HEAD), whole(table.shape)],
            out_specs=[some_rows(width), whole(payload.shape)],
            scratch_shapes=[pltpu.VMEM((size, HEAD), F32)],
        ),
        out_shape=[jax.ShapeDtypeStruct((rows, width), F32), payload],
        compiler_params=params(),
        name="cotangent",
    )(places, near_sum, *far, out_weight, out_weight, opened, queries, dcol, table)

    returned, _ = exchanged(head, -1)

    returned, right, left = lax.optimization_barrier((returned, right, left))
    across_a = turned_by(right[:2], "cy", -1)
    across_b = turned_by(left[2:], "cy", 1)

    grad_query = pl.pallas_call(
        query_kernel,
        grid=(blocks,),
        in_specs=[rows_of(width)] * 3
        + [rows_of(HEAD), row_block, whole(table.shape), state_block],
        out_specs=rows_of(width),
        out_shape=jax.ShapeDtypeStruct((rows, width), BF16),
        compiler_params=params(),
        name="grad_query",
    )(grad_opened, keys, values, dcol, drow, table, states)

    back_row = pl.BlockSpec((1, CHUNK), lambda i: (0, blocks - 1 - i))
    grad_key, grad_value = pl.pallas_call(
        key_value_kernel,
        grid=(blocks,),
        in_specs=[rows_of(width, blocks)] * 4
        + [rows_of(HEAD, blocks), back_row, whole(table.shape)]
        + [whole(payload.shape)] * len(returned),
        out_specs=[rows_of(width, blocks)] * 2,
        out_shape=[jax.ShapeDtypeStruct((rows, width), BF16)] * 2,
        scratch_shapes=[pltpu.VMEM((size, HEAD), F32)],
        compiler_params=params(),
        name="grad_key_value",
    )(grad_opened, queries, keys, values, dcol, drow, table, *returned)

    around = [2 * ((z + cy + s) % 4) + (core if o == 0 else 1 - core) for s in range(4) for o in range(2)]
    heads_at = [(cx - s) % 4 for s in range(4)]
    attended = pl.pallas_call(
        attended_kernel,
        grid_spec=pltpu.PrefetchScalarGridSpec(
            num_scalar_prefetch=1,
            grid=(blocks,),
            in_specs=[pl.BlockSpec((groups, CHUNK, width), lambda i, at: (0, i, 0))] + [held] * 5,
            out_specs=pl.BlockSpec((CHUNK, share), lambda i, at: (i, 0)),
            scratch_shapes=[
                pltpu.VMEM((groups, width, share), BF16),
                pltpu.SemaphoreType.DMA((32,)),
            ],
        ),
        out_shape=jax.ShapeDtypeStruct((rows, share), BF16),
        compiler_params=params(),
        name="attended",
    )(jnp.stack(around + heads_at), low_whole, own, right, left, across_a, across_b)
    grad_part, attended, grad_key = lax.optimization_barrier((grad_part, attended, grad_key))
    grad_weight = row_sum(grad_part, cy)
    return attended, grad_query, grad_key, grad_value, grad_weight


def solution(mesh):
    finer = Mesh(mesh.devices.reshape(4, 4, 4, 2), ("cx", "cy", "z", "core"))
    by_both = P(CTX, TENSOR)
    return jax.shard_map(
        body,
        mesh=finer,
        in_specs=(by_both, by_both, by_both, P(CTX), P(TENSOR, None), by_both),
        out_specs=(by_both, by_both, by_both, by_both, P(TENSOR, CTX)),
        check_vma=False,
    )
```

```python
import jax
import jax.numpy as jnp
from jax import lax
from jax.experimental import pallas as pl
from jax.experimental.pallas import tpu as pltpu
from jax.sharding import Mesh
from jax.sharding import PartitionSpec as P

HEAD = 128
CHUNK = 256
CTX = ("cx", "cy")
TENSOR = ("z", "core")
EPSILON = 1e-06
F32 = jnp.float32
BF16 = jnp.bfloat16
NT = (((1,), (1,)), ((), ()))
TN = (((0,), (0,)), ((), ()))
NN = (((1,), (0,)), ((), ()))


def dot(a, b, dims):
    return lax.dot_general(a, b, dims, preferred_element_type=F32)


def whole(shape):
    return pl.BlockSpec(shape, lambda *_: (0,) * len(shape))


def rows_of(width, count=None):
    if count is None:
        return pl.BlockSpec((CHUNK, width), lambda i: (i, 0))
    return pl.BlockSpec((CHUNK, width), lambda i: (count - 1 - i, 0))


def head_cols(h):
    return slice(h * HEAD, (h + 1) * HEAD)


def params():
    return pltpu.CompilerParams(vmem_limit_bytes=56 << 20, dimension_semantics=("arbitrary",))


def state_of(ref):
    return ref[:-16, :].astype(F32), ref[-16:-15, :].astype(F32)


def entering_state(beside, rows, doc, place):
    total = None
    for s, ref in enumerate(beside):
        state, found = state_of(ref)
        part = jnp.where((found == doc) & (place > s + 0.5), state, 0.0)
        total = part if total is None else total + part
    for ref in rows:
        state, found = state_of(ref)
        total = total + jnp.where(found == doc, state, 0.0)
    return total


def row_kernel(latest, *refs):
    states = [state_of(ref) for ref in refs[:-1]]
    out = refs[-1]
    doc = states[0][1]
    for _, found in states[1:]:
        doc = jnp.maximum(doc, found) if latest else jnp.minimum(doc, found)
    total = None
    for state, found in states:
        part = jnp.where(found == doc, state, 0.0)
        total = part if total is None else total + part
    out[:-16, :] = total.astype(BF16)
    out[-16:, :] = jnp.broadcast_to(doc, (16, HEAD)).astype(BF16)


def tail_kernel(k, v, dcol, table, out):
    heads = k.shape[1] // HEAD
    last = table[7:8, :]
    tail = dcol[...] == last
    for h in range(heads):
        c = head_cols(h)
        kept = jnp.where(tail, k[:, c].astype(F32), 0.0).astype(BF16)
        out[c, :] = dot(kept, v[:, c], TN).astype(BF16)
    out[heads * HEAD :, :] = jnp.broadcast_to(last, (16, HEAD)).astype(BF16)


def forward_kernel(q, k, v, dcol, drow, table, *refs):
    arrived, (opened, low, turned, states, carry) = refs[:-5], refs[-5:]
    i = pl.program_id(0)
    heads = q.shape[1] // HEAD
    first = table[pl.ds(i, 1), :]
    following = table[pl.ds(i + 1, 1), :]

    @pl.when(i == 0)
    def _():
        carry[...] = entering_state(arrived[:3], arrived[3:], first, table[8:9, :])

    docs = dcol[...]
    joined = docs == first
    tail = docs == following
    keep = following == first
    t = lax.broadcasted_iota(jnp.int32, (CHUNK, CHUNK), 0)
    u = lax.broadcasted_iota(jnp.int32, (CHUNK, CHUNK), 1)
    mask = (t >= u) & (docs[:, :1] == drow[...])
    for h in range(heads):
        c = head_cols(h)
        qh, kh, vh = q[:, c], k[:, c], v[:, c]
        state = carry[c, :]
        state_low = state.astype(BF16)
        states[0, c, :] = state_low
        scores = jnp.where(mask, dot(qh, kh, NT), 0.0).astype(BF16)
        out = dot(scores, vh, NN) + jnp.where(joined, dot(qh, state_low, NN), 0.0)
        opened[:, c] = out
        inverse = lax.rsqrt(jnp.mean(out * out, axis=-1, keepdims=True) + EPSILON)
        normed = (out * inverse).astype(BF16)
        low[:, c] = normed
        turned[c, :] = normed.T
        kept = jnp.where(tail, kh.astype(F32), 0.0).astype(BF16)
        carry[c, :] = jnp.where(keep, state, 0.0) + dot(kept, vh, TN)


def cotangent_kernel(grad, weight, opened, q, dcol, table, grad_opened, out, carry):
    i = pl.program_id(0)
    heads = q.shape[1] // HEAD
    width = grad.shape[2]
    gn = dot(grad[0], weight[:, :width], NT)
    for j in range(1, grad.shape[0]):
        gn = gn + dot(grad[j], weight[:, j * width : (j + 1) * width], NT)

    @pl.when(i == 0)
    def _():
        carry[...] = jnp.zeros_like(carry)

    first = table[0:1, :]
    starts = dcol[...] == first
    for h in range(heads):
        c = head_cols(h)
        opened_h = opened[:, c]
        gh = gn[:, c]
        inverse = lax.rsqrt(jnp.mean(opened_h * opened_h, axis=-1, keepdims=True) + EPSILON)
        normed = opened_h * inverse
        go = inverse * (gh - normed * jnp.mean(gh * normed, axis=-1, keepdims=True))
        grad_opened[:, c] = go
        kept = jnp.where(starts, q[:, c].astype(F32), 0.0).astype(BF16)
        carry[c, :] += dot(kept, go.astype(BF16), TN)

    @pl.when(i == pl.num_programs(0) - 1)
    def _():
        size = heads * HEAD
        out[:size, :] = carry[...].astype(BF16)
        out[size:, :] = jnp.broadcast_to(first, (16, HEAD)).astype(BF16)


def split(value):
    high = value.astype(BF16)
    return high, (value - high.astype(F32)).astype(BF16)


def query_kernel(go, k, v, dcol, drow, table, states, out):
    i = pl.program_id(0)
    heads = k.shape[1] // HEAD
    first = table[pl.ds(i, 1), :]
    docs = dcol[...]
    joined = docs == first
    t = lax.broadcasted_iota(jnp.int32, (CHUNK, CHUNK), 0)
    u = lax.broadcasted_iota(jnp.int32, (CHUNK, CHUNK), 1)
    mask = (t >= u) & (docs[:, :1] == drow[...])
    for h in range(heads):
        c = head_cols(h)
        high, rest = split(go[:, c])
        vh = v[:, c]
        both = jnp.concatenate([high, rest], axis=1)
        twice = jnp.concatenate([vh, vh], axis=1)
        scores = jnp.where(mask, dot(both, twice, NT), 0.0).astype(BF16)
        carried = jnp.where(joined, dot(high, states[0, c, :], NT), 0.0)
        out[:, c] = (dot(scores, k[:, c], NN) + carried).astype(BF16)


def key_value_kernel(go, q, k, v, dcol, drow, table, *refs):
    arrived, (grad_k, grad_v, carry) = refs[:-3], refs[-3:]
    step = pl.program_id(0)
    i = pl.num_programs(0) - 1 - step
    heads = k.shape[1] // HEAD
    last = table[pl.ds(4 + i, 1), :]
    previous = table[pl.ds(3 + i, 1), :]

    @pl.when(step == 0)
    def _():
        carry[...] = entering_state(arrived[:3], arrived[3:], last, table[9:10, :])

    docs = dcol[...]
    joined = docs == last
    ahead = docs == previous
    keep = previous == last
    u = lax.broadcasted_iota(jnp.int32, (CHUNK, CHUNK), 0)
    t = lax.broadcasted_iota(jnp.int32, (CHUNK, CHUNK), 1)
    mask = (t >= u) & (docs[:, :1] == drow[...])
    for h in range(heads):
        c = head_cols(h)
        high, rest = split(go[:, c])
        qh, kh, vh = q[:, c], k[:, c], v[:, c]
        state = carry[c, :]
        state_low = state.astype(BF16)
        both = jnp.concatenate([high, rest], axis=1)
        twice = jnp.concatenate([vh, vh], axis=1)
        scores = jnp.where(mask, dot(kh, qh, NT), 0.0).astype(BF16)
        grad_scores = jnp.where(mask, dot(twice, both, NT), 0.0).astype(BF16)
        grad_v[:, c] = (
            dot(scores, high, NN) + jnp.where(joined, dot(kh, state_low, NN), 0.0)
        ).astype(BF16)
        grad_k[:, c] = (
            dot(grad_scores, qh, NN) + jnp.where(joined, dot(vh, state_low, NT), 0.0)
        ).astype(BF16)
        kept = jnp.where(ahead, qh.astype(F32), 0.0).astype(BF16)
        carry[c, :] = jnp.where(keep, state, 0.0) + dot(kept, high, TN)


def put_columns(part, out):
    low = part.astype(BF16)
    half = low.shape[1] // 2
    out[0, 0] = low[:, :half]
    out[0, 1] = low[:, half:]


def weight_kernel(turned, grad, out):
    put_columns(dot(turned[...], grad[0], NN), out)


def sum_kernel(place, own, *refs):
    total = own[0].astype(F32)
    for ref in refs[:-1]:
        total = total + ref[...].astype(F32)
    refs[-1][...] = total


def attended_kernel(places, *refs):
    near, far, columns_of = refs[:6], refs[6:10], refs[10:18]
    out, columns, sems = refs[18:]
    i = pl.program_id(0)

    def copies():
        for y in range(4):
            for x in range(4):
                for o in range(2):
                    group = places[2 * y + o]
                    row = pl.multiple_of(places[8 + x] * HEAD, HEAD)
                    to = columns.at[group, pl.ds(row, HEAD)]
                    piece = columns_of[2 * y + x // 2].at[x % 2, o]
                    yield pltpu.make_async_copy(piece, to, sems.at[8 * y + 2 * x + o])

    @pl.when(i == 0)
    def _():
        for copy in copies():
            copy.start()
        for copy in copies():
            copy.wait()

    early = i < pl.num_programs(0) // 2
    pieces = [ref[...] for ref in near]
    pieces += [jnp.where(early, far[p][...], far[p + 1][...]) for p in (0, 2)]
    total = None
    for p, piece in enumerate(pieces):
        part = dot(piece, columns[places[12 + p]], NN)
        total = part if total is None else total + part
    out[...] = total.astype(BF16)


def turned_by(value, axis, step):
    size = lax.axis_size(axis)
    return lax.ppermute(value, axis, [(i, (i + step) % size) for i in range(size)])


def moved_by(value, axis, step):
    size = lax.axis_size(axis)
    pairs = [(i, i + step) for i in range(size) if 0 <= i + step < size]
    return lax.ppermute(value, axis, pairs)


def swapped(value):
    return lax.ppermute(value, "core", [(0, 1), (1, 0)])


def pick(value, index, axis=0):
    return lax.dynamic_index_in_dim(value, index, axis, keepdims=False)


def exchanged(state, step, extra=()):
    beside = [turned_by(state, "cy", step * s) for s in range(1, 4)]
    beside, extra = lax.optimization_barrier((beside, extra))
    row = pl.pallas_call(
        lambda *refs: row_kernel(step > 0, *refs),
        out_shape=jax.ShapeDtypeStruct(state.shape, state.dtype),
        name="row_state",
    )(state, *beside)
    return beside + [moved_by(row, "cx", step * s) for s in range(1, 3)], extra


def column_strip(out_weight, share, cx):
    cy, z = lax.axis_index("cy"), lax.axis_index("z")
    at = (cx * HEAD, (z - cy) % 4 * 2 * share)
    sent = lax.dynamic_slice(out_weight, at, (HEAD, 2 * share))
    pairs = [(4 * y + (i + y) % 4, 4 * y + i) for y in range(4) for i in range(4)]
    return lax.ppermute(sent, ("cy", "z"), pairs)


def column_pieces(strip, share, core):
    mine = lax.dynamic_slice(strip, (0, core * share), (HEAD, share))
    other = lax.dynamic_slice(strip, (0, (1 - core) * share), (HEAD, share))
    both = jnp.stack([mine, swapped(other)])
    lines = [both] + [turned_by(both, "cx", s) for s in range(1, 4)]
    return jnp.stack(lines[:2]), jnp.stack(lines[2:])


def row_sum(mine, cy):
    got = [turned_by(pick(mine, (cy + s) % 4), "cy", s) for s in range(1, 4)]
    height, part = mine.shape[1:]
    block = (CHUNK, part)
    return pl.pallas_call(
        sum_kernel,
        grid_spec=pltpu.PrefetchScalarGridSpec(
            num_scalar_prefetch=1,
            grid=(height // CHUNK,),
            in_specs=[pl.BlockSpec((1, *block), lambda i, p: (p[0], i, 0))]
            + [pl.BlockSpec(block, lambda i, p: (i, 0))] * 3,
            out_specs=pl.BlockSpec(block, lambda i, p: (i, 0)),
        ),
        out_shape=jax.ShapeDtypeStruct((height, part), F32),
        compiler_params=params(),
        name="last_sum",
    )(cy[None], mine, *got)


def body(queries, keys, values, doc_ids, out_weight, grad_out):
    rows, width = queries.shape
    blocks = rows // CHUNK
    groups = lax.axis_size(TENSOR)
    share = grad_out.shape[1]
    size = width
    payload = jax.ShapeDtypeStruct((size + 16, HEAD), BF16)
    cx, cy = lax.axis_index("cx"), lax.axis_index("cy")
    z, core = lax.axis_index("z"), lax.axis_index("core")

    grad_whole = lax.all_gather(grad_out, TENSOR, axis=0)

    docs = doc_ids.astype(F32)
    dcol = jnp.broadcast_to(docs[:, None], (rows, HEAD))
    drow = docs[None, :]
    chunked = docs.reshape(blocks, CHUNK)
    place = cy.astype(F32)[None]
    table = jnp.concatenate([chunked[:, 0], chunked[:, -1], place, 3 - place, jnp.zeros((6,), F32)])
    table = jnp.broadcast_to(table[:, None], (16, HEAD))

    tail = pl.pallas_call(tail_kernel, out_shape=payload, name="tail")(keys, values, dcol, table)
    strip = column_strip(out_weight, share, cx)
    arrived, strip = exchanged(tail, 1, strip)
    own = column_pieces(strip, share, core)
    arrived, own = lax.optimization_barrier((arrived, own))

    row_block = pl.BlockSpec((1, CHUNK), lambda i: (0, i))
    state_block = pl.BlockSpec((1, size, HEAD), lambda i: (i, 0, 0))
    opened, low, turned, states = pl.pallas_call(
        forward_kernel,
        grid=(blocks,),
        in_specs=[rows_of(width)] * 3
        + [rows_of(HEAD), row_block, whole(table.shape)]
        + [whole(payload.shape)] * len(arrived),
        out_specs=[
            rows_of(width),
            rows_of(width),
            pl.BlockSpec((width, CHUNK), lambda i: (0, i)),
            state_block,
        ],
        out_shape=[
            jax.ShapeDtypeStruct((rows, width), F32),
            jax.ShapeDtypeStruct((rows, width), BF16),
            jax.ShapeDtypeStruct((width, rows), BF16),
            jax.ShapeDtypeStruct((blocks, size, HEAD), BF16),
        ],
        scratch_shapes=[pltpu.VMEM((size, HEAD), F32)],
        compiler_params=params(),
        name="forward",
    )(queries, keys, values, dcol, drow, table, *arrived)

    early = [turned_by(own[0], "cy", s) for s in (-1, 1)]
    turned, early = lax.optimization_barrier((turned, early))
    later = [turned_by(own[1], "cy", s) for s in (-1, 1)]

    term = pl.pallas_call(
        weight_kernel,
        grid=(groups,),
        in_specs=[whole((width, rows)), pl.BlockSpec((1, rows, share), lambda j: (j, 0, 0))],
        out_specs=pl.BlockSpec((1, 2, width, share // 2), lambda j: (j // 2, j % 2, 0, 0)),
        out_shape=jax.ShapeDtypeStruct((4, 4, width, share // 2), BF16),
        compiler_params=params(),
        name="weight_grad",
    )(turned, grad_whole)
    term, low = lax.optimization_barrier((term, low))
    grad_part = lax.psum_scatter(term, "cx", scatter_dimension=0, tiled=True)[0]

    half_rows = rows // 2
    above = turned_by(low, "z", -1)
    below = turned_by(low, "z", 1)
    far_a = turned_by(above[:half_rows], "z", -1)
    far_b = turned_by(below[half_rows:], "z", 1)
    near = [low, swapped(low), above, swapped(above), below, swapped(below)]
    far = [far_a, far_b, swapped(far_a), swapped(far_b)]

    grad_opened, head = pl.pallas_call(
        cotangent_kernel,
        grid=(blocks,),
        in_specs=[
            pl.BlockSpec((groups, CHUNK, share), lambda i: (0, i, 0)),
            whole(out_weight.shape),
            rows_of(width),
            rows_of(width),
            rows_of(HEAD),
            whole(table.shape),
        ],
        out_specs=[rows_of(width), whole(payload.shape)],
        out_shape=[jax.ShapeDtypeStruct((rows, width), F32), payload],
        scratch_shapes=[pltpu.VMEM((size, HEAD), F32)],
        compiler_params=params(),
        name="cotangent",
    )(grad_whole, out_weight, opened, queries, dcol, table)
    head, later = lax.optimization_barrier((head, later))
    returned, _ = exchanged(head, -1)

    returned, early, later = lax.optimization_barrier((returned, early, later))
    across = (turned_by(early[0], "cy", -1), turned_by(later[1], "cy", 1))
    columns = [*own, early[0], later[0], *across, early[1], later[1]]

    grad_query = pl.pallas_call(
        query_kernel,
        grid=(blocks,),
        in_specs=[rows_of(width)] * 3
        + [rows_of(HEAD), row_block, whole(table.shape), state_block],
        out_specs=rows_of(width),
        out_shape=jax.ShapeDtypeStruct((rows, width), BF16),
        compiler_params=params(),
        name="grad_query",
    )(grad_opened, keys, values, dcol, drow, table, states)

    back_row = pl.BlockSpec((1, CHUNK), lambda i: (0, blocks - 1 - i))
    grad_key, grad_value = pl.pallas_call(
        key_value_kernel,
        grid=(blocks,),
        in_specs=[rows_of(width, blocks)] * 4
        + [rows_of(HEAD, blocks), back_row, whole(table.shape)]
        + [whole(payload.shape)] * len(returned),
        out_specs=[rows_of(width, blocks)] * 2,
        out_shape=[jax.ShapeDtypeStruct((rows, width), BF16)] * 2,
        scratch_shapes=[pltpu.VMEM((size, HEAD), F32)],
        compiler_params=params(),
        name="grad_key_value",
    )(grad_opened, queries, keys, values, dcol, drow, table, *returned)

    sides = (core, 1 - core)
    around = [2 * ((z + cy + s) % 4) + side for s in range(4) for side in sides]
    heads_at = [(cx - s) % 4 for s in range(4)]
    groups_at = [2 * ((z + s) % 4) + side for s in (0, 1, 3, 2) for side in sides]
    held = pl.BlockSpec(memory_space=pl.ANY)
    every = pl.BlockSpec((CHUNK, width), lambda i, at: (i, 0))
    upper = pl.BlockSpec((CHUNK, width), lambda i, at: (jnp.minimum(i, blocks // 2 - 1), 0))
    lower = pl.BlockSpec((CHUNK, width), lambda i, at: (jnp.maximum(i - blocks // 2, 0), 0))
    attended = pl.pallas_call(
        attended_kernel,
        grid_spec=pltpu.PrefetchScalarGridSpec(
            num_scalar_prefetch=1,
            grid=(blocks,),
            in_specs=[every] * 6 + [upper, lower] * 2 + [held] * 8,
            out_specs=pl.BlockSpec((CHUNK, share), lambda i, at: (i, 0)),
            scratch_shapes=[
                pltpu.VMEM((groups, width, share), BF16),
                pltpu.SemaphoreType.DMA((32,)),
            ],
        ),
        out_shape=jax.ShapeDtypeStruct((rows, share), BF16),
        compiler_params=params(),
        name="attended",
    )(jnp.stack(around + heads_at + groups_at), *near, *far, *columns)
    grad_part, attended, grad_key = lax.optimization_barrier((grad_part, attended, grad_key))
    grad_weight = row_sum(grad_part, cy)
    return attended, grad_query, grad_key, grad_value, grad_weight


def solution(mesh):
    finer = Mesh(mesh.devices.reshape(4, 4, 4, 2), ("cx", "cy", "z", "core"))
    by_both = P(CTX, TENSOR)
    return jax.shard_map(
        body,
        mesh=finer,
        in_specs=(by_both, by_both, by_both, P(CTX), P(TENSOR, None), by_both),
        out_specs=(by_both, by_both, by_both, by_both, P(TENSOR, CTX)),
        check_vma=False,
    )
```

```python
import jax
import jax.numpy as jnp
from jax import lax
from jax.experimental import pallas as pl
from jax.experimental.pallas import tpu as pltpu
from jax.sharding import Mesh
from jax.sharding import PartitionSpec as P

HEAD = 128
CHUNK = 256
CTX = ("cx", "cy")
TENSOR = ("z", "core")
EPSILON = 1e-06
F32 = jnp.float32
BF16 = jnp.bfloat16
NT = (((1,), (1,)), ((), ()))
TN = (((0,), (0,)), ((), ()))
NN = (((1,), (0,)), ((), ()))


def dot(a, b, dims):
    return lax.dot_general(a, b, dims, preferred_element_type=F32)


def whole(shape):
    return pl.BlockSpec(shape, lambda *_: (0,) * len(shape))


def rows_of(width, count=None):
    if count is None:
        return pl.BlockSpec((CHUNK, width), lambda i: (i, 0))
    return pl.BlockSpec((CHUNK, width), lambda i: (count - 1 - i, 0))


def head_cols(h):
    return slice(h * HEAD, (h + 1) * HEAD)


def params():
    return pltpu.CompilerParams(vmem_limit_bytes=56 << 20, dimension_semantics=("arbitrary",))


def state_of(ref):
    return ref[:-16, :].astype(F32), ref[-16:-15, :].astype(F32)


def entering_state(beside, rows, doc, place):
    total = None
    for s, ref in enumerate(beside):
        state, found = state_of(ref)
        part = jnp.where((found == doc) & (place > s + 0.5), state, 0.0)
        total = part if total is None else total + part
    for ref in rows:
        state, found = state_of(ref)
        total = total + jnp.where(found == doc, state, 0.0)
    return total


def row_kernel(latest, *refs):
    states = [state_of(ref) for ref in refs[:-1]]
    out = refs[-1]
    doc = states[0][1]
    for _, found in states[1:]:
        doc = jnp.maximum(doc, found) if latest else jnp.minimum(doc, found)
    total = None
    for state, found in states:
        part = jnp.where(found == doc, state, 0.0)
        total = part if total is None else total + part
    out[:-16, :] = total.astype(BF16)
    out[-16:, :] = jnp.broadcast_to(doc, (16, HEAD)).astype(BF16)


def tail_kernel(k, v, dcol, table, out):
    heads = k.shape[1] // HEAD
    last = table[7:8, :]
    tail = dcol[...] == last
    for h in range(heads):
        c = head_cols(h)
        kept = jnp.where(tail, k[:, c].astype(F32), 0.0).astype(BF16)
        out[c, :] = dot(kept, v[:, c], TN).astype(BF16)
    out[heads * HEAD :, :] = jnp.broadcast_to(last, (16, HEAD)).astype(BF16)


def forward_kernel(q, k, v, dcol, drow, table, *refs):
    arrived, (opened, low, turned, states, carry) = refs[:-5], refs[-5:]
    i = pl.program_id(0)
    heads = q.shape[1] // HEAD
    first = table[pl.ds(i, 1), :]
    following = table[pl.ds(i + 1, 1), :]

    @pl.when(i == 0)
    def _():
        carry[...] = entering_state(arrived[:3], arrived[3:], first, table[8:9, :])

    docs = dcol[...]
    joined = docs == first
    tail = docs == following
    keep = following == first
    t = lax.broadcasted_iota(jnp.int32, (CHUNK, CHUNK), 0)
    u = lax.broadcasted_iota(jnp.int32, (CHUNK, CHUNK), 1)
    mask = (t >= u) & (docs[:, :1] == drow[...])
    for h in range(heads):
        c = head_cols(h)
        qh, kh, vh = q[:, c], k[:, c], v[:, c]
        state = carry[c, :]
        state_low = state.astype(BF16)
        states[0, c, :] = state_low
        scores = jnp.where(mask, dot(qh, kh, NT), 0.0).astype(BF16)
        out = dot(scores, vh, NN) + jnp.where(joined, dot(qh, state_low, NN), 0.0)
        opened[:, c] = out
        inverse = lax.rsqrt(jnp.mean(out * out, axis=-1, keepdims=True) + EPSILON)
        normed = (out * inverse).astype(BF16)
        low[:, c] = normed
        turned[c, :] = normed.T
        kept = jnp.where(tail, kh.astype(F32), 0.0).astype(BF16)
        carry[c, :] = jnp.where(keep, state, 0.0) + dot(kept, vh, TN)


def cotangent_kernel(grad, weight, opened, q, dcol, table, grad_opened, out, carry):
    i = pl.program_id(0)
    heads = q.shape[1] // HEAD
    width = grad.shape[2]
    gn = dot(grad[0], weight[:, :width], NT)
    for j in range(1, grad.shape[0]):
        gn = gn + dot(grad[j], weight[:, j * width : (j + 1) * width], NT)

    @pl.when(i == 0)
    def _():
        carry[...] = jnp.zeros_like(carry)

    first = table[0:1, :]
    starts = dcol[...] == first
    for h in range(heads):
        c = head_cols(h)
        opened_h = opened[:, c]
        gh = gn[:, c]
        inverse = lax.rsqrt(jnp.mean(opened_h * opened_h, axis=-1, keepdims=True) + EPSILON)
        normed = opened_h * inverse
        go = inverse * (gh - normed * jnp.mean(gh * normed, axis=-1, keepdims=True))
        grad_opened[:, c] = go
        kept = jnp.where(starts, q[:, c].astype(F32), 0.0).astype(BF16)
        carry[c, :] += dot(kept, go.astype(BF16), TN)

    @pl.when(i == pl.num_programs(0) - 1)
    def _():
        size = heads * HEAD
        out[:size, :] = carry[...].astype(BF16)
        out[size:, :] = jnp.broadcast_to(first, (16, HEAD)).astype(BF16)


def split(value):
    high = value.astype(BF16)
    return high, (value - high.astype(F32)).astype(BF16)


def query_kernel(go, k, v, dcol, drow, table, states, out):
    i = pl.program_id(0)
    heads = k.shape[1] // HEAD
    first = table[pl.ds(i, 1), :]
    docs = dcol[...]
    joined = docs == first
    t = lax.broadcasted_iota(jnp.int32, (CHUNK, CHUNK), 0)
    u = lax.broadcasted_iota(jnp.int32, (CHUNK, CHUNK), 1)
    mask = (t >= u) & (docs[:, :1] == drow[...])
    for h in range(heads):
        c = head_cols(h)
        high, rest = split(go[:, c])
        vh = v[:, c]
        both = jnp.concatenate([high, rest], axis=1)
        twice = jnp.concatenate([vh, vh], axis=1)
        scores = jnp.where(mask, dot(both, twice, NT), 0.0).astype(BF16)
        carried = jnp.where(joined, dot(high, states[0, c, :], NT), 0.0)
        out[:, c] = (dot(scores, k[:, c], NN) + carried).astype(BF16)


def key_value_kernel(go, q, k, v, dcol, drow, table, *refs):
    arrived, (grad_k, grad_v, carry) = refs[:-3], refs[-3:]
    step = pl.program_id(0)
    i = pl.num_programs(0) - 1 - step
    heads = k.shape[1] // HEAD
    last = table[pl.ds(4 + i, 1), :]
    previous = table[pl.ds(3 + i, 1), :]

    @pl.when(step == 0)
    def _():
        carry[...] = entering_state(arrived[:3], arrived[3:], last, table[9:10, :])

    docs = dcol[...]
    joined = docs == last
    ahead = docs == previous
    keep = previous == last
    u = lax.broadcasted_iota(jnp.int32, (CHUNK, CHUNK), 0)
    t = lax.broadcasted_iota(jnp.int32, (CHUNK, CHUNK), 1)
    mask = (t >= u) & (docs[:, :1] == drow[...])
    for h in range(heads):
        c = head_cols(h)
        high, rest = split(go[:, c])
        qh, kh, vh = q[:, c], k[:, c], v[:, c]
        state = carry[c, :]
        state_low = state.astype(BF16)
        both = jnp.concatenate([high, rest], axis=1)
        twice = jnp.concatenate([vh, vh], axis=1)
        scores = jnp.where(mask, dot(kh, qh, NT), 0.0).astype(BF16)
        grad_scores = jnp.where(mask, dot(twice, both, NT), 0.0).astype(BF16)
        grad_v[:, c] = (
            dot(scores, high, NN) + jnp.where(joined, dot(kh, state_low, NN), 0.0)
        ).astype(BF16)
        grad_k[:, c] = (
            dot(grad_scores, qh, NN) + jnp.where(joined, dot(vh, state_low, NT), 0.0)
        ).astype(BF16)
        kept = jnp.where(ahead, qh.astype(F32), 0.0).astype(BF16)
        carry[c, :] = jnp.where(keep, state, 0.0) + dot(kept, high, TN)


def put_columns(part, out):
    low = part.astype(BF16)
    half = low.shape[1] // 2
    out[0, 0] = low[:, :half]
    out[0, 1] = low[:, half:]


def weight_kernel(turned, grad, out):
    put_columns(dot(turned[...], grad[0], NN), out)


def sum_kernel(place, own, *refs):
    total = own[0].astype(F32)
    for ref in refs[:-1]:
        total = total + ref[...].astype(F32)
    refs[-1][...] = total


def attended_kernel(places, *refs):
    near, far, columns_of = refs[:6], refs[6:10], refs[10:18]
    out, columns, sems = refs[18:]
    i = pl.program_id(0)

    def copies():
        for y in range(4):
            for x in range(4):
                for o in range(2):
                    group = places[2 * y + o]
                    row = pl.multiple_of(places[8 + x] * HEAD, HEAD)
                    to = columns.at[group, pl.ds(row, HEAD)]
                    piece = columns_of[2 * y + x // 2].at[x % 2, o]
                    yield pltpu.make_async_copy(piece, to, sems.at[8 * y + 2 * x + o])

    @pl.when(i == 0)
    def _():
        for copy in copies():
            copy.start()
        for copy in copies():
            copy.wait()

    early = i < pl.num_programs(0) // 2
    pieces = [ref[...] for ref in near]
    pieces += [jnp.where(early, far[p][...], far[p + 1][...]) for p in (0, 2)]
    total = None
    for p, piece in enumerate(pieces):
        part = dot(piece, columns[places[12 + p]], NN)
        total = part if total is None else total + part
    out[...] = total.astype(BF16)


def turned_by(value, axis, step):
    size = lax.axis_size(axis)
    return lax.ppermute(value, axis, [(i, (i + step) % size) for i in range(size)])


def moved_by(value, axis, step):
    size = lax.axis_size(axis)
    pairs = [(i, i + step) for i in range(size) if 0 <= i + step < size]
    return lax.ppermute(value, axis, pairs)


def swapped(value):
    return lax.ppermute(value, "core", [(0, 1), (1, 0)])


def pick(value, index, axis=0):
    return lax.dynamic_index_in_dim(value, index, axis, keepdims=False)


def exchanged(state, step, extra=()):
    beside = [turned_by(state, "cy", step * s) for s in range(1, 4)]
    beside, extra = lax.optimization_barrier((beside, extra))
    row = pl.pallas_call(
        lambda *refs: row_kernel(step > 0, *refs),
        out_shape=jax.ShapeDtypeStruct(state.shape, state.dtype),
        name="row_state",
    )(state, *beside)
    return beside + [moved_by(row, "cx", step * s) for s in range(1, 3)], extra


def column_strip(out_weight, share, cx):
    cy, z = lax.axis_index("cy"), lax.axis_index("z")
    at = (cx * HEAD, (z - cy) % 4 * 2 * share)
    sent = lax.dynamic_slice(out_weight, at, (HEAD, 2 * share))
    pairs = [(4 * y + (i + y) % 4, 4 * y + i) for y in range(4) for i in range(4)]
    return lax.ppermute(sent, ("cy", "z"), pairs)


def column_pieces(strip, share, core):
    mine = lax.dynamic_slice(strip, (0, core * share), (HEAD, share))
    other = lax.dynamic_slice(strip, (0, (1 - core) * share), (HEAD, share))
    both = jnp.stack([mine, swapped(other)])
    lines = [both] + [turned_by(both, "cx", s) for s in range(1, 4)]
    return jnp.stack(lines[:2]), jnp.stack(lines[2:])


def row_sum(mine, cy):
    got = [turned_by(pick(mine, (cy + s) % 4), "cy", s) for s in range(1, 4)]
    height, part = mine.shape[1:]
    block = (CHUNK, part)
    return pl.pallas_call(
        sum_kernel,
        grid_spec=pltpu.PrefetchScalarGridSpec(
            num_scalar_prefetch=1,
            grid=(height // CHUNK,),
            in_specs=[pl.BlockSpec((1, *block), lambda i, p: (p[0], i, 0))]
            + [pl.BlockSpec(block, lambda i, p: (i, 0))] * 3,
            out_specs=pl.BlockSpec(block, lambda i, p: (i, 0)),
        ),
        out_shape=jax.ShapeDtypeStruct((height, part), F32),
        compiler_params=params(),
        name="last_sum",
    )(cy[None], mine, *got)


def body(queries, keys, values, doc_ids, out_weight, grad_out):
    rows, width = queries.shape
    blocks = rows // CHUNK
    groups = lax.axis_size(TENSOR)
    share = grad_out.shape[1]
    size = width
    payload = jax.ShapeDtypeStruct((size + 16, HEAD), BF16)
    cx, cy = lax.axis_index("cx"), lax.axis_index("cy")
    z, core = lax.axis_index("z"), lax.axis_index("core")

    grad_whole = lax.all_gather(grad_out, TENSOR, axis=0)

    docs = doc_ids.astype(F32)
    dcol = jnp.broadcast_to(docs[:, None], (rows, HEAD))
    drow = docs[None, :]
    chunked = docs.reshape(blocks, CHUNK)
    place = cy.astype(F32)[None]
    table = jnp.concatenate([chunked[:, 0], chunked[:, -1], place, 3 - place, jnp.zeros((6,), F32)])
    table = jnp.broadcast_to(table[:, None], (16, HEAD))

    tail = pl.pallas_call(tail_kernel, out_shape=payload, name="tail")(keys, values, dcol, table)
    own = column_pieces(column_strip(out_weight, share, cx), share, core)
    arrived, own = exchanged(tail, 1, own)
    early = [turned_by(own[0], "cy", -1), turned_by(own[1], "cy", 1)]
    arrived, early = lax.optimization_barrier((arrived, early))
    later = [turned_by(own[1], "cy", -1), turned_by(own[0], "cy", 1)]

    row_block = pl.BlockSpec((1, CHUNK), lambda i: (0, i))
    state_block = pl.BlockSpec((1, size, HEAD), lambda i: (i, 0, 0))
    opened, low, turned, states = pl.pallas_call(
        forward_kernel,
        grid=(blocks,),
        in_specs=[rows_of(width)] * 3
        + [rows_of(HEAD), row_block, whole(table.shape)]
        + [whole(payload.shape)] * len(arrived),
        out_specs=[
            rows_of(width),
            rows_of(width),
            pl.BlockSpec((width, CHUNK), lambda i: (0, i)),
            state_block,
        ],
        out_shape=[
            jax.ShapeDtypeStruct((rows, width), F32),
            jax.ShapeDtypeStruct((rows, width), BF16),
            jax.ShapeDtypeStruct((width, rows), BF16),
            jax.ShapeDtypeStruct((blocks, size, HEAD), BF16),
        ],
        scratch_shapes=[pltpu.VMEM((size, HEAD), F32)],
        compiler_params=params(),
        name="forward",
    )(queries, keys, values, dcol, drow, table, *arrived)

    turned, later = lax.optimization_barrier((turned, later))
    across = [turned_by(early[0], "cy", -1), turned_by(early[1], "cy", 1)]

    term = pl.pallas_call(
        weight_kernel,
        grid=(groups,),
        in_specs=[whole((width, rows)), pl.BlockSpec((1, rows, share), lambda j: (j, 0, 0))],
        out_specs=pl.BlockSpec((1, 2, width, share // 2), lambda j: (j // 2, j % 2, 0, 0)),
        out_shape=jax.ShapeDtypeStruct((4, 4, width, share // 2), BF16),
        compiler_params=params(),
        name="weight_grad",
    )(turned, grad_whole)
    term, low = lax.optimization_barrier((term, low))
    grad_part = lax.psum_scatter(term, "cx", scatter_dimension=0, tiled=True)[0]

    half_rows = rows // 2
    above = turned_by(low, "z", -1)
    below = turned_by(low, "z", 1)

    grad_opened, head = pl.pallas_call(
        cotangent_kernel,
        grid=(blocks,),
        in_specs=[
            pl.BlockSpec((groups, CHUNK, share), lambda i: (0, i, 0)),
            whole(out_weight.shape),
            rows_of(width),
            rows_of(width),
            rows_of(HEAD),
            whole(table.shape),
        ],
        out_specs=[rows_of(width), whole(payload.shape)],
        out_shape=[jax.ShapeDtypeStruct((rows, width), F32), payload],
        scratch_shapes=[pltpu.VMEM((size, HEAD), F32)],
        compiler_params=params(),
        name="cotangent",
    )(grad_whole, out_weight, opened, queries, dcol, table)
    head, across, above, below = lax.optimization_barrier((head, across, above, below))
    far_a = turned_by(above[:half_rows], "z", -1)
    far_b = turned_by(below[half_rows:], "z", 1)
    returned, (far_a, far_b, low) = exchanged(head, -1, (far_a, far_b, low))
    near = [low, swapped(low), above, swapped(above), below, swapped(below)]
    far = [far_a, far_b, swapped(far_a), swapped(far_b)]
    columns = [*own, early[0], later[0], *across, later[1], early[1]]

    grad_query = pl.pallas_call(
        query_kernel,
        grid=(blocks,),
        in_specs=[rows_of(width)] * 3
        + [rows_of(HEAD), row_block, whole(table.shape), state_block],
        out_specs=rows_of(width),
        out_shape=jax.ShapeDtypeStruct((rows, width), BF16),
        compiler_params=params(),
        name="grad_query",
    )(grad_opened, keys, values, dcol, drow, table, states)

    sides = (core, 1 - core)
    around = [2 * ((z + cy + s) % 4) + side for s in range(4) for side in sides]
    heads_at = [(cx - s) % 4 for s in range(4)]
    groups_at = [2 * ((z + s) % 4) + side for s in (0, 1, 3, 2) for side in sides]
    held = pl.BlockSpec(memory_space=pl.ANY)
    every = pl.BlockSpec((CHUNK, width), lambda i, at: (i, 0))
    upper = pl.BlockSpec((CHUNK, width), lambda i, at: (jnp.minimum(i, blocks // 2 - 1), 0))
    lower = pl.BlockSpec((CHUNK, width), lambda i, at: (jnp.maximum(i - blocks // 2, 0), 0))
    attended = pl.pallas_call(
        attended_kernel,
        grid_spec=pltpu.PrefetchScalarGridSpec(
            num_scalar_prefetch=1,
            grid=(blocks,),
            in_specs=[every] * 6 + [upper, lower] * 2 + [held] * 8,
            out_specs=pl.BlockSpec((CHUNK, share), lambda i, at: (i, 0)),
            scratch_shapes=[
                pltpu.VMEM((groups, width, share), BF16),
                pltpu.SemaphoreType.DMA((32,)),
            ],
        ),
        out_shape=jax.ShapeDtypeStruct((rows, share), BF16),
        compiler_params=params(),
        name="attended",
    )(jnp.stack(around + heads_at + groups_at), *near, *far, *columns)
    returned, attended = lax.optimization_barrier((returned, attended))

    back_row = pl.BlockSpec((1, CHUNK), lambda i: (0, blocks - 1 - i))
    grad_key, grad_value = pl.pallas_call(
        key_value_kernel,
        grid=(blocks,),
        in_specs=[rows_of(width, blocks)] * 4
        + [rows_of(HEAD, blocks), back_row, whole(table.shape)]
        + [whole(payload.shape)] * len(returned),
        out_specs=[rows_of(width, blocks)] * 2,
        out_shape=[jax.ShapeDtypeStruct((rows, width), BF16)] * 2,
        scratch_shapes=[pltpu.VMEM((size, HEAD), F32)],
        compiler_params=params(),
        name="grad_key_value",
    )(grad_opened, queries, keys, values, dcol, drow, table, *returned)

    grad_part, grad_key = lax.optimization_barrier((grad_part, grad_key))
    grad_weight = row_sum(grad_part, cy)
    return attended, grad_query, grad_key, grad_value, grad_weight


def solution(mesh):
    finer = Mesh(mesh.devices.reshape(4, 4, 4, 2), ("cx", "cy", "z", "core"))
    by_both = P(CTX, TENSOR)
    return jax.shard_map(
        body,
        mesh=finer,
        in_specs=(by_both, by_both, by_both, P(CTX), P(TENSOR, None), by_both),
        out_specs=(by_both, by_both, by_both, by_both, P(TENSOR, CTX)),
        check_vma=False,
    )
```

```python
import jax
import jax.numpy as jnp
from jax import lax
from jax.experimental import pallas as pl
from jax.experimental.pallas import tpu as pltpu
from jax.sharding import Mesh
from jax.sharding import PartitionSpec as P

HEAD = 128
CHUNK = 256
CTX = ("cx", "cy")
TENSOR = ("z", "core")
EPSILON = 1e-06
F32 = jnp.float32
BF16 = jnp.bfloat16
NT = (((1,), (1,)), ((), ()))
TN = (((0,), (0,)), ((), ()))
NN = (((1,), (0,)), ((), ()))


def dot(a, b, dims):
    return lax.dot_general(a, b, dims, preferred_element_type=F32)


def whole(shape):
    return pl.BlockSpec(shape, lambda *_: (0,) * len(shape))


def rows_of(width, count=None):
    if count is None:
        return pl.BlockSpec((CHUNK, width), lambda i: (i, 0))
    return pl.BlockSpec((CHUNK, width), lambda i: (count - 1 - i, 0))


def head_cols(h):
    return slice(h * HEAD, (h + 1) * HEAD)


def params():
    return pltpu.CompilerParams(vmem_limit_bytes=56 << 20, dimension_semantics=("arbitrary",))


def state_of(ref):
    return ref[:-16, :].astype(F32), ref[-16:-15, :].astype(F32)


def entering_state(beside, rows, doc, place):
    total = None
    for s, ref in enumerate(beside):
        state, found = state_of(ref)
        part = jnp.where((found == doc) & (place > s + 0.5), state, 0.0)
        total = part if total is None else total + part
    for ref in rows:
        state, found = state_of(ref)
        total = total + jnp.where(found == doc, state, 0.0)
    return total


def row_kernel(latest, *refs):
    states = [state_of(ref) for ref in refs[:-1]]
    out = refs[-1]
    doc = states[0][1]
    for _, found in states[1:]:
        doc = jnp.maximum(doc, found) if latest else jnp.minimum(doc, found)
    total = None
    for state, found in states:
        part = jnp.where(found == doc, state, 0.0)
        total = part if total is None else total + part
    out[:-16, :] = total.astype(BF16)
    out[-16:, :] = jnp.broadcast_to(doc, (16, HEAD)).astype(BF16)


def tail_kernel(k, v, dcol, table, out):
    heads = k.shape[1] // HEAD
    last = table[7:8, :]
    tail = dcol[...] == last
    for h in range(heads):
        c = head_cols(h)
        kept = jnp.where(tail, k[:, c].astype(F32), 0.0).astype(BF16)
        out[c, :] = dot(kept, v[:, c], TN).astype(BF16)
    out[heads * HEAD :, :] = jnp.broadcast_to(last, (16, HEAD)).astype(BF16)


def forward_kernel(q, k, v, dcol, drow, table, *refs):
    arrived, (opened, low, turned, states, carry) = refs[:-5], refs[-5:]
    i = pl.program_id(0)
    heads = q.shape[1] // HEAD
    first = table[pl.ds(i, 1), :]
    following = table[pl.ds(i + 1, 1), :]

    @pl.when(i == 0)
    def _():
        carry[...] = entering_state(arrived[:3], arrived[3:], first, table[8:9, :])

    docs = dcol[...]
    joined = docs == first
    tail = docs == following
    keep = following == first
    t = lax.broadcasted_iota(jnp.int32, (CHUNK, CHUNK), 0)
    u = lax.broadcasted_iota(jnp.int32, (CHUNK, CHUNK), 1)
    mask = (t >= u) & (docs[:, :1] == drow[...])
    for h in range(heads):
        c = head_cols(h)
        qh, kh, vh = q[:, c], k[:, c], v[:, c]
        state = carry[c, :]
        state_low = state.astype(BF16)
        states[0, c, :] = state_low
        scores = jnp.where(mask, dot(qh, kh, NT), 0.0).astype(BF16)
        out = dot(scores, vh, NN) + jnp.where(joined, dot(qh, state_low, NN), 0.0)
        opened[:, c] = out
        inverse = lax.rsqrt(jnp.mean(out * out, axis=-1, keepdims=True) + EPSILON)
        normed = (out * inverse).astype(BF16)
        low[:, c] = normed
        turned[c, :] = normed.T
        kept = jnp.where(tail, kh.astype(F32), 0.0).astype(BF16)
        carry[c, :] = jnp.where(keep, state, 0.0) + dot(kept, vh, TN)


def cotangent_kernel(grad, weight, opened, q, dcol, table, grad_opened, out, carry):
    i = pl.program_id(0)
    heads = q.shape[1] // HEAD
    width = grad.shape[2]
    gn = dot(grad[0], weight[:, :width], NT)
    for j in range(1, grad.shape[0]):
        gn = gn + dot(grad[j], weight[:, j * width : (j + 1) * width], NT)

    @pl.when(i == 0)
    def _():
        carry[...] = jnp.zeros_like(carry)

    first = table[0:1, :]
    starts = dcol[...] == first
    for h in range(heads):
        c = head_cols(h)
        opened_h = opened[:, c]
        gh = gn[:, c]
        inverse = lax.rsqrt(jnp.mean(opened_h * opened_h, axis=-1, keepdims=True) + EPSILON)
        normed = opened_h * inverse
        go = inverse * (gh - normed * jnp.mean(gh * normed, axis=-1, keepdims=True))
        grad_opened[:, c] = go
        kept = jnp.where(starts, q[:, c].astype(F32), 0.0).astype(BF16)
        carry[c, :] += dot(kept, go.astype(BF16), TN)

    @pl.when(i == pl.num_programs(0) - 1)
    def _():
        size = heads * HEAD
        out[:size, :] = carry[...].astype(BF16)
        out[size:, :] = jnp.broadcast_to(first, (16, HEAD)).astype(BF16)


def split(value):
    high = value.astype(BF16)
    return high, (value - high.astype(F32)).astype(BF16)


def query_kernel(go, k, v, dcol, drow, table, states, out):
    i = pl.program_id(0)
    heads = k.shape[1] // HEAD
    first = table[pl.ds(i, 1), :]
    docs = dcol[...]
    joined = docs == first
    t = lax.broadcasted_iota(jnp.int32, (CHUNK, CHUNK), 0)
    u = lax.broadcasted_iota(jnp.int32, (CHUNK, CHUNK), 1)
    mask = (t >= u) & (docs[:, :1] == drow[...])
    for h in range(heads):
        c = head_cols(h)
        high, rest = split(go[:, c])
        vh = v[:, c]
        both = jnp.concatenate([high, rest], axis=1)
        twice = jnp.concatenate([vh, vh], axis=1)
        scores = jnp.where(mask, dot(both, twice, NT), 0.0).astype(BF16)
        carried = jnp.where(joined, dot(high, states[0, c, :], NT), 0.0)
        out[:, c] = (dot(scores, k[:, c], NN) + carried).astype(BF16)


def key_value_kernel(go, q, k, v, dcol, drow, table, *refs):
    arrived, (grad_k, grad_v, carry) = refs[:-3], refs[-3:]
    step = pl.program_id(0)
    i = pl.num_programs(0) - 1 - step
    heads = k.shape[1] // HEAD
    last = table[pl.ds(4 + i, 1), :]
    previous = table[pl.ds(3 + i, 1), :]

    @pl.when(step == 0)
    def _():
        carry[...] = entering_state(arrived[:3], arrived[3:], last, table[9:10, :])

    docs = dcol[...]
    joined = docs == last
    ahead = docs == previous
    keep = previous == last
    u = lax.broadcasted_iota(jnp.int32, (CHUNK, CHUNK), 0)
    t = lax.broadcasted_iota(jnp.int32, (CHUNK, CHUNK), 1)
    mask = (t >= u) & (docs[:, :1] == drow[...])
    for h in range(heads):
        c = head_cols(h)
        high, rest = split(go[:, c])
        qh, kh, vh = q[:, c], k[:, c], v[:, c]
        state = carry[c, :]
        state_low = state.astype(BF16)
        both = jnp.concatenate([high, rest], axis=1)
        twice = jnp.concatenate([vh, vh], axis=1)
        scores = jnp.where(mask, dot(kh, qh, NT), 0.0).astype(BF16)
        grad_scores = jnp.where(mask, dot(twice, both, NT), 0.0).astype(BF16)
        grad_v[:, c] = (
            dot(scores, high, NN) + jnp.where(joined, dot(kh, state_low, NN), 0.0)
        ).astype(BF16)
        grad_k[:, c] = (
            dot(grad_scores, qh, NN) + jnp.where(joined, dot(vh, state_low, NT), 0.0)
        ).astype(BF16)
        kept = jnp.where(ahead, qh.astype(F32), 0.0).astype(BF16)
        carry[c, :] = jnp.where(keep, state, 0.0) + dot(kept, high, TN)


def put_columns(part, out):
    low = part.astype(BF16)
    half = low.shape[1] // 2
    out[0, 0] = low[:, :half]
    out[0, 1] = low[:, half:]


def weight_kernel(turned, grad, out):
    put_columns(dot(turned[...], grad[0], NN), out)


def sum_kernel(place, own, *refs):
    total = own[0].astype(F32)
    for ref in refs[:-1]:
        total = total + ref[...].astype(F32)
    refs[-1][...] = total


def attended_kernel(places, *refs):
    near, far, columns_of = refs[:6], refs[6:10], refs[10:18]
    out, columns, sems = refs[18:]
    i = pl.program_id(0)

    def copies():
        for y in range(4):
            for x in range(4):
                for o in range(2):
                    group = places[2 * y + o]
                    row = pl.multiple_of(places[8 + x] * HEAD, HEAD)
                    to = columns.at[group, pl.ds(row, HEAD)]
                    piece = columns_of[2 * y + x // 2].at[x % 2, o]
                    yield pltpu.make_async_copy(piece, to, sems.at[8 * y + 2 * x + o])

    @pl.when(i == 0)
    def _():
        for copy in copies():
            copy.start()
        for copy in copies():
            copy.wait()

    early = i < pl.num_programs(0) // 2
    pieces = [ref[...] for ref in near]
    pieces += [jnp.where(early, far[p][...], far[p + 1][...]) for p in (0, 2)]
    total = None
    for p, piece in enumerate(pieces):
        part = dot(piece, columns[places[12 + p]], NN)
        total = part if total is None else total + part
    out[...] = total.astype(BF16)


def turned_by(value, axis, step):
    size = lax.axis_size(axis)
    return lax.ppermute(value, axis, [(i, (i + step) % size) for i in range(size)])


def moved_by(value, axis, step):
    size = lax.axis_size(axis)
    pairs = [(i, i + step) for i in range(size) if 0 <= i + step < size]
    return lax.ppermute(value, axis, pairs)


def swapped(value):
    return lax.ppermute(value, "core", [(0, 1), (1, 0)])


def pick(value, index, axis=0):
    return lax.dynamic_index_in_dim(value, index, axis, keepdims=False)


def exchanged(state, step, extra=()):
    beside = [turned_by(state, "cy", step * s) for s in range(1, 4)]
    beside, extra = lax.optimization_barrier((beside, extra))
    row = pl.pallas_call(
        lambda *refs: row_kernel(step > 0, *refs),
        out_shape=jax.ShapeDtypeStruct(state.shape, state.dtype),
        name="row_state",
    )(state, *beside)
    return beside + [moved_by(row, "cx", step * s) for s in range(1, 3)], extra


def column_strip(out_weight, share, cx):
    cy, z = lax.axis_index("cy"), lax.axis_index("z")
    at = (cx * HEAD, (z - cy) % 4 * 2 * share)
    sent = lax.dynamic_slice(out_weight, at, (HEAD, 2 * share))
    pairs = [(4 * y + (i + y) % 4, 4 * y + i) for y in range(4) for i in range(4)]
    return lax.ppermute(sent, ("cy", "z"), pairs)


def column_pieces(strip, share, core):
    mine = lax.dynamic_slice(strip, (0, core * share), (HEAD, share))
    other = lax.dynamic_slice(strip, (0, (1 - core) * share), (HEAD, share))
    both = jnp.stack([mine, swapped(other)])
    lines = [both] + [turned_by(both, "cx", s) for s in range(1, 4)]
    return jnp.stack(lines[:2]), jnp.stack(lines[2:])


def row_sum(mine, cy):
    got = [turned_by(pick(mine, (cy + s) % 4), "cy", s) for s in range(1, 4)]
    height, part = mine.shape[1:]
    block = (CHUNK, part)
    return pl.pallas_call(
        sum_kernel,
        grid_spec=pltpu.PrefetchScalarGridSpec(
            num_scalar_prefetch=1,
            grid=(height // CHUNK,),
            in_specs=[pl.BlockSpec((1, *block), lambda i, p: (p[0], i, 0))]
            + [pl.BlockSpec(block, lambda i, p: (i, 0))] * 3,
            out_specs=pl.BlockSpec(block, lambda i, p: (i, 0)),
        ),
        out_shape=jax.ShapeDtypeStruct((height, part), F32),
        compiler_params=params(),
        name="last_sum",
    )(cy[None], mine, *got)


def body(queries, keys, values, doc_ids, out_weight, grad_out):
    rows, width = queries.shape
    blocks = rows // CHUNK
    groups = lax.axis_size(TENSOR)
    share = grad_out.shape[1]
    size = width
    payload = jax.ShapeDtypeStruct((size + 16, HEAD), BF16)
    cx, cy = lax.axis_index("cx"), lax.axis_index("cy")
    z, core = lax.axis_index("z"), lax.axis_index("core")

    grad_whole = lax.all_gather(grad_out, TENSOR, axis=0)

    docs = doc_ids.astype(F32)
    dcol = jnp.broadcast_to(docs[:, None], (rows, HEAD))
    drow = docs[None, :]
    chunked = docs.reshape(blocks, CHUNK)
    place = cy.astype(F32)[None]
    table = jnp.concatenate([chunked[:, 0], chunked[:, -1], place, 3 - place, jnp.zeros((6,), F32)])
    table = jnp.broadcast_to(table[:, None], (16, HEAD))

    tail = pl.pallas_call(tail_kernel, out_shape=payload, name="tail")(keys, values, dcol, table)
    arrived, strip = exchanged(tail, 1, column_strip(out_weight, share, cx))
    own = column_pieces(strip, share, core)
    arrived, own = lax.optimization_barrier((arrived, own))
    early = [turned_by(own[0], "cy", -1), turned_by(own[1], "cy", 1)]

    row_block = pl.BlockSpec((1, CHUNK), lambda i: (0, i))
    state_block = pl.BlockSpec((1, size, HEAD), lambda i: (i, 0, 0))
    opened, low, turned, states = pl.pallas_call(
        forward_kernel,
        grid=(blocks,),
        in_specs=[rows_of(width)] * 3
        + [rows_of(HEAD), row_block, whole(table.shape)]
        + [whole(payload.shape)] * len(arrived),
        out_specs=[
            rows_of(width),
            rows_of(width),
            pl.BlockSpec((width, CHUNK), lambda i: (0, i)),
            state_block,
        ],
        out_shape=[
            jax.ShapeDtypeStruct((rows, width), F32),
            jax.ShapeDtypeStruct((rows, width), BF16),
            jax.ShapeDtypeStruct((width, rows), BF16),
            jax.ShapeDtypeStruct((blocks, size, HEAD), BF16),
        ],
        scratch_shapes=[pltpu.VMEM((size, HEAD), F32)],
        compiler_params=params(),
        name="forward",
    )(queries, keys, values, dcol, drow, table, *arrived)

    turned, early = lax.optimization_barrier((turned, early))
    term = pl.pallas_call(
        weight_kernel,
        grid=(groups,),
        in_specs=[whole((width, rows)), pl.BlockSpec((1, rows, share), lambda j: (j, 0, 0))],
        out_specs=pl.BlockSpec((1, 2, width, share // 2), lambda j: (j // 2, j % 2, 0, 0)),
        out_shape=jax.ShapeDtypeStruct((4, 4, width, share // 2), BF16),
        compiler_params=params(),
        name="weight_grad",
    )(turned, grad_whole)
    term, low, own = lax.optimization_barrier((term, low, own))
    later = [turned_by(own[1], "cy", -1), turned_by(own[0], "cy", 1)]
    grad_part = lax.psum_scatter(term, "cx", scatter_dimension=0, tiled=True)[0]

    half_rows = rows // 2
    above = turned_by(low, "z", -1)
    below = turned_by(low, "z", 1)

    grad_opened, head = pl.pallas_call(
        cotangent_kernel,
        grid=(blocks,),
        in_specs=[
            pl.BlockSpec((groups, CHUNK, share), lambda i: (0, i, 0)),
            whole(out_weight.shape),
            rows_of(width),
            rows_of(width),
            rows_of(HEAD),
            whole(table.shape),
        ],
        out_specs=[rows_of(width), whole(payload.shape)],
        out_shape=[jax.ShapeDtypeStruct((rows, width), F32), payload],
        scratch_shapes=[pltpu.VMEM((size, HEAD), F32)],
        compiler_params=params(),
        name="cotangent",
    )(grad_whole, out_weight, opened, queries, dcol, table)
    head, later, above, below = lax.optimization_barrier((head, later, above, below))
    far_a = turned_by(above[:half_rows], "z", -1)
    far_b = turned_by(below[half_rows:], "z", 1)
    moved = (far_a, far_b, low, above, below, early)
    returned, (far_a, far_b, low, above, below, early) = exchanged(head, -1, moved)
    across = [turned_by(early[0], "cy", -1), turned_by(early[1], "cy", 1)]
    near = [low, swapped(low), above, swapped(above), below, swapped(below)]
    far = [far_a, far_b, swapped(far_a), swapped(far_b)]
    columns = [*own, early[0], later[0], *across, later[1], early[1]]

    grad_query = pl.pallas_call(
        query_kernel,
        grid=(blocks,),
        in_specs=[rows_of(width)] * 3
        + [rows_of(HEAD), row_block, whole(table.shape), state_block],
        out_specs=rows_of(width),
        out_shape=jax.ShapeDtypeStruct((rows, width), BF16),
        compiler_params=params(),
        name="grad_query",
    )(grad_opened, keys, values, dcol, drow, table, states)

    ready = (returned, grad_query, near, far)
    returned, grad_query, near, far = lax.optimization_barrier(ready)

    back_row = pl.BlockSpec((1, CHUNK), lambda i: (0, blocks - 1 - i))
    grad_key, grad_value = pl.pallas_call(
        key_value_kernel,
        grid=(blocks,),
        in_specs=[rows_of(width, blocks)] * 4
        + [rows_of(HEAD, blocks), back_row, whole(table.shape)]
        + [whole(payload.shape)] * len(returned),
        out_specs=[rows_of(width, blocks)] * 2,
        out_shape=[jax.ShapeDtypeStruct((rows, width), BF16)] * 2,
        scratch_shapes=[pltpu.VMEM((size, HEAD), F32)],
        compiler_params=params(),
        name="grad_key_value",
    )(grad_opened, queries, keys, values, dcol, drow, table, *returned)

    ready = (grad_part, grad_key, columns)
    grad_part, grad_key, columns = lax.optimization_barrier(ready)
    sides = (core, 1 - core)
    around = [2 * ((z + cy + s) % 4) + side for s in range(4) for side in sides]
    heads_at = [(cx - s) % 4 for s in range(4)]
    groups_at = [2 * ((z + s) % 4) + side for s in (0, 1, 3, 2) for side in sides]
    held = pl.BlockSpec(memory_space=pl.ANY)
    every = pl.BlockSpec((CHUNK, width), lambda i, at: (i, 0))
    upper = pl.BlockSpec((CHUNK, width), lambda i, at: (jnp.minimum(i, blocks // 2 - 1), 0))
    lower = pl.BlockSpec((CHUNK, width), lambda i, at: (jnp.maximum(i - blocks // 2, 0), 0))
    attended = pl.pallas_call(
        attended_kernel,
        grid_spec=pltpu.PrefetchScalarGridSpec(
            num_scalar_prefetch=1,
            grid=(blocks,),
            in_specs=[every] * 6 + [upper, lower] * 2 + [held] * 8,
            out_specs=pl.BlockSpec((CHUNK, share), lambda i, at: (i, 0)),
            scratch_shapes=[
                pltpu.VMEM((groups, width, share), BF16),
                pltpu.SemaphoreType.DMA((32,)),
            ],
        ),
        out_shape=jax.ShapeDtypeStruct((rows, share), BF16),
        compiler_params=params(),
        name="attended",
    )(jnp.stack(around + heads_at + groups_at), *near, *far, *columns)
    grad_weight = row_sum(grad_part, cy)
    return attended, grad_query, grad_key, grad_value, grad_weight


def solution(mesh):
    finer = Mesh(mesh.devices.reshape(4, 4, 4, 2), ("cx", "cy", "z", "core"))
    by_both = P(CTX, TENSOR)
    return jax.shard_map(
        body,
        mesh=finer,
        in_specs=(by_both, by_both, by_both, P(CTX), P(TENSOR, None), by_both),
        out_specs=(by_both, by_both, by_both, by_both, P(TENSOR, CTX)),
        check_vma=False,
    )
```

```python
import jax
import jax.numpy as jnp
from jax import lax
from jax.experimental import pallas as pl
from jax.experimental.pallas import tpu as pltpu
from jax.sharding import Mesh
from jax.sharding import PartitionSpec as P

HEAD = 128
CHUNK = 256
CTX = ("cx", "cy")
TENSOR = ("z", "core")
EPSILON = 1e-06
F32 = jnp.float32
BF16 = jnp.bfloat16
NT = (((1,), (1,)), ((), ()))
TN = (((0,), (0,)), ((), ()))
NN = (((1,), (0,)), ((), ()))


def dot(a, b, dims):
    return lax.dot_general(a, b, dims, preferred_element_type=F32)


def whole(shape):
    return pl.BlockSpec(shape, lambda *_: (0,) * len(shape))


def rows_of(width, count=None):
    if count is None:
        return pl.BlockSpec((CHUNK, width), lambda i: (i, 0))
    return pl.BlockSpec((CHUNK, width), lambda i: (count - 1 - i, 0))


def head_cols(h):
    return slice(h * HEAD, (h + 1) * HEAD)


def params():
    return pltpu.CompilerParams(vmem_limit_bytes=56 << 20, dimension_semantics=("arbitrary",))


def state_of(ref):
    return ref[:-16, :].astype(F32), ref[-16:-15, :].astype(F32)


def entering_state(beside, rows, doc, place):
    total = None
    for s, ref in enumerate(beside):
        state, found = state_of(ref)
        part = jnp.where((found == doc) & (place > s + 0.5), state, 0.0)
        total = part if total is None else total + part
    for ref in rows:
        state, found = state_of(ref)
        total = total + jnp.where(found == doc, state, 0.0)
    return total


def row_kernel(latest, *refs):
    states = [state_of(ref) for ref in refs[:-1]]
    out = refs[-1]
    doc = states[0][1]
    for _, found in states[1:]:
        doc = jnp.maximum(doc, found) if latest else jnp.minimum(doc, found)
    total = None
    for state, found in states:
        part = jnp.where(found == doc, state, 0.0)
        total = part if total is None else total + part
    out[:-16, :] = total.astype(BF16)
    out[-16:, :] = jnp.broadcast_to(doc, (16, HEAD)).astype(BF16)


def tail_kernel(k, v, dcol, table, out):
    heads = k.shape[1] // HEAD
    last = table[7:8, :]
    tail = dcol[...] == last
    for h in range(heads):
        c = head_cols(h)
        kept = jnp.where(tail, k[:, c].astype(F32), 0.0).astype(BF16)
        out[c, :] = dot(kept, v[:, c], TN).astype(BF16)
    out[heads * HEAD :, :] = jnp.broadcast_to(last, (16, HEAD)).astype(BF16)


def forward_kernel(q, k, v, dcol, drow, table, *refs):
    arrived, (opened, low, turned, states, carry) = refs[:-5], refs[-5:]
    i = pl.program_id(0)
    heads = q.shape[1] // HEAD
    first = table[pl.ds(i, 1), :]
    following = table[pl.ds(i + 1, 1), :]

    @pl.when(i == 0)
    def _():
        carry[...] = entering_state(arrived[:3], arrived[3:], first, table[8:9, :])

    docs = dcol[...]
    joined = docs == first
    tail = docs == following
    keep = following == first
    t = lax.broadcasted_iota(jnp.int32, (CHUNK, CHUNK), 0)
    u = lax.broadcasted_iota(jnp.int32, (CHUNK, CHUNK), 1)
    mask = (t >= u) & (docs[:, :1] == drow[...])
    for h in range(heads):
        c = head_cols(h)
        qh, kh, vh = q[:, c], k[:, c], v[:, c]
        state = carry[c, :]
        state_low = state.astype(BF16)
        states[0, c, :] = state_low
        scores = jnp.where(mask, dot(qh, kh, NT), 0.0).astype(BF16)
        out = dot(scores, vh, NN) + jnp.where(joined, dot(qh, state_low, NN), 0.0)
        opened[:, c] = out
        inverse = lax.rsqrt(jnp.mean(out * out, axis=-1, keepdims=True) + EPSILON)
        normed = (out * inverse).astype(BF16)
        low[:, c] = normed
        turned[c, :] = normed.T
        kept = jnp.where(tail, kh.astype(F32), 0.0).astype(BF16)
        carry[c, :] = jnp.where(keep, state, 0.0) + dot(kept, vh, TN)


def cotangent_kernel(grad, weight, opened, q, dcol, table, grad_opened, out, carry):
    i = pl.program_id(0)
    heads = q.shape[1] // HEAD
    width = grad.shape[2]
    gn = dot(grad[0], weight[:, :width], NT)
    for j in range(1, grad.shape[0]):
        gn = gn + dot(grad[j], weight[:, j * width : (j + 1) * width], NT)

    @pl.when(i == 0)
    def _():
        carry[...] = jnp.zeros_like(carry)

    first = table[0:1, :]
    starts = dcol[...] == first
    for h in range(heads):
        c = head_cols(h)
        opened_h = opened[:, c]
        gh = gn[:, c]
        inverse = lax.rsqrt(jnp.mean(opened_h * opened_h, axis=-1, keepdims=True) + EPSILON)
        normed = opened_h * inverse
        go = inverse * (gh - normed * jnp.mean(gh * normed, axis=-1, keepdims=True))
        grad_opened[:, c] = go
        kept = jnp.where(starts, q[:, c].astype(F32), 0.0).astype(BF16)
        carry[c, :] += dot(kept, go.astype(BF16), TN)

    @pl.when(i == pl.num_programs(0) - 1)
    def _():
        size = heads * HEAD
        out[:size, :] = carry[...].astype(BF16)
        out[size:, :] = jnp.broadcast_to(first, (16, HEAD)).astype(BF16)


def split(value):
    high = value.astype(BF16)
    return high, (value - high.astype(F32)).astype(BF16)


def query_kernel(go, k, v, dcol, drow, table, states, out):
    i = pl.program_id(0)
    heads = k.shape[1] // HEAD
    first = table[pl.ds(i, 1), :]
    docs = dcol[...]
    joined = docs == first
    t = lax.broadcasted_iota(jnp.int32, (CHUNK, CHUNK), 0)
    u = lax.broadcasted_iota(jnp.int32, (CHUNK, CHUNK), 1)
    mask = (t >= u) & (docs[:, :1] == drow[...])
    for h in range(heads):
        c = head_cols(h)
        high, rest = split(go[:, c])
        vh = v[:, c]
        both = jnp.concatenate([high, rest], axis=1)
        twice = jnp.concatenate([vh, vh], axis=1)
        scores = jnp.where(mask, dot(both, twice, NT), 0.0).astype(BF16)
        carried = jnp.where(joined, dot(high, states[0, c, :], NT), 0.0)
        out[:, c] = (dot(scores, k[:, c], NN) + carried).astype(BF16)


def key_value_kernel(go, q, k, v, dcol, drow, table, *refs):
    arrived, (grad_k, grad_v, carry) = refs[:-3], refs[-3:]
    step = pl.program_id(0)
    i = pl.num_programs(0) - 1 - step
    heads = k.shape[1] // HEAD
    last = table[pl.ds(4 + i, 1), :]
    previous = table[pl.ds(3 + i, 1), :]

    @pl.when(step == 0)
    def _():
        carry[...] = entering_state(arrived[:3], arrived[3:], last, table[9:10, :])

    docs = dcol[...]
    joined = docs == last
    ahead = docs == previous
    keep = previous == last
    u = lax.broadcasted_iota(jnp.int32, (CHUNK, CHUNK), 0)
    t = lax.broadcasted_iota(jnp.int32, (CHUNK, CHUNK), 1)
    mask = (t >= u) & (docs[:, :1] == drow[...])
    for h in range(heads):
        c = head_cols(h)
        high, rest = split(go[:, c])
        qh, kh, vh = q[:, c], k[:, c], v[:, c]
        state = carry[c, :]
        state_low = state.astype(BF16)
        both = jnp.concatenate([high, rest], axis=1)
        twice = jnp.concatenate([vh, vh], axis=1)
        scores = jnp.where(mask, dot(kh, qh, NT), 0.0).astype(BF16)
        grad_scores = jnp.where(mask, dot(twice, both, NT), 0.0).astype(BF16)
        grad_v[:, c] = (
            dot(scores, high, NN) + jnp.where(joined, dot(kh, state_low, NN), 0.0)
        ).astype(BF16)
        grad_k[:, c] = (
            dot(grad_scores, qh, NN) + jnp.where(joined, dot(vh, state_low, NT), 0.0)
        ).astype(BF16)
        kept = jnp.where(ahead, qh.astype(F32), 0.0).astype(BF16)
        carry[c, :] = jnp.where(keep, state, 0.0) + dot(kept, high, TN)


def put_columns(part, out):
    low = part.astype(BF16)
    half = low.shape[1] // 2
    out[0, 0] = low[:, :half]
    out[0, 1] = low[:, half:]


def weight_kernel(turned, grad, out):
    put_columns(dot(turned[...], grad[0], NN), out)


def sum_kernel(place, own, *refs):
    total = own[0].astype(F32)
    for ref in refs[:-1]:
        total = total + ref[...].astype(F32)
    refs[-1][...] = total


def attended_kernel(places, *refs):
    near, far, columns_of = refs[:6], refs[6:10], refs[10:18]
    out, columns, sems = refs[18:]
    i = pl.program_id(0)

    def copies():
        for y in range(4):
            for x in range(4):
                for o in range(2):
                    group = places[2 * y + o]
                    row = pl.multiple_of(places[8 + x] * HEAD, HEAD)
                    to = columns.at[group, pl.ds(row, HEAD)]
                    piece = columns_of[2 * y + x // 2].at[x % 2, o]
                    yield pltpu.make_async_copy(piece, to, sems.at[8 * y + 2 * x + o])

    @pl.when(i == 0)
    def _():
        for copy in copies():
            copy.start()
        for copy in copies():
            copy.wait()

    early = i < pl.num_programs(0) // 2
    pieces = [ref[...] for ref in near]
    pieces += [jnp.where(early, far[p][...], far[p + 1][...]) for p in (0, 2)]
    total = None
    for p, piece in enumerate(pieces):
        part = dot(piece, columns[places[12 + p]], NN)
        total = part if total is None else total + part
    out[...] = total.astype(BF16)


def turned_by(value, axis, step):
    size = lax.axis_size(axis)
    return lax.ppermute(value, axis, [(i, (i + step) % size) for i in range(size)])


def moved_by(value, axis, step):
    size = lax.axis_size(axis)
    pairs = [(i, i + step) for i in range(size) if 0 <= i + step < size]
    return lax.ppermute(value, axis, pairs)


def swapped(value):
    return lax.ppermute(value, "core", [(0, 1), (1, 0)])


def pick(value, index, axis=0):
    return lax.dynamic_index_in_dim(value, index, axis, keepdims=False)


def exchanged(state, step, extra=()):
    beside = [turned_by(state, "cy", step * s) for s in range(1, 4)]
    beside, extra = lax.optimization_barrier((beside, extra))
    row = pl.pallas_call(
        lambda *refs: row_kernel(step > 0, *refs),
        out_shape=jax.ShapeDtypeStruct(state.shape, state.dtype),
        name="row_state",
    )(state, *beside)
    return beside + [moved_by(row, "cx", step * s) for s in range(1, 3)], extra


def column_strip(out_weight, share, cx):
    cy, z = lax.axis_index("cy"), lax.axis_index("z")
    at = (cx * HEAD, (z - cy) % 4 * 2 * share)
    sent = lax.dynamic_slice(out_weight, at, (HEAD, 2 * share))
    pairs = [(4 * y + (i + y) % 4, 4 * y + i) for y in range(4) for i in range(4)]
    return lax.ppermute(sent, ("cy", "z"), pairs)


def column_pieces(strip, share, core):
    mine = lax.dynamic_slice(strip, (0, core * share), (HEAD, share))
    other = lax.dynamic_slice(strip, (0, (1 - core) * share), (HEAD, share))
    both = jnp.stack([mine, swapped(other)])
    lines = [both] + [turned_by(both, "cx", s) for s in range(1, 4)]
    return jnp.stack(lines[:2]), jnp.stack(lines[2:])


def row_sum(mine, cy):
    got = [turned_by(pick(mine, (cy + s) % 4), "cy", s) for s in range(1, 4)]
    height, part = mine.shape[1:]
    block = (CHUNK, part)
    return pl.pallas_call(
        sum_kernel,
        grid_spec=pltpu.PrefetchScalarGridSpec(
            num_scalar_prefetch=1,
            grid=(height // CHUNK,),
            in_specs=[pl.BlockSpec((1, *block), lambda i, p: (p[0], i, 0))]
            + [pl.BlockSpec(block, lambda i, p: (i, 0))] * 3,
            out_specs=pl.BlockSpec(block, lambda i, p: (i, 0)),
        ),
        out_shape=jax.ShapeDtypeStruct((height, part), F32),
        compiler_params=params(),
        name="last_sum",
    )(cy[None], mine, *got)


def body(queries, keys, values, doc_ids, out_weight, grad_out):
    rows, width = queries.shape
    blocks = rows // CHUNK
    groups = lax.axis_size(TENSOR)
    share = grad_out.shape[1]
    size = width
    payload = jax.ShapeDtypeStruct((size + 16, HEAD), BF16)
    cx, cy = lax.axis_index("cx"), lax.axis_index("cy")
    z, core = lax.axis_index("z"), lax.axis_index("core")

    grad_whole = lax.all_gather(grad_out, TENSOR, axis=0)

    docs = doc_ids.astype(F32)
    dcol = jnp.broadcast_to(docs[:, None], (rows, HEAD))
    drow = docs[None, :]
    chunked = docs.reshape(blocks, CHUNK)
    place = cy.astype(F32)[None]
    table = jnp.concatenate([chunked[:, 0], chunked[:, -1], place, 3 - place, jnp.zeros((6,), F32)])
    table = jnp.broadcast_to(table[:, None], (16, HEAD))

    tail = pl.pallas_call(tail_kernel, out_shape=payload, name="tail")(keys, values, dcol, table)
    arrived, strip = exchanged(tail, 1, column_strip(out_weight, share, cx))
    own = column_pieces(strip, share, core)
    arrived, own = lax.optimization_barrier((arrived, own))
    early = [turned_by(own[0], "cy", -1), turned_by(own[1], "cy", 1)]
    later = [turned_by(own[1], "cy", -1), turned_by(own[0], "cy", 1)]

    row_block = pl.BlockSpec((1, CHUNK), lambda i: (0, i))
    state_block = pl.BlockSpec((1, size, HEAD), lambda i: (i, 0, 0))
    opened, low, turned, states = pl.pallas_call(
        forward_kernel,
        grid=(blocks,),
        in_specs=[rows_of(width)] * 3
        + [rows_of(HEAD), row_block, whole(table.shape)]
        + [whole(payload.shape)] * len(arrived),
        out_specs=[
            rows_of(width),
            rows_of(width),
            pl.BlockSpec((width, CHUNK), lambda i: (0, i)),
            state_block,
        ],
        out_shape=[
            jax.ShapeDtypeStruct((rows, width), F32),
            jax.ShapeDtypeStruct((rows, width), BF16),
            jax.ShapeDtypeStruct((width, rows), BF16),
            jax.ShapeDtypeStruct((blocks, size, HEAD), BF16),
        ],
        scratch_shapes=[pltpu.VMEM((size, HEAD), F32)],
        compiler_params=params(),
        name="forward",
    )(queries, keys, values, dcol, drow, table, *arrived)

    term = pl.pallas_call(
        weight_kernel,
        grid=(groups,),
        in_specs=[whole((width, rows)), pl.BlockSpec((1, rows, share), lambda j: (j, 0, 0))],
        out_specs=pl.BlockSpec((1, 2, width, share // 2), lambda j: (j // 2, j % 2, 0, 0)),
        out_shape=jax.ShapeDtypeStruct((4, 4, width, share // 2), BF16),
        compiler_params=params(),
        name="weight_grad",
    )(turned, grad_whole)
    term, low, early, later = lax.optimization_barrier((term, low, early, later))
    across = [turned_by(early[0], "cy", -1), turned_by(early[1], "cy", 1)]
    grad_part = lax.psum_scatter(term, "cx", scatter_dimension=0, tiled=True)[0]

    half_rows = rows // 2
    above = turned_by(low, "z", -1)
    below = turned_by(low, "z", 1)

    grad_opened, head = pl.pallas_call(
        cotangent_kernel,
        grid=(blocks,),
        in_specs=[
            pl.BlockSpec((groups, CHUNK, share), lambda i: (0, i, 0)),
            whole(out_weight.shape),
            rows_of(width),
            rows_of(width),
            rows_of(HEAD),
            whole(table.shape),
        ],
        out_specs=[rows_of(width), whole(payload.shape)],
        out_shape=[jax.ShapeDtypeStruct((rows, width), F32), payload],
        scratch_shapes=[pltpu.VMEM((size, HEAD), F32)],
        compiler_params=params(),
        name="cotangent",
    )(grad_whole, out_weight, opened, queries, dcol, table)
    head, across, above, below = lax.optimization_barrier((head, across, above, below))
    far_a = turned_by(above[:half_rows], "z", -1)
    far_b = turned_by(below[half_rows:], "z", 1)
    moved = (far_a, far_b, low, above, below)
    returned, (far_a, far_b, low, above, below) = exchanged(head, -1, moved)
    near = [low, swapped(low), above, swapped(above), below, swapped(below)]
    far = [far_a, far_b, swapped(far_a), swapped(far_b)]
    columns = [*own, early[0], later[0], *across, later[1], early[1]]

    sides = (core, 1 - core)
    around = [2 * ((z + cy + s) % 4) + side for s in range(4) for side in sides]
    heads_at = [(cx - s) % 4 for s in range(4)]
    groups_at = [2 * ((z + s) % 4) + side for s in (0, 1, 3, 2) for side in sides]
    held = pl.BlockSpec(memory_space=pl.ANY)
    every = pl.BlockSpec((CHUNK, width), lambda i, at: (i, 0))
    upper = pl.BlockSpec((CHUNK, width), lambda i, at: (jnp.minimum(i, blocks // 2 - 1), 0))
    lower = pl.BlockSpec((CHUNK, width), lambda i, at: (jnp.maximum(i - blocks // 2, 0), 0))
    attended = pl.pallas_call(
        attended_kernel,
        grid_spec=pltpu.PrefetchScalarGridSpec(
            num_scalar_prefetch=1,
            grid=(blocks,),
            in_specs=[every] * 6 + [upper, lower] * 2 + [held] * 8,
            out_specs=pl.BlockSpec((CHUNK, share), lambda i, at: (i, 0)),
            scratch_shapes=[
                pltpu.VMEM((groups, width, share), BF16),
                pltpu.SemaphoreType.DMA((32,)),
            ],
        ),
        out_shape=jax.ShapeDtypeStruct((rows, share), BF16),
        compiler_params=params(),
        name="attended",
    )(jnp.stack(around + heads_at + groups_at), *near, *far, *columns)
    ready = (returned, grad_opened, grad_part, attended)
    returned, grad_opened, grad_part, attended = lax.optimization_barrier(ready)

    grad_query = pl.pallas_call(
        query_kernel,
        grid=(blocks,),
        in_specs=[rows_of(width)] * 3
        + [rows_of(HEAD), row_block, whole(table.shape), state_block],
        out_specs=rows_of(width),
        out_shape=jax.ShapeDtypeStruct((rows, width), BF16),
        compiler_params=params(),
        name="grad_query",
    )(grad_opened, keys, values, dcol, drow, table, states)


    back_row = pl.BlockSpec((1, CHUNK), lambda i: (0, blocks - 1 - i))
    grad_key, grad_value = pl.pallas_call(
        key_value_kernel,
        grid=(blocks,),
        in_specs=[rows_of(width, blocks)] * 4
        + [rows_of(HEAD, blocks), back_row, whole(table.shape)]
        + [whole(payload.shape)] * len(returned),
        out_specs=[rows_of(width, blocks)] * 2,
        out_shape=[jax.ShapeDtypeStruct((rows, width), BF16)] * 2,
        scratch_shapes=[pltpu.VMEM((size, HEAD), F32)],
        compiler_params=params(),
        name="grad_key_value",
    )(grad_opened, queries, keys, values, dcol, drow, table, *returned)

    grad_weight = row_sum(grad_part, cy)
    return attended, grad_query, grad_key, grad_value, grad_weight


def solution(mesh):
    finer = Mesh(mesh.devices.reshape(4, 4, 4, 2), ("cx", "cy", "z", "core"))
    by_both = P(CTX, TENSOR)
    return jax.shard_map(
        body,
        mesh=finer,
        in_specs=(by_both, by_both, by_both, P(CTX), P(TENSOR, None), by_both),
        out_specs=(by_both, by_both, by_both, by_both, P(TENSOR, CTX)),
        check_vma=False,
    )
```

```python
import jax
import jax.numpy as jnp
from jax import lax
from jax.experimental import pallas as pl
from jax.experimental.pallas import tpu as pltpu
from jax.sharding import Mesh
from jax.sharding import PartitionSpec as P

HEAD = 128
CHUNK = 256
CTX = ("cx", "cy")
TENSOR = ("z", "core")
EPSILON = 1e-06
F32 = jnp.float32
BF16 = jnp.bfloat16
NT = (((1,), (1,)), ((), ()))
TN = (((0,), (0,)), ((), ()))
NN = (((1,), (0,)), ((), ()))


def dot(a, b, dims):
    return lax.dot_general(a, b, dims, preferred_element_type=F32)


def whole(shape):
    return pl.BlockSpec(shape, lambda *_: (0,) * len(shape))


def rows_of(width, count=None):
    if count is None:
        return pl.BlockSpec((CHUNK, width), lambda i: (i, 0))
    return pl.BlockSpec((CHUNK, width), lambda i: (count - 1 - i, 0))


def head_cols(h):
    return slice(h * HEAD, (h + 1) * HEAD)


def params():
    return pltpu.CompilerParams(vmem_limit_bytes=56 << 20, dimension_semantics=("arbitrary",))


def state_of(ref):
    return ref[:-16, :].astype(F32), ref[-16:-15, :].astype(F32)


def entering_state(beside, rows, doc, place):
    total = None
    for s, ref in enumerate(beside):
        state, found = state_of(ref)
        part = jnp.where((found == doc) & (place > s + 0.5), state, 0.0)
        total = part if total is None else total + part
    for ref in rows:
        state, found = state_of(ref)
        total = total + jnp.where(found == doc, state, 0.0)
    return total


def row_kernel(latest, *refs):
    states = [state_of(ref) for ref in refs[:-1]]
    out = refs[-1]
    doc = states[0][1]
    for _, found in states[1:]:
        doc = jnp.maximum(doc, found) if latest else jnp.minimum(doc, found)
    total = None
    for state, found in states:
        part = jnp.where(found == doc, state, 0.0)
        total = part if total is None else total + part
    out[:-16, :] = total.astype(BF16)
    out[-16:, :] = jnp.broadcast_to(doc, (16, HEAD)).astype(BF16)


def tail_kernel(k, v, dcol, table, out):
    heads = k.shape[1] // HEAD
    last = table[7:8, :]
    tail = dcol[...] == last
    for h in range(heads):
        c = head_cols(h)
        kept = jnp.where(tail, k[:, c].astype(F32), 0.0).astype(BF16)
        out[c, :] = dot(kept, v[:, c], TN).astype(BF16)
    out[heads * HEAD :, :] = jnp.broadcast_to(last, (16, HEAD)).astype(BF16)


def forward_kernel(q, k, v, dcol, drow, table, *refs):
    arrived, (opened, low, turned, states, carry) = refs[:-5], refs[-5:]
    i = pl.program_id(0)
    heads = q.shape[1] // HEAD
    first = table[pl.ds(i, 1), :]
    following = table[pl.ds(i + 1, 1), :]

    @pl.when(i == 0)
    def _():
        carry[...] = entering_state(arrived[:3], arrived[3:], first, table[8:9, :])

    docs = dcol[...]
    joined = docs == first
    tail = docs == following
    keep = following == first
    t = lax.broadcasted_iota(jnp.int32, (CHUNK, CHUNK), 0)
    u = lax.broadcasted_iota(jnp.int32, (CHUNK, CHUNK), 1)
    mask = (t >= u) & (docs[:, :1] == drow[...])
    for h in range(heads):
        c = head_cols(h)
        qh, kh, vh = q[:, c], k[:, c], v[:, c]
        state = carry[c, :]
        state_low = state.astype(BF16)
        states[0, c, :] = state_low
        scores = jnp.where(mask, dot(qh, kh, NT), 0.0).astype(BF16)
        out = dot(scores, vh, NN) + jnp.where(joined, dot(qh, state_low, NN), 0.0)
        opened[:, c] = out
        inverse = lax.rsqrt(jnp.mean(out * out, axis=-1, keepdims=True) + EPSILON)
        normed = (out * inverse).astype(BF16)
        low[:, c] = normed
        turned[c, :] = normed.T
        kept = jnp.where(tail, kh.astype(F32), 0.0).astype(BF16)
        carry[c, :] = jnp.where(keep, state, 0.0) + dot(kept, vh, TN)


def near_cotangent_kernel(places, own, beside, first, second, out):
    out[...] = dot(own[...], first[...], NT) + dot(beside[...], second[...], NT)


def cotangent_kernel(places, near, *refs):
    grads, weights = refs[:6], refs[6:12]
    opened, q, dcol, table, grad_opened, out, carry = refs[12:]
    i = pl.program_id(0)
    heads = q.shape[1] // HEAD
    gn = near[...]
    for grad, weight in zip(grads, weights):
        gn = gn + dot(grad[0], weight[...], NT)

    @pl.when(i == 0)
    def _():
        carry[...] = jnp.zeros_like(carry)

    first = table[0:1, :]
    starts = dcol[...] == first
    for h in range(heads):
        c = head_cols(h)
        opened_h = opened[:, c]
        gh = gn[:, c]
        inverse = lax.rsqrt(jnp.mean(opened_h * opened_h, axis=-1, keepdims=True) + EPSILON)
        normed = opened_h * inverse
        go = inverse * (gh - normed * jnp.mean(gh * normed, axis=-1, keepdims=True))
        grad_opened[:, c] = go
        kept = jnp.where(starts, q[:, c].astype(F32), 0.0).astype(BF16)
        carry[c, :] += dot(kept, go.astype(BF16), TN)

    @pl.when(i == pl.num_programs(0) - 1)
    def _():
        size = heads * HEAD
        out[:size, :] = carry[...].astype(BF16)
        out[size:, :] = jnp.broadcast_to(first, (16, HEAD)).astype(BF16)


def split(value):
    high = value.astype(BF16)
    return high, (value - high.astype(F32)).astype(BF16)


def query_kernel(go, k, v, dcol, drow, table, states, out):
    i = pl.program_id(0)
    heads = k.shape[1] // HEAD
    first = table[pl.ds(i, 1), :]
    docs = dcol[...]
    joined = docs == first
    t = lax.broadcasted_iota(jnp.int32, (CHUNK, CHUNK), 0)
    u = lax.broadcasted_iota(jnp.int32, (CHUNK, CHUNK), 1)
    mask = (t >= u) & (docs[:, :1] == drow[...])
    for h in range(heads):
        c = head_cols(h)
        high, rest = split(go[:, c])
        vh = v[:, c]
        both = jnp.concatenate([high, rest], axis=1)
        twice = jnp.concatenate([vh, vh], axis=1)
        scores = jnp.where(mask, dot(both, twice, NT), 0.0).astype(BF16)
        carried = jnp.where(joined, dot(high, states[0, c, :], NT), 0.0)
        out[:, c] = (dot(scores, k[:, c], NN) + carried).astype(BF16)


def key_value_kernel(go, q, k, v, dcol, drow, table, *refs):
    arrived, (grad_k, grad_v, carry) = refs[:-3], refs[-3:]
    step = pl.program_id(0)
    i = pl.num_programs(0) - 1 - step
    heads = k.shape[1] // HEAD
    last = table[pl.ds(4 + i, 1), :]
    previous = table[pl.ds(3 + i, 1), :]

    @pl.when(step == 0)
    def _():
        carry[...] = entering_state(arrived[:3], arrived[3:], last, table[9:10, :])

    docs = dcol[...]
    joined = docs == last
    ahead = docs == previous
    keep = previous == last
    u = lax.broadcasted_iota(jnp.int32, (CHUNK, CHUNK), 0)
    t = lax.broadcasted_iota(jnp.int32, (CHUNK, CHUNK), 1)
    mask = (t >= u) & (docs[:, :1] == drow[...])
    for h in range(heads):
        c = head_cols(h)
        high, rest = split(go[:, c])
        qh, kh, vh = q[:, c], k[:, c], v[:, c]
        state = carry[c, :]
        state_low = state.astype(BF16)
        both = jnp.concatenate([high, rest], axis=1)
        twice = jnp.concatenate([vh, vh], axis=1)
        scores = jnp.where(mask, dot(kh, qh, NT), 0.0).astype(BF16)
        grad_scores = jnp.where(mask, dot(twice, both, NT), 0.0).astype(BF16)
        grad_v[:, c] = (
            dot(scores, high, NN) + jnp.where(joined, dot(kh, state_low, NN), 0.0)
        ).astype(BF16)
        grad_k[:, c] = (
            dot(grad_scores, qh, NN) + jnp.where(joined, dot(vh, state_low, NT), 0.0)
        ).astype(BF16)
        kept = jnp.where(ahead, qh.astype(F32), 0.0).astype(BF16)
        carry[c, :] = jnp.where(keep, state, 0.0) + dot(kept, high, TN)


def put_columns(part, out):
    low = part.astype(BF16)
    half = low.shape[1] // 2
    out[0] = low[:, :half]
    out[1] = low[:, half:]


def near_weight_kernel(places, turned, own, beside, out):
    for p, piece in enumerate((own, beside)):

        @pl.when(pl.program_id(0) == p)
        def _():
            put_columns(dot(turned[...], piece[...], NN), out)


def weight_kernel(places, turned, grad, started, out):
    put_columns(dot(turned[...], grad[0], NN), out)


def attended_kernel(places, *refs):
    near, far, columns_of = refs[:6], refs[6:10], refs[10:18]
    out, columns, sems = refs[18:]
    i = pl.program_id(0)

    def copies():
        for y in range(4):
            for x in range(4):
                for o in range(2):
                    group = places[2 * y + o]
                    row = pl.multiple_of(places[8 + x] * HEAD, HEAD)
                    to = columns.at[group, pl.ds(row, HEAD)]
                    piece = columns_of[2 * y + x // 2].at[x % 2, o]
                    yield pltpu.make_async_copy(piece, to, sems.at[8 * y + 2 * x + o])

    @pl.when(i == 0)
    def _():
        for copy in copies():
            copy.start()
        for copy in copies():
            copy.wait()

    early = i < pl.num_programs(0) // 2
    pieces = [ref[...] for ref in near]
    pieces += [jnp.where(early, far[p][...], far[p + 1][...]) for p in (0, 2)]
    total = None
    for p, piece in enumerate(pieces):
        part = dot(piece, columns[places[12 + p]], NN)
        total = part if total is None else total + part
    out[...] = total.astype(BF16)


def turned_by(value, axis, step):
    size = lax.axis_size(axis)
    return lax.ppermute(value, axis, [(i, (i + step) % size) for i in range(size)])


def moved_by(value, axis, step):
    size = lax.axis_size(axis)
    pairs = [(i, i + step) for i in range(size) if 0 <= i + step < size]
    return lax.ppermute(value, axis, pairs)


def swapped(value):
    return lax.ppermute(value, "core", [(0, 1), (1, 0)])


def pick(value, index, axis=0):
    return lax.dynamic_index_in_dim(value, index, axis, keepdims=False)


def exchanged(state, step, extra=()):
    beside = [turned_by(state, "cy", step * s) for s in range(1, 4)]
    beside, extra = lax.optimization_barrier((beside, extra))
    row = pl.pallas_call(
        lambda *refs: row_kernel(step > 0, *refs),
        out_shape=jax.ShapeDtypeStruct(state.shape, state.dtype),
        name="row_state",
    )(state, *beside)
    return beside + [moved_by(row, "cx", step * s) for s in range(1, 3)], extra


def column_strip(out_weight, share, cx):
    cy, z = lax.axis_index("cy"), lax.axis_index("z")
    at = (cx * HEAD, (z - cy) % 4 * 2 * share)
    sent = lax.dynamic_slice(out_weight, at, (HEAD, 2 * share))
    pairs = [(4 * y + (i + y) % 4, 4 * y + i) for y in range(4) for i in range(4)]
    return lax.ppermute(sent, ("cy", "z"), pairs)


def column_pieces(strip, share, core):
    mine = lax.dynamic_slice(strip, (0, core * share), (HEAD, share))
    other = lax.dynamic_slice(strip, (0, (1 - core) * share), (HEAD, share))
    both = jnp.stack([mine, swapped(other)])
    lines = [both] + [turned_by(both, "cx", s) for s in range(1, 4)]
    return jnp.stack(lines[:2]), jnp.stack(lines[2:])


def body(queries, keys, values, doc_ids, out_weight, grad_out):
    rows, width = queries.shape
    blocks = rows // CHUNK
    groups = lax.axis_size(TENSOR)
    share = grad_out.shape[1]
    size = width
    payload = jax.ShapeDtypeStruct((size + 16, HEAD), BF16)
    cx, cy = lax.axis_index("cx"), lax.axis_index("cy")
    z, core = lax.axis_index("z"), lax.axis_index("core")

    grad_whole = lax.all_gather(grad_out, TENSOR, axis=0)
    beside = swapped(grad_out)

    docs = doc_ids.astype(F32)
    dcol = jnp.broadcast_to(docs[:, None], (rows, HEAD))
    drow = docs[None, :]
    chunked = docs.reshape(blocks, CHUNK)
    place = cy.astype(F32)[None]
    table = jnp.concatenate([chunked[:, 0], chunked[:, -1], place, 3 - place, jnp.zeros((6,), F32)])
    table = jnp.broadcast_to(table[:, None], (16, HEAD))

    tail = pl.pallas_call(tail_kernel, out_shape=payload, name="tail")(keys, values, dcol, table)
    strip = column_strip(out_weight, share, cx)
    arrived, (strip, beside) = exchanged(tail, 1, (strip, beside))
    own = column_pieces(strip, share, core)
    arrived, own = lax.optimization_barrier((arrived, own))
    early = [turned_by(own[0], "cy", -1), turned_by(own[1], "cy", 1)]
    later = [turned_by(own[1], "cy", -1), turned_by(own[0], "cy", 1)]

    row_block = pl.BlockSpec((1, CHUNK), lambda i: (0, i))
    state_block = pl.BlockSpec((1, size, HEAD), lambda i: (i, 0, 0))
    opened, low, turned, states = pl.pallas_call(
        forward_kernel,
        grid=(blocks,),
        in_specs=[rows_of(width)] * 3
        + [rows_of(HEAD), row_block, whole(table.shape)]
        + [whole(payload.shape)] * len(arrived),
        out_specs=[
            rows_of(width),
            rows_of(width),
            pl.BlockSpec((width, CHUNK), lambda i: (0, i)),
            state_block,
        ],
        out_shape=[
            jax.ShapeDtypeStruct((rows, width), F32),
            jax.ShapeDtypeStruct((rows, width), BF16),
            jax.ShapeDtypeStruct((width, rows), BF16),
            jax.ShapeDtypeStruct((blocks, size, HEAD), BF16),
        ],
        scratch_shapes=[pltpu.VMEM((size, HEAD), F32)],
        compiler_params=params(),
        name="forward",
    )(queries, keys, values, dcol, drow, table, *arrived)

    sides = (core, 1 - core)
    places = jnp.stack([2 * ((z + s) % 4) + side for s in range(4) for side in sides])

    def weight_block(p):
        return pl.BlockSpec((width, share), lambda i, at: (0, at[p]))

    def some_rows(columns):
        return pl.BlockSpec((CHUNK, columns), lambda i, at: (i, 0))

    def grad_block(p):
        return pl.BlockSpec((1, CHUNK, share), lambda i, at: (at[p], i, 0))

    near_sum = pl.pallas_call(
        near_cotangent_kernel,
        grid_spec=pltpu.PrefetchScalarGridSpec(
            num_scalar_prefetch=1,
            grid=(blocks,),
            in_specs=[some_rows(share)] * 2 + [weight_block(0), weight_block(1)],
            out_specs=some_rows(width),
        ),
        out_shape=jax.ShapeDtypeStruct((rows, width), F32),
        compiler_params=params(),
        name="near_cotangent",
    )(places, grad_out, beside, out_weight, out_weight)

    def column_block(base):
        return pl.BlockSpec((2, width, share // 2), lambda j, at: (at[base + j], 0, 0))

    held = pl.BlockSpec(memory_space=pl.ANY)
    term_shape = jax.ShapeDtypeStruct((2 * groups, width, share // 2), BF16)
    started = pl.pallas_call(
        near_weight_kernel,
        grid_spec=pltpu.PrefetchScalarGridSpec(
            num_scalar_prefetch=1,
            grid=(2,),
            in_specs=[whole((width, rows))] + [whole((rows, share))] * 2,
            out_specs=column_block(0),
        ),
        out_shape=term_shape,
        compiler_params=params(),
        name="near_weight",
    )(places, turned, grad_out, beside)
    started, near_sum = lax.optimization_barrier((started, near_sum))
    term = pl.pallas_call(
        weight_kernel,
        grid_spec=pltpu.PrefetchScalarGridSpec(
            num_scalar_prefetch=1,
            grid=(groups - 2,),
            in_specs=[
                whole((width, rows)),
                pl.BlockSpec((1, rows, share), lambda j, at: (at[2 + j], 0, 0)),
                held,
            ],
            out_specs=column_block(2),
        ),
        out_shape=term_shape,
        input_output_aliases={3: 0},
        compiler_params=params(),
        name="weight_grad",
    )(places, turned, grad_whole, started)
    term, low, early, later = lax.optimization_barrier((term, low, early, later))
    across = [turned_by(early[0], "cy", -1), turned_by(early[1], "cy", 1)]
    grad_part = lax.psum_scatter(term, CTX, scatter_dimension=0, tiled=True)

    half_rows = rows // 2
    above = turned_by(low, "z", -1)
    below = turned_by(low, "z", 1)

    grad_opened, head = pl.pallas_call(
        cotangent_kernel,
        grid_spec=pltpu.PrefetchScalarGridSpec(
            num_scalar_prefetch=1,
            grid=(blocks,),
            in_specs=[some_rows(width)]
            + [grad_block(p) for p in range(2, 8)]
            + [weight_block(p) for p in range(2, 8)]
            + [some_rows(width), some_rows(width), some_rows(HEAD), whole(table.shape)],
            out_specs=[some_rows(width), whole(payload.shape)],
            scratch_shapes=[pltpu.VMEM((size, HEAD), F32)],
        ),
        out_shape=[jax.ShapeDtypeStruct((rows, width), F32), payload],
        compiler_params=params(),
        name="cotangent",
    )(places, near_sum, *[grad_whole] * 6, *[out_weight] * 6, opened, queries, dcol, table)
    head, across, above, below = lax.optimization_barrier((head, across, above, below))
    far_a = turned_by(above[:half_rows], "z", -1)
    far_b = turned_by(below[half_rows:], "z", 1)
    moved = (far_a, far_b, low, above, below)
    returned, (far_a, far_b, low, above, below) = exchanged(head, -1, moved)
    near = [low, swapped(low), above, swapped(above), below, swapped(below)]
    far = [far_a, far_b, swapped(far_a), swapped(far_b)]
    columns = [*own, early[0], later[0], *across, later[1], early[1]]

    around = [2 * ((z + cy + s) % 4) + side for s in range(4) for side in sides]
    heads_at = [(cx - s) % 4 for s in range(4)]
    groups_at = [2 * ((z + s) % 4) + side for s in (0, 1, 3, 2) for side in sides]
    held = pl.BlockSpec(memory_space=pl.ANY)
    every = pl.BlockSpec((CHUNK, width), lambda i, at: (i, 0))
    upper = pl.BlockSpec((CHUNK, width), lambda i, at: (jnp.minimum(i, blocks // 2 - 1), 0))
    lower = pl.BlockSpec((CHUNK, width), lambda i, at: (jnp.maximum(i - blocks // 2, 0), 0))
    attended = pl.pallas_call(
        attended_kernel,
        grid_spec=pltpu.PrefetchScalarGridSpec(
            num_scalar_prefetch=1,
            grid=(blocks,),
            in_specs=[every] * 6 + [upper, lower] * 2 + [held] * 8,
            out_specs=pl.BlockSpec((CHUNK, share), lambda i, at: (i, 0)),
            scratch_shapes=[
                pltpu.VMEM((groups, width, share), BF16),
                pltpu.SemaphoreType.DMA((32,)),
            ],
        ),
        out_shape=jax.ShapeDtypeStruct((rows, share), BF16),
        compiler_params=params(),
        name="attended",
    )(jnp.stack(around + heads_at + groups_at), *near, *far, *columns)
    ready = (returned, grad_opened, attended)
    returned, grad_opened, attended = lax.optimization_barrier(ready)

    grad_query = pl.pallas_call(
        query_kernel,
        grid=(blocks,),
        in_specs=[rows_of(width)] * 3
        + [rows_of(HEAD), row_block, whole(table.shape), state_block],
        out_specs=rows_of(width),
        out_shape=jax.ShapeDtypeStruct((rows, width), BF16),
        compiler_params=params(),
        name="grad_query",
    )(grad_opened, keys, values, dcol, drow, table, states)


    back_row = pl.BlockSpec((1, CHUNK), lambda i: (0, blocks - 1 - i))
    grad_key, grad_value = pl.pallas_call(
        key_value_kernel,
        grid=(blocks,),
        in_specs=[rows_of(width, blocks)] * 4
        + [rows_of(HEAD, blocks), back_row, whole(table.shape)]
        + [whole(payload.shape)] * len(returned),
        out_specs=[rows_of(width, blocks)] * 2,
        out_shape=[jax.ShapeDtypeStruct((rows, width), BF16)] * 2,
        scratch_shapes=[pltpu.VMEM((size, HEAD), F32)],
        compiler_params=params(),
        name="grad_key_value",
    )(grad_opened, queries, keys, values, dcol, drow, table, *returned)

    ready = (grad_part, grad_query, grad_key)
    grad_part, grad_query, grad_key = lax.optimization_barrier(ready)
    grad_weight = grad_part.reshape(width, share // 2).astype(F32)
    return attended, grad_query, grad_key, grad_value, grad_weight


def solution(mesh):
    finer = Mesh(mesh.devices.reshape(4, 4, 4, 2), ("cx", "cy", "z", "core"))
    by_both = P(CTX, TENSOR)
    return jax.shard_map(
        body,
        mesh=finer,
        in_specs=(by_both, by_both, by_both, P(CTX), P(TENSOR, None), by_both),
        out_specs=(by_both, by_both, by_both, by_both, P(TENSOR, CTX)),
        check_vma=False,
    )
```

```python
import jax
import jax.numpy as jnp
from jax import lax
from jax.experimental import pallas as pl
from jax.experimental.pallas import tpu as pltpu
from jax.sharding import Mesh
from jax.sharding import PartitionSpec as P

HEAD = 128
CHUNK = 256
CTX = ("cx", "cy")
TENSOR = ("z", "core")
EPSILON = 1e-06
F32 = jnp.float32
BF16 = jnp.bfloat16
NT = (((1,), (1,)), ((), ()))
TN = (((0,), (0,)), ((), ()))
NN = (((1,), (0,)), ((), ()))


def dot(a, b, dims):
    return lax.dot_general(a, b, dims, preferred_element_type=F32)


def whole(shape):
    return pl.BlockSpec(shape, lambda *_: (0,) * len(shape))


def rows_of(width, count=None):
    if count is None:
        return pl.BlockSpec((CHUNK, width), lambda i: (i, 0))
    return pl.BlockSpec((CHUNK, width), lambda i: (count - 1 - i, 0))


def head_cols(h):
    return slice(h * HEAD, (h + 1) * HEAD)


def params():
    return pltpu.CompilerParams(vmem_limit_bytes=56 << 20, dimension_semantics=("arbitrary",))


def state_of(ref):
    return ref[:-16, :].astype(F32), ref[-16:-15, :].astype(F32)


def entering_state(beside, rows, doc, place):
    total = None
    for s, ref in enumerate(beside):
        state, found = state_of(ref)
        part = jnp.where((found == doc) & (place > s + 0.5), state, 0.0)
        total = part if total is None else total + part
    for ref in rows:
        state, found = state_of(ref)
        total = total + jnp.where(found == doc, state, 0.0)
    return total


def row_kernel(latest, *refs):
    states = [state_of(ref) for ref in refs[:-1]]
    out = refs[-1]
    doc = states[0][1]
    for _, found in states[1:]:
        doc = jnp.maximum(doc, found) if latest else jnp.minimum(doc, found)
    total = None
    for state, found in states:
        part = jnp.where(found == doc, state, 0.0)
        total = part if total is None else total + part
    out[:-16, :] = total.astype(BF16)
    out[-16:, :] = jnp.broadcast_to(doc, (16, HEAD)).astype(BF16)


def tail_kernel(k, v, dcol, table, out):
    heads = k.shape[1] // HEAD
    last = table[7:8, :]
    tail = dcol[...] == last
    for h in range(heads):
        c = head_cols(h)
        kept = jnp.where(tail, k[:, c].astype(F32), 0.0).astype(BF16)
        out[c, :] = dot(kept, v[:, c], TN).astype(BF16)
    out[heads * HEAD :, :] = jnp.broadcast_to(last, (16, HEAD)).astype(BF16)


def forward_kernel(q, k, v, dcol, drow, table, *refs):
    arrived, (opened, low, turned, states, carry) = refs[:-5], refs[-5:]
    i = pl.program_id(0)
    heads = q.shape[1] // HEAD
    first = table[pl.ds(i, 1), :]
    following = table[pl.ds(i + 1, 1), :]

    @pl.when(i == 0)
    def _():
        carry[...] = entering_state(arrived[:3], arrived[3:], first, table[8:9, :])

    docs = dcol[...]
    joined = docs == first
    tail = docs == following
    keep = following == first
    t = lax.broadcasted_iota(jnp.int32, (CHUNK, CHUNK), 0)
    u = lax.broadcasted_iota(jnp.int32, (CHUNK, CHUNK), 1)
    mask = (t >= u) & (docs[:, :1] == drow[...])
    for h in range(heads):
        c = head_cols(h)
        qh, kh, vh = q[:, c], k[:, c], v[:, c]
        state = carry[c, :]
        state_low = state.astype(BF16)
        states[0, c, :] = state_low
        scores = jnp.where(mask, dot(qh, kh, NT), 0.0).astype(BF16)
        out = dot(scores, vh, NN) + jnp.where(joined, dot(qh, state_low, NN), 0.0)
        opened[:, c] = out
        inverse = lax.rsqrt(jnp.mean(out * out, axis=-1, keepdims=True) + EPSILON)
        normed = (out * inverse).astype(BF16)
        low[:, c] = normed
        turned[c, :] = normed.T
        kept = jnp.where(tail, kh.astype(F32), 0.0).astype(BF16)
        carry[c, :] = jnp.where(keep, state, 0.0) + dot(kept, vh, TN)


def cotangent_kernel(grad, weight, opened, q, dcol, table, grad_opened, out, carry):
    i = pl.program_id(0)
    heads = q.shape[1] // HEAD
    width = grad.shape[2]
    gn = dot(grad[0], weight[:, :width], NT)
    for j in range(1, grad.shape[0]):
        gn = gn + dot(grad[j], weight[:, j * width : (j + 1) * width], NT)

    @pl.when(i == 0)
    def _():
        carry[...] = jnp.zeros_like(carry)

    first = table[0:1, :]
    starts = dcol[...] == first
    for h in range(heads):
        c = head_cols(h)
        opened_h = opened[:, c]
        gh = gn[:, c]
        inverse = lax.rsqrt(jnp.mean(opened_h * opened_h, axis=-1, keepdims=True) + EPSILON)
        normed = opened_h * inverse
        go = inverse * (gh - normed * jnp.mean(gh * normed, axis=-1, keepdims=True))
        grad_opened[:, c] = go
        kept = jnp.where(starts, q[:, c].astype(F32), 0.0).astype(BF16)
        carry[c, :] += dot(kept, go.astype(BF16), TN)

    @pl.when(i == pl.num_programs(0) - 1)
    def _():
        size = heads * HEAD
        out[:size, :] = carry[...].astype(BF16)
        out[size:, :] = jnp.broadcast_to(first, (16, HEAD)).astype(BF16)


def split(value):
    high = value.astype(BF16)
    return high, (value - high.astype(F32)).astype(BF16)


def query_kernel(go, k, v, dcol, drow, table, states, out):
    i = pl.program_id(0)
    heads = k.shape[1] // HEAD
    first = table[pl.ds(i, 1), :]
    docs = dcol[...]
    joined = docs == first
    t = lax.broadcasted_iota(jnp.int32, (CHUNK, CHUNK), 0)
    u = lax.broadcasted_iota(jnp.int32, (CHUNK, CHUNK), 1)
    mask = (t >= u) & (docs[:, :1] == drow[...])
    for h in range(heads):
        c = head_cols(h)
        high, rest = split(go[:, c])
        vh = v[:, c]
        both = jnp.concatenate([high, rest], axis=1)
        twice = jnp.concatenate([vh, vh], axis=1)
        scores = jnp.where(mask, dot(both, twice, NT), 0.0).astype(BF16)
        carried = jnp.where(joined, dot(high, states[0, c, :], NT), 0.0)
        out[:, c] = (dot(scores, k[:, c], NN) + carried).astype(BF16)


def key_value_kernel(go, q, k, v, dcol, drow, table, *refs):
    arrived, (grad_k, grad_v, carry) = refs[:-3], refs[-3:]
    step = pl.program_id(0)
    i = pl.num_programs(0) - 1 - step
    heads = k.shape[1] // HEAD
    last = table[pl.ds(4 + i, 1), :]
    previous = table[pl.ds(3 + i, 1), :]

    @pl.when(step == 0)
    def _():
        carry[...] = entering_state(arrived[:3], arrived[3:], last, table[9:10, :])

    docs = dcol[...]
    joined = docs == last
    ahead = docs == previous
    keep = previous == last
    u = lax.broadcasted_iota(jnp.int32, (CHUNK, CHUNK), 0)
    t = lax.broadcasted_iota(jnp.int32, (CHUNK, CHUNK), 1)
    mask = (t >= u) & (docs[:, :1] == drow[...])
    for h in range(heads):
        c = head_cols(h)
        high, rest = split(go[:, c])
        qh, kh, vh = q[:, c], k[:, c], v[:, c]
        state = carry[c, :]
        state_low = state.astype(BF16)
        both = jnp.concatenate([high, rest], axis=1)
        twice = jnp.concatenate([vh, vh], axis=1)
        scores = jnp.where(mask, dot(kh, qh, NT), 0.0).astype(BF16)
        grad_scores = jnp.where(mask, dot(twice, both, NT), 0.0).astype(BF16)
        grad_v[:, c] = (
            dot(scores, high, NN) + jnp.where(joined, dot(kh, state_low, NN), 0.0)
        ).astype(BF16)
        grad_k[:, c] = (
            dot(grad_scores, qh, NN) + jnp.where(joined, dot(vh, state_low, NT), 0.0)
        ).astype(BF16)
        kept = jnp.where(ahead, qh.astype(F32), 0.0).astype(BF16)
        carry[c, :] = jnp.where(keep, state, 0.0) + dot(kept, high, TN)


def weight_kernel(turned, grad, out):
    low = dot(turned[...], grad[0], NN).astype(BF16)
    half = low.shape[1] // 2
    out[0] = low[:, :half]
    out[1] = low[:, half:]


def attended_kernel(places, *refs):
    near, far, columns_of = refs[:6], refs[6:10], refs[10:18]
    out, columns, sems = refs[18:]
    i = pl.program_id(0)

    def copies():
        for y in range(4):
            for x in range(4):
                for o in range(2):
                    group = places[2 * y + o]
                    row = pl.multiple_of(places[8 + x] * HEAD, HEAD)
                    to = columns.at[group, pl.ds(row, HEAD)]
                    piece = columns_of[2 * y + x // 2].at[x % 2, o]
                    yield pltpu.make_async_copy(piece, to, sems.at[8 * y + 2 * x + o])

    @pl.when(i == 0)
    def _():
        for copy in copies():
            copy.start()
        for copy in copies():
            copy.wait()

    early = i < pl.num_programs(0) // 2
    pieces = [ref[...] for ref in near]
    pieces += [jnp.where(early, far[p][...], far[p + 1][...]) for p in (0, 2)]
    total = None
    for p, piece in enumerate(pieces):
        part = dot(piece, columns[places[12 + p]], NN)
        total = part if total is None else total + part
    out[...] = total.astype(BF16)


def turned_by(value, axis, step):
    size = lax.axis_size(axis)
    return lax.ppermute(value, axis, [(i, (i + step) % size) for i in range(size)])


def moved_by(value, axis, step):
    size = lax.axis_size(axis)
    pairs = [(i, i + step) for i in range(size) if 0 <= i + step < size]
    return lax.ppermute(value, axis, pairs)


def swapped(value):
    return lax.ppermute(value, "core", [(0, 1), (1, 0)])


def pick(value, index, axis=0):
    return lax.dynamic_index_in_dim(value, index, axis, keepdims=False)


def exchanged(state, step, extra=()):
    beside = [turned_by(state, "cy", step * s) for s in range(1, 4)]
    beside, extra = lax.optimization_barrier((beside, extra))
    row = pl.pallas_call(
        lambda *refs: row_kernel(step > 0, *refs),
        out_shape=jax.ShapeDtypeStruct(state.shape, state.dtype),
        name="row_state",
    )(state, *beside)
    return beside + [moved_by(row, "cx", step * s) for s in range(1, 3)], extra


def column_strip(out_weight, share, cx):
    cy, z = lax.axis_index("cy"), lax.axis_index("z")
    at = (cx * HEAD, (z - cy) % 4 * 2 * share)
    sent = lax.dynamic_slice(out_weight, at, (HEAD, 2 * share))
    pairs = [(4 * y + (i + y) % 4, 4 * y + i) for y in range(4) for i in range(4)]
    return lax.ppermute(sent, ("cy", "z"), pairs)


def column_pieces(strip, share, core):
    mine = lax.dynamic_slice(strip, (0, core * share), (HEAD, share))
    other = lax.dynamic_slice(strip, (0, (1 - core) * share), (HEAD, share))
    both = jnp.stack([mine, swapped(other)])
    lines = [both] + [turned_by(both, "cx", s) for s in range(1, 4)]
    return jnp.stack(lines[:2]), jnp.stack(lines[2:])


def body(queries, keys, values, doc_ids, out_weight, grad_out):
    rows, width = queries.shape
    blocks = rows // CHUNK
    groups = lax.axis_size(TENSOR)
    share = grad_out.shape[1]
    size = width
    payload = jax.ShapeDtypeStruct((size + 16, HEAD), BF16)
    cx, cy = lax.axis_index("cx"), lax.axis_index("cy")
    z, core = lax.axis_index("z"), lax.axis_index("core")

    grad_whole = lax.all_gather(grad_out, TENSOR, axis=0)

    docs = doc_ids.astype(F32)
    dcol = jnp.broadcast_to(docs[:, None], (rows, HEAD))
    drow = docs[None, :]
    chunked = docs.reshape(blocks, CHUNK)
    place = cy.astype(F32)[None]
    table = jnp.concatenate([chunked[:, 0], chunked[:, -1], place, 3 - place, jnp.zeros((6,), F32)])
    table = jnp.broadcast_to(table[:, None], (16, HEAD))

    tail = pl.pallas_call(tail_kernel, out_shape=payload, name="tail")(keys, values, dcol, table)
    arrived, strip = exchanged(tail, 1, column_strip(out_weight, share, cx))
    own = column_pieces(strip, share, core)
    arrived, own = lax.optimization_barrier((arrived, own))
    early = [turned_by(own[0], "cy", -1), turned_by(own[1], "cy", 1)]
    later = [turned_by(own[1], "cy", -1), turned_by(own[0], "cy", 1)]

    row_block = pl.BlockSpec((1, CHUNK), lambda i: (0, i))
    state_block = pl.BlockSpec((1, size, HEAD), lambda i: (i, 0, 0))
    opened, low, turned, states = pl.pallas_call(
        forward_kernel,
        grid=(blocks,),
        in_specs=[rows_of(width)] * 3
        + [rows_of(HEAD), row_block, whole(table.shape)]
        + [whole(payload.shape)] * len(arrived),
        out_specs=[
            rows_of(width),
            rows_of(width),
            pl.BlockSpec((width, CHUNK), lambda i: (0, i)),
            state_block,
        ],
        out_shape=[
            jax.ShapeDtypeStruct((rows, width), F32),
            jax.ShapeDtypeStruct((rows, width), BF16),
            jax.ShapeDtypeStruct((width, rows), BF16),
            jax.ShapeDtypeStruct((blocks, size, HEAD), BF16),
        ],
        scratch_shapes=[pltpu.VMEM((size, HEAD), F32)],
        compiler_params=params(),
        name="forward",
    )(queries, keys, values, dcol, drow, table, *arrived)

    term = pl.pallas_call(
        weight_kernel,
        grid=(groups,),
        in_specs=[whole((width, rows)), pl.BlockSpec((1, rows, share), lambda j: (j, 0, 0))],
        out_specs=pl.BlockSpec((2, width, share // 2), lambda j: (j, 0, 0)),
        out_shape=jax.ShapeDtypeStruct((2 * groups, width, share // 2), BF16),
        compiler_params=params(),
        name="weight_grad",
    )(turned, grad_whole)
    term, low, early, later = lax.optimization_barrier((term, low, early, later))
    across = [turned_by(early[0], "cy", -1), turned_by(early[1], "cy", 1)]
    grad_part = lax.psum_scatter(term, CTX, scatter_dimension=0, tiled=True)

    half_rows = rows // 2
    above = turned_by(low, "z", -1)
    below = turned_by(low, "z", 1)

    grad_opened, head = pl.pallas_call(
        cotangent_kernel,
        grid=(blocks,),
        in_specs=[
            pl.BlockSpec((groups, CHUNK, share), lambda i: (0, i, 0)),
            whole(out_weight.shape),
            rows_of(width),
            rows_of(width),
            rows_of(HEAD),
            whole(table.shape),
        ],
        out_specs=[rows_of(width), whole(payload.shape)],
        out_shape=[jax.ShapeDtypeStruct((rows, width), F32), payload],
        scratch_shapes=[pltpu.VMEM((size, HEAD), F32)],
        compiler_params=params(),
        name="cotangent",
    )(grad_whole, out_weight, opened, queries, dcol, table)
    head, above, below = lax.optimization_barrier((head, above, below))
    returned, (low, above, below) = exchanged(head, -1, (low, above, below))
    far_a = turned_by(above[:half_rows], "z", -1)
    far_b = turned_by(below[half_rows:], "z", 1)
    near = [low, swapped(low), above, swapped(above), below, swapped(below)]
    grad_opened, across = lax.optimization_barrier((grad_opened, across))
    grad_query = pl.pallas_call(
        query_kernel,
        grid=(blocks,),
        in_specs=[rows_of(width)] * 3
        + [rows_of(HEAD), row_block, whole(table.shape), state_block],
        out_specs=rows_of(width),
        out_shape=jax.ShapeDtypeStruct((rows, width), BF16),
        compiler_params=params(),
        name="grad_query",
    )(grad_opened, keys, values, dcol, drow, table, states)


    ready = (returned, grad_query, far_a, far_b)
    returned, grad_query, far_a, far_b = lax.optimization_barrier(ready)
    far = [far_a, far_b, swapped(far_a), swapped(far_b)]
    back_row = pl.BlockSpec((1, CHUNK), lambda i: (0, blocks - 1 - i))
    grad_key, grad_value = pl.pallas_call(
        key_value_kernel,
        grid=(blocks,),
        in_specs=[rows_of(width, blocks)] * 4
        + [rows_of(HEAD, blocks), back_row, whole(table.shape)]
        + [whole(payload.shape)] * len(returned),
        out_specs=[rows_of(width, blocks)] * 2,
        out_shape=[jax.ShapeDtypeStruct((rows, width), BF16)] * 2,
        scratch_shapes=[pltpu.VMEM((size, HEAD), F32)],
        compiler_params=params(),
        name="grad_key_value",
    )(grad_opened, queries, keys, values, dcol, drow, table, *returned)

    near, grad_key = lax.optimization_barrier((near, grad_key))
    columns = [*own, early[0], later[0], *across, later[1], early[1]]
    sides = (core, 1 - core)
    around = [2 * ((z + cy + s) % 4) + side for s in range(4) for side in sides]
    heads_at = [(cx - s) % 4 for s in range(4)]
    groups_at = [2 * ((z + s) % 4) + side for s in (0, 1, 3, 2) for side in sides]
    held = pl.BlockSpec(memory_space=pl.ANY)
    every = pl.BlockSpec((CHUNK, width), lambda i, at: (i, 0))
    upper = pl.BlockSpec((CHUNK, width), lambda i, at: (jnp.minimum(i, blocks // 2 - 1), 0))
    lower = pl.BlockSpec((CHUNK, width), lambda i, at: (jnp.maximum(i - blocks // 2, 0), 0))
    attended = pl.pallas_call(
        attended_kernel,
        grid_spec=pltpu.PrefetchScalarGridSpec(
            num_scalar_prefetch=1,
            grid=(blocks,),
            in_specs=[every] * 6 + [upper, lower] * 2 + [held] * 8,
            out_specs=pl.BlockSpec((CHUNK, share), lambda i, at: (i, 0)),
            scratch_shapes=[
                pltpu.VMEM((groups, width, share), BF16),
                pltpu.SemaphoreType.DMA((32,)),
            ],
        ),
        out_shape=jax.ShapeDtypeStruct((rows, share), BF16),
        compiler_params=params(),
        name="attended",
    )(jnp.stack(around + heads_at + groups_at), *near, *far, *columns)
    ready = (grad_part, attended)
    grad_part, attended = lax.optimization_barrier(ready)
    grad_weight = grad_part.reshape(width, share // 2).astype(F32)
    return attended, grad_query, grad_key, grad_value, grad_weight


def solution(mesh):
    finer = Mesh(mesh.devices.reshape(4, 4, 4, 2), ("cx", "cy", "z", "core"))
    by_both = P(CTX, TENSOR)
    return jax.shard_map(
        body,
        mesh=finer,
        in_specs=(by_both, by_both, by_both, P(CTX), P(TENSOR, None), by_both),
        out_specs=(by_both, by_both, by_both, by_both, P(TENSOR, CTX)),
        check_vma=False,
    )
```

```python
import jax
import jax.numpy as jnp
from jax import lax
from jax.experimental import pallas as pl
from jax.experimental.pallas import tpu as pltpu
from jax.sharding import Mesh
from jax.sharding import PartitionSpec as P

HEAD = 128
CHUNK = 256
CTX = ("cx", "cy")
TENSOR = ("z", "core")
EPSILON = 1e-06
F32 = jnp.float32
BF16 = jnp.bfloat16
NT = (((1,), (1,)), ((), ()))
TN = (((0,), (0,)), ((), ()))
NN = (((1,), (0,)), ((), ()))


def dot(a, b, dims):
    return lax.dot_general(a, b, dims, preferred_element_type=F32)


def whole(shape):
    return pl.BlockSpec(shape, lambda *_: (0,) * len(shape))


def rows_of(width, count=None):
    if count is None:
        return pl.BlockSpec((CHUNK, width), lambda i: (i, 0))
    return pl.BlockSpec((CHUNK, width), lambda i: (count - 1 - i, 0))


def head_cols(h):
    return slice(h * HEAD, (h + 1) * HEAD)


def params():
    return pltpu.CompilerParams(vmem_limit_bytes=56 << 20, dimension_semantics=("arbitrary",))


def state_of(ref):
    return ref[:-16, :].astype(F32), ref[-16:-15, :].astype(F32)


def entering_state(beside, rows, doc, place):
    total = None
    for s, ref in enumerate(beside):
        state, found = state_of(ref)
        part = jnp.where((found == doc) & (place > s + 0.5), state, 0.0)
        total = part if total is None else total + part
    for ref in rows:
        state, found = state_of(ref)
        total = total + jnp.where(found == doc, state, 0.0)
    return total


def row_kernel(latest, *refs):
    states = [state_of(ref) for ref in refs[:-1]]
    out = refs[-1]
    doc = states[0][1]
    for _, found in states[1:]:
        doc = jnp.maximum(doc, found) if latest else jnp.minimum(doc, found)
    total = None
    for state, found in states:
        part = jnp.where(found == doc, state, 0.0)
        total = part if total is None else total + part
    out[:-16, :] = total.astype(BF16)
    out[-16:, :] = jnp.broadcast_to(doc, (16, HEAD)).astype(BF16)


def tail_kernel(k, v, dcol, table, out):
    heads = k.shape[1] // HEAD
    last = table[7:8, :]
    tail = dcol[...] == last
    for h in range(heads):
        c = head_cols(h)
        kept = jnp.where(tail, k[:, c].astype(F32), 0.0).astype(BF16)
        out[c, :] = dot(kept, v[:, c], TN).astype(BF16)
    out[heads * HEAD :, :] = jnp.broadcast_to(last, (16, HEAD)).astype(BF16)


def forward_kernel(q, k, v, dcol, drow, table, *refs):
    arrived, (opened, low, turned, states, carry) = refs[:-5], refs[-5:]
    i = pl.program_id(0)
    heads = q.shape[1] // HEAD
    first = table[pl.ds(i, 1), :]
    following = table[pl.ds(i + 1, 1), :]

    @pl.when(i == 0)
    def _():
        carry[...] = entering_state(arrived[:3], arrived[3:], first, table[8:9, :])

    docs = dcol[...]
    joined = docs == first
    tail = docs == following
    keep = following == first
    t = lax.broadcasted_iota(jnp.int32, (CHUNK, CHUNK), 0)
    u = lax.broadcasted_iota(jnp.int32, (CHUNK, CHUNK), 1)
    mask = (t >= u) & (docs[:, :1] == drow[...])
    for h in range(heads):
        c = head_cols(h)
        qh, kh, vh = q[:, c], k[:, c], v[:, c]
        state = carry[c, :]
        state_low = state.astype(BF16)
        states[0, c, :] = state_low
        scores = jnp.where(mask, dot(qh, kh, NT), 0.0).astype(BF16)
        out = dot(scores, vh, NN) + jnp.where(joined, dot(qh, state_low, NN), 0.0)
        opened[:, c] = out
        inverse = lax.rsqrt(jnp.mean(out * out, axis=-1, keepdims=True) + EPSILON)
        normed = (out * inverse).astype(BF16)
        low[:, c] = normed
        turned[c, :] = normed.T
        kept = jnp.where(tail, kh.astype(F32), 0.0).astype(BF16)
        carry[c, :] = jnp.where(keep, state, 0.0) + dot(kept, vh, TN)


def cotangent_kernel(grad, weight, opened, q, dcol, table, grad_opened, out, carry):
    i = pl.program_id(0)
    heads = q.shape[1] // HEAD
    width = grad.shape[2]
    gn = dot(grad[0], weight[:, :width], NT)
    for j in range(1, grad.shape[0]):
        gn = gn + dot(grad[j], weight[:, j * width : (j + 1) * width], NT)

    @pl.when(i == 0)
    def _():
        carry[...] = jnp.zeros_like(carry)

    first = table[0:1, :]
    starts = dcol[...] == first
    for h in range(heads):
        c = head_cols(h)
        opened_h = opened[:, c]
        gh = gn[:, c]
        inverse = lax.rsqrt(jnp.mean(opened_h * opened_h, axis=-1, keepdims=True) + EPSILON)
        normed = opened_h * inverse
        go = inverse * (gh - normed * jnp.mean(gh * normed, axis=-1, keepdims=True))
        grad_opened[:, c] = go
        kept = jnp.where(starts, q[:, c].astype(F32), 0.0).astype(BF16)
        carry[c, :] += dot(kept, go.astype(BF16), TN)

    @pl.when(i == pl.num_programs(0) - 1)
    def _():
        size = heads * HEAD
        out[:size, :] = carry[...].astype(BF16)
        out[size:, :] = jnp.broadcast_to(first, (16, HEAD)).astype(BF16)


def split(value):
    high = value.astype(BF16)
    return high, (value - high.astype(F32)).astype(BF16)


def query_kernel(go, k, v, dcol, drow, table, states, out):
    i = pl.program_id(0)
    heads = k.shape[1] // HEAD
    first = table[pl.ds(i, 1), :]
    docs = dcol[...]
    joined = docs == first
    t = lax.broadcasted_iota(jnp.int32, (CHUNK, CHUNK), 0)
    u = lax.broadcasted_iota(jnp.int32, (CHUNK, CHUNK), 1)
    mask = (t >= u) & (docs[:, :1] == drow[...])
    for h in range(heads):
        c = head_cols(h)
        high, rest = split(go[:, c])
        vh = v[:, c]
        both = jnp.concatenate([high, rest], axis=1)
        twice = jnp.concatenate([vh, vh], axis=1)
        scores = jnp.where(mask, dot(both, twice, NT), 0.0).astype(BF16)
        carried = jnp.where(joined, dot(high, states[0, c, :], NT), 0.0)
        out[:, c] = (dot(scores, k[:, c], NN) + carried).astype(BF16)


def key_value_kernel(go, q, k, v, dcol, drow, table, *refs):
    arrived, (grad_k, grad_v, carry) = refs[:-3], refs[-3:]
    step = pl.program_id(0)
    i = pl.num_programs(0) - 1 - step
    heads = k.shape[1] // HEAD
    last = table[pl.ds(4 + i, 1), :]
    previous = table[pl.ds(3 + i, 1), :]

    @pl.when(step == 0)
    def _():
        carry[...] = entering_state(arrived[:3], arrived[3:], last, table[9:10, :])

    docs = dcol[...]
    joined = docs == last
    ahead = docs == previous
    keep = previous == last
    u = lax.broadcasted_iota(jnp.int32, (CHUNK, CHUNK), 0)
    t = lax.broadcasted_iota(jnp.int32, (CHUNK, CHUNK), 1)
    mask = (t >= u) & (docs[:, :1] == drow[...])
    for h in range(heads):
        c = head_cols(h)
        high, rest = split(go[:, c])
        qh, kh, vh = q[:, c], k[:, c], v[:, c]
        state = carry[c, :]
        state_low = state.astype(BF16)
        both = jnp.concatenate([high, rest], axis=1)
        twice = jnp.concatenate([vh, vh], axis=1)
        scores = jnp.where(mask, dot(kh, qh, NT), 0.0).astype(BF16)
        grad_scores = jnp.where(mask, dot(twice, both, NT), 0.0).astype(BF16)
        grad_v[:, c] = (
            dot(scores, high, NN) + jnp.where(joined, dot(kh, state_low, NN), 0.0)
        ).astype(BF16)
        grad_k[:, c] = (
            dot(grad_scores, qh, NN) + jnp.where(joined, dot(vh, state_low, NT), 0.0)
        ).astype(BF16)
        kept = jnp.where(ahead, qh.astype(F32), 0.0).astype(BF16)
        carry[c, :] = jnp.where(keep, state, 0.0) + dot(kept, high, TN)


def weight_kernel(turned, grad, out):
    for p in range(2):
        low = dot(turned[...], grad[p], NN).astype(BF16)
        half = low.shape[1] // 2
        out[0, 2 * p] = low[:, :half]
        out[0, 2 * p + 1] = low[:, half:]


def sum_kernel(place, own, *refs):
    total = own[0].astype(F32)
    for ref in refs[:-1]:
        total = total + ref[...].astype(F32)
    refs[-1][...] = total


def attended_kernel(places, *refs):
    near, far, columns_of = refs[:6], refs[6:10], refs[10:18]
    out, columns, sems = refs[18:]
    i = pl.program_id(0)

    def copies():
        for y in range(4):
            for x in range(4):
                for o in range(2):
                    group = places[2 * y + o]
                    row = pl.multiple_of(places[8 + x] * HEAD, HEAD)
                    to = columns.at[group, pl.ds(row, HEAD)]
                    cut = (3, 3, 2, 1)[y]
                    piece = columns_of[2 * y + (x >= cut)].at[x if x < cut else x - cut, o]
                    yield pltpu.make_async_copy(piece, to, sems.at[8 * y + 2 * x + o])

    @pl.when(i == 0)
    def _():
        for copy in copies():
            copy.start()
        for copy in copies():
            copy.wait()

    early = i < pl.num_programs(0) // 2
    pieces = [ref[...] for ref in near]
    pieces += [jnp.where(early, far[p][...], far[p + 1][...]) for p in (0, 2)]
    total = None
    for p, piece in enumerate(pieces):
        part = dot(piece, columns[places[12 + p]], NN)
        total = part if total is None else total + part
    out[...] = total.astype(BF16)


def turned_by(value, axis, step):
    size = lax.axis_size(axis)
    return lax.ppermute(value, axis, [(i, (i + step) % size) for i in range(size)])


def moved_by(value, axis, step):
    size = lax.axis_size(axis)
    pairs = [(i, i + step) for i in range(size) if 0 <= i + step < size]
    return lax.ppermute(value, axis, pairs)


def swapped(value):
    return lax.ppermute(value, "core", [(0, 1), (1, 0)])


def pick(value, index, axis=0):
    return lax.dynamic_index_in_dim(value, index, axis, keepdims=False)


def exchanged(state, step, extra=()):
    beside = [turned_by(state, "cy", step * s) for s in range(1, 4)]
    beside, extra = lax.optimization_barrier((beside, extra))
    row = pl.pallas_call(
        lambda *refs: row_kernel(step > 0, *refs),
        out_shape=jax.ShapeDtypeStruct(state.shape, state.dtype),
        name="row_state",
    )(state, *beside)
    return beside + [moved_by(row, "cx", step * s) for s in range(1, 3)], extra


def column_strip(out_weight, share, cx):
    cy, z = lax.axis_index("cy"), lax.axis_index("z")
    at = (cx * HEAD, (z - cy) % 4 * 2 * share)
    sent = lax.dynamic_slice(out_weight, at, (HEAD, 2 * share))
    pairs = [(4 * y + (i + y) % 4, 4 * y + i) for y in range(4) for i in range(4)]
    return lax.ppermute(sent, ("cy", "z"), pairs)


def column_pieces(strip, share, core):
    mine = lax.dynamic_slice(strip, (0, core * share), (HEAD, share))
    other = lax.dynamic_slice(strip, (0, (1 - core) * share), (HEAD, share))
    both = jnp.stack([mine, swapped(other)])
    lines = [both] + [turned_by(both, "cx", s) for s in range(1, 4)]
    return jnp.stack(lines[:3]), jnp.stack(lines[1:]), lines[0][None], lines[3][None]


def row_sum(mine, cy):
    got = [turned_by(pick(mine, (cy + s) % 4), "cy", s) for s in range(1, 4)]
    height, part = mine.shape[1:]
    block = (CHUNK, part)
    return pl.pallas_call(
        sum_kernel,
        grid_spec=pltpu.PrefetchScalarGridSpec(
            num_scalar_prefetch=1,
            grid=(height // CHUNK,),
            in_specs=[pl.BlockSpec((1, *block), lambda i, p: (p[0], i, 0))]
            + [pl.BlockSpec(block, lambda i, p: (i, 0))] * 3,
            out_specs=pl.BlockSpec(block, lambda i, p: (i, 0)),
        ),
        out_shape=jax.ShapeDtypeStruct((height, part), F32),
        compiler_params=params(),
        name="last_sum",
    )(cy[None], mine, *got)


def body(queries, keys, values, doc_ids, out_weight, grad_out):
    rows, width = queries.shape
    blocks = rows // CHUNK
    groups = lax.axis_size(TENSOR)
    share = grad_out.shape[1]
    size = width
    payload = jax.ShapeDtypeStruct((size + 16, HEAD), BF16)
    cx, cy = lax.axis_index("cx"), lax.axis_index("cy")
    z, core = lax.axis_index("z"), lax.axis_index("core")

    grad_whole = lax.all_gather(grad_out, TENSOR, axis=0)

    docs = doc_ids.astype(F32)
    dcol = jnp.broadcast_to(docs[:, None], (rows, HEAD))
    drow = docs[None, :]
    chunked = docs.reshape(blocks, CHUNK)
    place = cy.astype(F32)[None]
    table = jnp.concatenate([chunked[:, 0], chunked[:, -1], place, 3 - place, jnp.zeros((6,), F32)])
    table = jnp.broadcast_to(table[:, None], (16, HEAD))

    tail = pl.pallas_call(tail_kernel, out_shape=payload, name="tail")(keys, values, dcol, table)
    arrived, strip = exchanged(tail, 1, column_strip(out_weight, share, cx))
    own = column_pieces(strip, share, core)
    arrived, own = lax.optimization_barrier((arrived, own))
    early = [turned_by(own[0], "cy", -1), turned_by(own[1], "cy", 1)]

    row_block = pl.BlockSpec((1, CHUNK), lambda i: (0, i))
    state_block = pl.BlockSpec((1, size, HEAD), lambda i: (i, 0, 0))
    opened, low, turned, states = pl.pallas_call(
        forward_kernel,
        grid=(blocks,),
        in_specs=[rows_of(width)] * 3
        + [rows_of(HEAD), row_block, whole(table.shape)]
        + [whole(payload.shape)] * len(arrived),
        out_specs=[
            rows_of(width),
            rows_of(width),
            pl.BlockSpec((width, CHUNK), lambda i: (0, i)),
            state_block,
        ],
        out_shape=[
            jax.ShapeDtypeStruct((rows, width), F32),
            jax.ShapeDtypeStruct((rows, width), BF16),
            jax.ShapeDtypeStruct((width, rows), BF16),
            jax.ShapeDtypeStruct((blocks, size, HEAD), BF16),
        ],
        scratch_shapes=[pltpu.VMEM((size, HEAD), F32)],
        compiler_params=params(),
        name="forward",
    )(queries, keys, values, dcol, drow, table, *arrived)

    term = pl.pallas_call(
        weight_kernel,
        grid=(groups // 2,),
        in_specs=[whole((width, rows)), pl.BlockSpec((2, rows, share), lambda j: (j, 0, 0))],
        out_specs=pl.BlockSpec((1, 4, width, share // 2), lambda j: (j, 0, 0, 0)),
        out_shape=jax.ShapeDtypeStruct((4, 4, width, share // 2), BF16),
        compiler_params=params(),
        name="weight_grad",
    )(turned, grad_whole)
    term, low, early, own = lax.optimization_barrier((term, low, early, own))
    across = [turned_by(early[0][:2], "cy", -1), turned_by(early[1][1:], "cy", 1)]
    later = turned_by(own[3], "cy", -1)
    grad_part = lax.psum_scatter(term, "cx", scatter_dimension=0, tiled=True)[0]

    half_rows = rows // 2
    above = turned_by(low, "z", -1)
    below = turned_by(low, "z", 1)

    grad_opened, head = pl.pallas_call(
        cotangent_kernel,
        grid=(blocks,),
        in_specs=[
            pl.BlockSpec((groups, CHUNK, share), lambda i: (0, i, 0)),
            whole(out_weight.shape),
            rows_of(width),
            rows_of(width),
            rows_of(HEAD),
            whole(table.shape),
        ],
        out_specs=[rows_of(width), whole(payload.shape)],
        out_shape=[jax.ShapeDtypeStruct((rows, width), F32), payload],
        scratch_shapes=[pltpu.VMEM((size, HEAD), F32)],
        compiler_params=params(),
        name="cotangent",
    )(grad_whole, out_weight, opened, queries, dcol, table)
    ready = (head, across, later, above, below)
    head, across, later, above, below = lax.optimization_barrier(ready)
    far_a = turned_by(above[:half_rows], "z", -1)
    far_b = turned_by(below[half_rows:], "z", 1)
    moved = (far_a, far_b, low, above, below, own)
    returned, (far_a, far_b, low, above, below, own) = exchanged(head, -1, moved)
    near = [low, swapped(low), above, swapped(above), below, swapped(below)]
    far = [far_a, far_b, swapped(far_a), swapped(far_b)]
    near, far, own = lax.optimization_barrier((near, far, own))
    last = turned_by(own[2], "cy", 1)
    grad_query = pl.pallas_call(
        query_kernel,
        grid=(blocks,),
        in_specs=[rows_of(width)] * 3
        + [rows_of(HEAD), row_block, whole(table.shape), state_block],
        out_specs=rows_of(width),
        out_shape=jax.ShapeDtypeStruct((rows, width), BF16),
        compiler_params=params(),
        name="grad_query",
    )(grad_opened, keys, values, dcol, drow, table, states)


    last, grad_query = lax.optimization_barrier((last, grad_query))
    columns = [own[0], own[3], early[0], later, *across, last, early[1]]

    sides = (core, 1 - core)
    around = [2 * ((z + cy + s) % 4) + side for s in range(4) for side in sides]
    heads_at = [(cx - s) % 4 for s in range(4)]
    groups_at = [2 * ((z + s) % 4) + side for s in (0, 1, 3, 2) for side in sides]
    held = pl.BlockSpec(memory_space=pl.ANY)
    every = pl.BlockSpec((CHUNK, width), lambda i, at: (i, 0))
    upper = pl.BlockSpec((CHUNK, width), lambda i, at: (jnp.minimum(i, blocks // 2 - 1), 0))
    lower = pl.BlockSpec((CHUNK, width), lambda i, at: (jnp.maximum(i - blocks // 2, 0), 0))
    attended = pl.pallas_call(
        attended_kernel,
        grid_spec=pltpu.PrefetchScalarGridSpec(
            num_scalar_prefetch=1,
            grid=(blocks,),
            in_specs=[every] * 6 + [upper, lower] * 2 + [held] * 8,
            out_specs=pl.BlockSpec((CHUNK, share), lambda i, at: (i, 0)),
            scratch_shapes=[
                pltpu.VMEM((groups, width, share), BF16),
                pltpu.SemaphoreType.DMA((32,)),
            ],
        ),
        out_shape=jax.ShapeDtypeStruct((rows, share), BF16),
        compiler_params=params(),
        name="attended",
    )(jnp.stack(around + heads_at + groups_at), *near, *far, *columns)
    ready = (returned, grad_opened, grad_part, attended)
    returned, grad_opened, grad_part, attended = lax.optimization_barrier(ready)

    back_row = pl.BlockSpec((1, CHUNK), lambda i: (0, blocks - 1 - i))
    grad_key, grad_value = pl.pallas_call(
        key_value_kernel,
        grid=(blocks,),
        in_specs=[rows_of(width, blocks)] * 4
        + [rows_of(HEAD, blocks), back_row, whole(table.shape)]
        + [whole(payload.shape)] * len(returned),
        out_specs=[rows_of(width, blocks)] * 2,
        out_shape=[jax.ShapeDtypeStruct((rows, width), BF16)] * 2,
        scratch_shapes=[pltpu.VMEM((size, HEAD), F32)],
        compiler_params=params(),
        name="grad_key_value",
    )(grad_opened, queries, keys, values, dcol, drow, table, *returned)

    grad_weight = row_sum(grad_part, cy)
    return attended, grad_query, grad_key, grad_value, grad_weight


def solution(mesh):
    finer = Mesh(mesh.devices.reshape(4, 4, 4, 2), ("cx", "cy", "z", "core"))
    by_both = P(CTX, TENSOR)
    return jax.shard_map(
        body,
        mesh=finer,
        in_specs=(by_both, by_both, by_both, P(CTX), P(TENSOR, None), by_both),
        out_specs=(by_both, by_both, by_both, by_both, P(TENSOR, CTX)),
        check_vma=False,
    )
```

```python
import jax
import jax.numpy as jnp
from jax import lax
from jax.experimental import pallas as pl
from jax.experimental.pallas import tpu as pltpu
from jax.sharding import Mesh
from jax.sharding import PartitionSpec as P

HEAD = 128
CHUNK = 256
CTX = ("cx", "cy")
TENSOR = ("z", "core")
EPSILON = 1e-06
F32 = jnp.float32
BF16 = jnp.bfloat16
NT = (((1,), (1,)), ((), ()))
TN = (((0,), (0,)), ((), ()))
NN = (((1,), (0,)), ((), ()))


def dot(a, b, dims):
    return lax.dot_general(a, b, dims, preferred_element_type=F32)


def whole(shape):
    return pl.BlockSpec(shape, lambda *_: (0,) * len(shape))


def rows_of(width, count=None):
    if count is None:
        return pl.BlockSpec((CHUNK, width), lambda i: (i, 0))
    return pl.BlockSpec((CHUNK, width), lambda i: (count - 1 - i, 0))


def head_cols(h):
    return slice(h * HEAD, (h + 1) * HEAD)


def params():
    return pltpu.CompilerParams(vmem_limit_bytes=56 << 20, dimension_semantics=("arbitrary",))


def state_of(ref):
    return ref[:-16, :].astype(F32), ref[-16:-15, :].astype(F32)


def entering_state(beside, rows, doc, place):
    total = None
    for s, ref in enumerate(beside):
        state, found = state_of(ref)
        part = jnp.where((found == doc) & (place > s + 0.5), state, 0.0)
        total = part if total is None else total + part
    for ref in rows:
        state, found = state_of(ref)
        total = total + jnp.where(found == doc, state, 0.0)
    return total


def row_kernel(latest, *refs):
    states = [state_of(ref) for ref in refs[:-1]]
    out = refs[-1]
    doc = states[0][1]
    for _, found in states[1:]:
        doc = jnp.maximum(doc, found) if latest else jnp.minimum(doc, found)
    total = None
    for state, found in states:
        part = jnp.where(found == doc, state, 0.0)
        total = part if total is None else total + part
    out[:-16, :] = total.astype(BF16)
    out[-16:, :] = jnp.broadcast_to(doc, (16, HEAD)).astype(BF16)


def tail_kernel(k, v, dcol, table, out):
    heads = k.shape[1] // HEAD
    last = table[7:8, :]
    tail = dcol[...] == last
    for h in range(heads):
        c = head_cols(h)
        kept = jnp.where(tail, k[:, c].astype(F32), 0.0).astype(BF16)
        out[c, :] = dot(kept, v[:, c], TN).astype(BF16)
    out[heads * HEAD :, :] = jnp.broadcast_to(last, (16, HEAD)).astype(BF16)


def forward_kernel(q, k, v, dcol, drow, table, *refs):
    arrived, (opened, low, turned, states, carry) = refs[:-5], refs[-5:]
    i = pl.program_id(0)
    heads = q.shape[1] // HEAD
    first = table[pl.ds(i, 1), :]
    following = table[pl.ds(i + 1, 1), :]

    @pl.when(i == 0)
    def _():
        carry[...] = entering_state(arrived[:3], arrived[3:], first, table[8:9, :])

    docs = dcol[...]
    joined = docs == first
    tail = docs == following
    keep = following == first
    t = lax.broadcasted_iota(jnp.int32, (CHUNK, CHUNK), 0)
    u = lax.broadcasted_iota(jnp.int32, (CHUNK, CHUNK), 1)
    mask = (t >= u) & (docs[:, :1] == drow[...])
    for h in range(heads):
        c = head_cols(h)
        qh, kh, vh = q[:, c], k[:, c], v[:, c]
        state = carry[c, :]
        state_low = state.astype(BF16)
        states[0, c, :] = state_low
        scores = jnp.where(mask, dot(qh, kh, NT), 0.0).astype(BF16)
        out = dot(scores, vh, NN) + jnp.where(joined, dot(qh, state_low, NN), 0.0)
        opened[:, c] = out
        inverse = lax.rsqrt(jnp.mean(out * out, axis=-1, keepdims=True) + EPSILON)
        normed = (out * inverse).astype(BF16)
        low[:, c] = normed
        turned[c, :] = normed.T
        kept = jnp.where(tail, kh.astype(F32), 0.0).astype(BF16)
        carry[c, :] = jnp.where(keep, state, 0.0) + dot(kept, vh, TN)


def cotangent_kernel(grad, weight, opened, q, dcol, table, grad_opened, out, carry):
    i = pl.program_id(0)
    heads = q.shape[1] // HEAD
    width = grad.shape[2]
    gn = dot(grad[0], weight[:, :width], NT)
    for j in range(1, grad.shape[0]):
        gn = gn + dot(grad[j], weight[:, j * width : (j + 1) * width], NT)

    @pl.when(i == 0)
    def _():
        carry[...] = jnp.zeros_like(carry)

    first = table[0:1, :]
    starts = dcol[...] == first
    for h in range(heads):
        c = head_cols(h)
        opened_h = opened[:, c]
        gh = gn[:, c]
        inverse = lax.rsqrt(jnp.mean(opened_h * opened_h, axis=-1, keepdims=True) + EPSILON)
        normed = opened_h * inverse
        go = inverse * (gh - normed * jnp.mean(gh * normed, axis=-1, keepdims=True))
        grad_opened[:, c] = go
        kept = jnp.where(starts, q[:, c].astype(F32), 0.0).astype(BF16)
        carry[c, :] += dot(kept, go.astype(BF16), TN)

    @pl.when(i == pl.num_programs(0) - 1)
    def _():
        size = heads * HEAD
        out[:size, :] = carry[...].astype(BF16)
        out[size:, :] = jnp.broadcast_to(first, (16, HEAD)).astype(BF16)


def split(value):
    high = value.astype(BF16)
    return high, (value - high.astype(F32)).astype(BF16)


def query_kernel(go, k, v, dcol, drow, table, states, out):
    i = pl.program_id(0)
    heads = k.shape[1] // HEAD
    first = table[pl.ds(i, 1), :]
    docs = dcol[...]
    joined = docs == first
    t = lax.broadcasted_iota(jnp.int32, (CHUNK, CHUNK), 0)
    u = lax.broadcasted_iota(jnp.int32, (CHUNK, CHUNK), 1)
    mask = (t >= u) & (docs[:, :1] == drow[...])
    for h in range(heads):
        c = head_cols(h)
        high, rest = split(go[:, c])
        vh = v[:, c]
        both = jnp.concatenate([high, rest], axis=1)
        twice = jnp.concatenate([vh, vh], axis=1)
        scores = jnp.where(mask, dot(both, twice, NT), 0.0).astype(BF16)
        carried = jnp.where(joined, dot(high, states[0, c, :], NT), 0.0)
        out[:, c] = (dot(scores, k[:, c], NN) + carried).astype(BF16)


def key_value_kernel(go, q, k, v, dcol, drow, table, *refs):
    arrived, (grad_k, grad_v, carry) = refs[:-3], refs[-3:]
    step = pl.program_id(0)
    i = pl.num_programs(0) - 1 - step
    heads = k.shape[1] // HEAD
    last = table[pl.ds(4 + i, 1), :]
    previous = table[pl.ds(3 + i, 1), :]

    @pl.when(step == 0)
    def _():
        carry[...] = entering_state(arrived[:3], arrived[3:], last, table[9:10, :])

    docs = dcol[...]
    joined = docs == last
    ahead = docs == previous
    keep = previous == last
    u = lax.broadcasted_iota(jnp.int32, (CHUNK, CHUNK), 0)
    t = lax.broadcasted_iota(jnp.int32, (CHUNK, CHUNK), 1)
    mask = (t >= u) & (docs[:, :1] == drow[...])
    for h in range(heads):
        c = head_cols(h)
        high, rest = split(go[:, c])
        qh, kh, vh = q[:, c], k[:, c], v[:, c]
        state = carry[c, :]
        state_low = state.astype(BF16)
        both = jnp.concatenate([high, rest], axis=1)
        twice = jnp.concatenate([vh, vh], axis=1)
        scores = jnp.where(mask, dot(kh, qh, NT), 0.0).astype(BF16)
        grad_scores = jnp.where(mask, dot(twice, both, NT), 0.0).astype(BF16)
        grad_v[:, c] = (
            dot(scores, high, NN) + jnp.where(joined, dot(kh, state_low, NN), 0.0)
        ).astype(BF16)
        grad_k[:, c] = (
            dot(grad_scores, qh, NN) + jnp.where(joined, dot(vh, state_low, NT), 0.0)
        ).astype(BF16)
        kept = jnp.where(ahead, qh.astype(F32), 0.0).astype(BF16)
        carry[c, :] = jnp.where(keep, state, 0.0) + dot(kept, high, TN)


def weight_kernel(turned, grad, out):
    for p in range(2):
        low = dot(turned[...], grad[p], NN).astype(BF16)
        half = low.shape[1] // 2
        out[0, 2 * p] = low[:, :half]
        out[0, 2 * p + 1] = low[:, half:]


def sum_kernel(place, own, *refs):
    total = own[0].astype(F32)
    for ref in refs[:-1]:
        total = total + ref[...].astype(F32)
    refs[-1][...] = total


def attended_kernel(places, *refs):
    near, far, columns_of = refs[:6], refs[6:10], refs[10:18]
    out, columns, sems = refs[18:]
    i = pl.program_id(0)

    def copies():
        for y in range(4):
            for x in range(4):
                for o in range(2):
                    group = places[2 * y + o]
                    row = pl.multiple_of(places[8 + x] * HEAD, HEAD)
                    to = columns.at[group, pl.ds(row, HEAD)]
                    piece = columns_of[2 * y + x // 2].at[x % 2, o]
                    yield pltpu.make_async_copy(piece, to, sems.at[8 * y + 2 * x + o])

    @pl.when(i == 0)
    def _():
        for copy in copies():
            copy.start()
        for copy in copies():
            copy.wait()

    early = i < pl.num_programs(0) // 2
    pieces = [ref[...] for ref in near]
    pieces += [jnp.where(early, far[p][...], far[p + 1][...]) for p in (0, 2)]
    total = None
    for p, piece in enumerate(pieces):
        part = dot(piece, columns[places[12 + p]], NN)
        total = part if total is None else total + part
    out[...] = total.astype(BF16)


def turned_by(value, axis, step):
    size = lax.axis_size(axis)
    return lax.ppermute(value, axis, [(i, (i + step) % size) for i in range(size)])


def moved_by(value, axis, step):
    size = lax.axis_size(axis)
    pairs = [(i, i + step) for i in range(size) if 0 <= i + step < size]
    return lax.ppermute(value, axis, pairs)


def swapped(value):
    return lax.ppermute(value, "core", [(0, 1), (1, 0)])


def pick(value, index, axis=0):
    return lax.dynamic_index_in_dim(value, index, axis, keepdims=False)


def exchanged(state, step, extra=()):
    beside = [turned_by(state, "cy", step * s) for s in range(1, 4)]
    beside, extra = lax.optimization_barrier((beside, extra))
    row = pl.pallas_call(
        lambda *refs: row_kernel(step > 0, *refs),
        out_shape=jax.ShapeDtypeStruct(state.shape, state.dtype),
        name="row_state",
    )(state, *beside)
    return beside + [moved_by(row, "cx", step * s) for s in range(1, 3)], extra


def column_strip(out_weight, share, cx):
    cy, z = lax.axis_index("cy"), lax.axis_index("z")
    at = (cx * HEAD, (z - cy) % 4 * 2 * share)
    sent = lax.dynamic_slice(out_weight, at, (HEAD, 2 * share))
    pairs = [(4 * y + (i + y) % 4, 4 * y + i) for y in range(4) for i in range(4)]
    return lax.ppermute(sent, ("cy", "z"), pairs)


def column_pieces(strip, share, core):
    mine = lax.dynamic_slice(strip, (0, core * share), (HEAD, share))
    other = lax.dynamic_slice(strip, (0, (1 - core) * share), (HEAD, share))
    both = jnp.stack([mine, swapped(other)])
    lines = [both] + [turned_by(both, "cx", s) for s in range(1, 4)]
    return jnp.stack(lines[:2]), jnp.stack(lines[2:])


def row_sum(mine, cy):
    got = [turned_by(pick(mine, (cy + s) % 4), "cy", s) for s in range(1, 4)]
    height, part = mine.shape[1:]
    block = (CHUNK, part)
    return pl.pallas_call(
        sum_kernel,
        grid_spec=pltpu.PrefetchScalarGridSpec(
            num_scalar_prefetch=1,
            grid=(height // CHUNK,),
            in_specs=[pl.BlockSpec((1, *block), lambda i, p: (p[0], i, 0))]
            + [pl.BlockSpec(block, lambda i, p: (i, 0))] * 3,
            out_specs=pl.BlockSpec(block, lambda i, p: (i, 0)),
        ),
        out_shape=jax.ShapeDtypeStruct((height, part), F32),
        compiler_params=params(),
        name="last_sum",
    )(cy[None], mine, *got)


def body(queries, keys, values, doc_ids, out_weight, grad_out):
    rows, width = queries.shape
    blocks = rows // CHUNK
    groups = lax.axis_size(TENSOR)
    share = grad_out.shape[1]
    size = width
    payload = jax.ShapeDtypeStruct((size + 16, HEAD), BF16)
    cx, cy = lax.axis_index("cx"), lax.axis_index("cy")
    z, core = lax.axis_index("z"), lax.axis_index("core")

    grad_whole = lax.all_gather(grad_out, TENSOR, axis=0)

    docs = doc_ids.astype(F32)
    dcol = jnp.broadcast_to(docs[:, None], (rows, HEAD))
    drow = docs[None, :]
    chunked = docs.reshape(blocks, CHUNK)
    place = cy.astype(F32)[None]
    table = jnp.concatenate([chunked[:, 0], chunked[:, -1], place, 3 - place, jnp.zeros((6,), F32)])
    table = jnp.broadcast_to(table[:, None], (16, HEAD))

    tail = pl.pallas_call(tail_kernel, out_shape=payload, name="tail")(keys, values, dcol, table)
    arrived, strip = exchanged(tail, 1, column_strip(out_weight, share, cx))
    own = column_pieces(strip, share, core)
    arrived, own = lax.optimization_barrier((arrived, own))
    early = [turned_by(own[0], "cy", -1), turned_by(own[1], "cy", 1)]
    later = [turned_by(own[1], "cy", -1), turned_by(own[0], "cy", 1)]

    row_block = pl.BlockSpec((1, CHUNK), lambda i: (0, i))
    state_block = pl.BlockSpec((1, size, HEAD), lambda i: (i, 0, 0))
    opened, low, turned, states = pl.pallas_call(
        forward_kernel,
        grid=(blocks,),
        in_specs=[rows_of(width)] * 3
        + [rows_of(HEAD), row_block, whole(table.shape)]
        + [whole(payload.shape)] * len(arrived),
        out_specs=[
            rows_of(width),
            rows_of(width),
            pl.BlockSpec((width, CHUNK), lambda i: (0, i)),
            state_block,
        ],
        out_shape=[
            jax.ShapeDtypeStruct((rows, width), F32),
            jax.ShapeDtypeStruct((rows, width), BF16),
            jax.ShapeDtypeStruct((width, rows), BF16),
            jax.ShapeDtypeStruct((blocks, size, HEAD), BF16),
        ],
        scratch_shapes=[pltpu.VMEM((size, HEAD), F32)],
        compiler_params=params(),
        name="forward",
    )(queries, keys, values, dcol, drow, table, *arrived)

    term = pl.pallas_call(
        weight_kernel,
        grid=(groups // 2,),
        in_specs=[whole((width, rows)), pl.BlockSpec((2, rows, share), lambda j: (j, 0, 0))],
        out_specs=pl.BlockSpec((1, 4, width, share // 2), lambda j: (j, 0, 0, 0)),
        out_shape=jax.ShapeDtypeStruct((4, 4, width, share // 2), BF16),
        compiler_params=params(),
        name="weight_grad",
    )(turned, grad_whole)
    term, low, early, later = lax.optimization_barrier((term, low, early, later))
    across = [turned_by(early[0], "cy", -1), turned_by(early[1], "cy", 1)]
    grad_part = lax.psum_scatter(term, "cx", scatter_dimension=0, tiled=True)[0]

    half_rows = rows // 2
    above = turned_by(low, "z", -1)
    below = turned_by(low, "z", 1)

    grad_opened, head = pl.pallas_call(
        cotangent_kernel,
        grid=(blocks,),
        in_specs=[
            pl.BlockSpec((groups, CHUNK, share), lambda i: (0, i, 0)),
            whole(out_weight.shape),
            rows_of(width),
            rows_of(width),
            rows_of(HEAD),
            whole(table.shape),
        ],
        out_specs=[rows_of(width), whole(payload.shape)],
        out_shape=[jax.ShapeDtypeStruct((rows, width), F32), payload],
        scratch_shapes=[pltpu.VMEM((size, HEAD), F32)],
        compiler_params=params(),
        name="cotangent",
    )(grad_whole, out_weight, opened, queries, dcol, table)
    head, across, above, below = lax.optimization_barrier((head, across, above, below))
    far_a = turned_by(above[:half_rows], "z", -1)
    far_b = turned_by(below[half_rows:], "z", 1)
    moved = (far_a, far_b, low, above, below)
    returned, (far_a, far_b, low, above, below) = exchanged(head, -1, moved)
    near = [low, swapped(low), above, swapped(above), below, swapped(below)]
    far = [far_a, far_b, swapped(far_a), swapped(far_b)]
    columns = [*own, early[0], later[0], *across, later[1], early[1]]

    sides = (core, 1 - core)
    around = [2 * ((z + cy + s) % 4) + side for s in range(4) for side in sides]
    heads_at = [(cx - s) % 4 for s in range(4)]
    groups_at = [2 * ((z + s) % 4) + side for s in (0, 1, 3, 2) for side in sides]
    held = pl.BlockSpec(memory_space=pl.ANY)
    every = pl.BlockSpec((CHUNK, width), lambda i, at: (i, 0))
    upper = pl.BlockSpec((CHUNK, width), lambda i, at: (jnp.minimum(i, blocks // 2 - 1), 0))
    lower = pl.BlockSpec((CHUNK, width), lambda i, at: (jnp.maximum(i - blocks // 2, 0), 0))
    attended = pl.pallas_call(
        attended_kernel,
        grid_spec=pltpu.PrefetchScalarGridSpec(
            num_scalar_prefetch=1,
            grid=(blocks,),
            in_specs=[every] * 6 + [upper, lower] * 2 + [held] * 8,
            out_specs=pl.BlockSpec((CHUNK, share), lambda i, at: (i, 0)),
            scratch_shapes=[
                pltpu.VMEM((groups, width, share), BF16),
                pltpu.SemaphoreType.DMA((32,)),
            ],
        ),
        out_shape=jax.ShapeDtypeStruct((rows, share), BF16),
        compiler_params=params(),
        name="attended",
    )(jnp.stack(around + heads_at + groups_at), *near, *far, *columns)
    ready = (returned, grad_opened, grad_part, attended)
    returned, grad_opened, grad_part, attended = lax.optimization_barrier(ready)

    grad_query = pl.pallas_call(
        query_kernel,
        grid=(blocks,),
        in_specs=[rows_of(width)] * 3
        + [rows_of(HEAD), row_block, whole(table.shape), state_block],
        out_specs=rows_of(width),
        out_shape=jax.ShapeDtypeStruct((rows, width), BF16),
        compiler_params=params(),
        name="grad_query",
    )(grad_opened, keys, values, dcol, drow, table, states)


    back_row = pl.BlockSpec((1, CHUNK), lambda i: (0, blocks - 1 - i))
    grad_key, grad_value = pl.pallas_call(
        key_value_kernel,
        grid=(blocks,),
        in_specs=[rows_of(width, blocks)] * 4
        + [rows_of(HEAD, blocks), back_row, whole(table.shape)]
        + [whole(payload.shape)] * len(returned),
        out_specs=[rows_of(width, blocks)] * 2,
        out_shape=[jax.ShapeDtypeStruct((rows, width), BF16)] * 2,
        scratch_shapes=[pltpu.VMEM((size, HEAD), F32)],
        compiler_params=params(),
        name="grad_key_value",
    )(grad_opened, queries, keys, values, dcol, drow, table, *returned)

    grad_weight = row_sum(grad_part, cy)
    return attended, grad_query, grad_key, grad_value, grad_weight


def solution(mesh):
    finer = Mesh(mesh.devices.reshape(4, 4, 4, 2), ("cx", "cy", "z", "core"))
    by_both = P(CTX, TENSOR)
    return jax.shard_map(
        body,
        mesh=finer,
        in_specs=(by_both, by_both, by_both, P(CTX), P(TENSOR, None), by_both),
        out_specs=(by_both, by_both, by_both, by_both, P(TENSOR, CTX)),
        check_vma=False,
    )
```
